32 devices in a mesh: slab: 8 (over y, x, core), coil: 4 (over z).
Axes of the slice: x: 2, y: 2, z: 4, core: 2. Of those that a mesh axis runs over, the one named last changes fastest.
Arguments:
- samples: bfloat16 [8, 65536, 128], P('coil', 'slab'), may hold values from -6 to 6
- sample_pos: bfloat16 [65536, 64], P('slab'), may hold values from 0 to 64
- block_count: int32 [65536], P('slab'), may hold values from 16 to 64
- grid_block: int32 [65536], P('slab'), may hold values from 0 to 32767
- block_slab: int32 [65536, 1], P('slab'), may hold values from 0 to 7, as said below
- sensitivity: bfloat16 [8, 256, 16, 512], P(None, 'slab', 'coil'), may hold values from -3 to 3
Outputs:
- image: float32 [256, 16, 512], P('slab', 'coil')
The draws below stay inside these ranges and needn't reach their ends.
Inputs may be any that keep to these rules, and one draw needn't show every extreme that they name: `block_slab`: within the rows of one device no slab is named more than 2560 times; one slab, the same for every device, is named exactly 2560 times by every device.
All inputs are finite; a program needn't handle non-finite values.
Results may differ from the reference program's by a relative error of at most 0.02.
The reference program's roundings to bfloat16 on the way count: a program that leaves them out, or rounds other values in their place, can miss the bound.
Values may be sent and summed in bfloat16 or wider, within the bound.
A program may use at most 128 MiB of HBM per device.

```python
import math
import jax
import jax.numpy as jnp
from jax import lax

COILS = 8
KX = 256
KY = 256
Z = 256
BLOCK_LEN = 64
XW = 16
BLK_DEV = 8192
ZP = 32
BLOCKS = 65536
CAP = 2560
NGB = 32768


def draw_block_slab(key, part):
    slab_total = BLOCKS // BLK_DEV
    remaining = BLK_DEV - CAP
    key_busy, key_share, key_order = jax.random.split(key, 3)
    busiest = jax.random.randint(key_busy, (), 0, slab_total)
    row_index = jnp.arange(BLK_DEV, dtype=jnp.int32)
    beyond = jnp.maximum(row_index - CAP, 0)

    def one_device(share_key, order_key):
        shares = jax.random.randint(share_key, (slab_total - 1,), 1, 3)
        bounds = remaining * jnp.cumsum(shares) // jnp.sum(shares)
        other_slab = 1 + jnp.sum((bounds[None, :] <= beyond[:, None]).astype(jnp.int32), axis=1)
        offset_row = jnp.where(row_index < CAP, 0, other_slab)
        slab_of = (busiest + offset_row) % slab_total
        return slab_of[jax.random.permutation(order_key, BLK_DEV)]
    drawn = jax.vmap(one_device)(jax.random.split(key_share, slab_total), jax.random.split(key_order, slab_total))
    return drawn.reshape(BLOCKS, 1).astype(jnp.int32)


def set_ends(values, key, smallest, largest):
    spot = [jax.random.randint(jax.random.fold_in(key, axis), (), 0, length) for axis, length in enumerate(values.shape)]
    widest = values.shape.index(max(values.shape))
    beside = spot[:widest] + [(spot[widest] + 1) % values.shape[widest]] + spot[widest + 1:]
    return values.at[tuple(spot)].set(smallest).at[tuple(beside)].set(largest)


def level_of(key, dims, cuts, low, high):
    def one(dim, blocks):
        steps = jax.random.uniform(jax.random.fold_in(jax.random.fold_in(key, 6), dim), (blocks,), jnp.float32, low / len(cuts), high / len(cuts))
        return jnp.repeat(jnp.exp(steps), dims[dim] // blocks).reshape((-1,) + (1,) * (len(dims) - dim - 1))

    loudness = one(*cuts[0])
    for cut in cuts[1:]:
        loudness = loudness * one(*cut)
    return loudness


def centred(key, dims, deviation, most, cuts=(), kind=jnp.bfloat16):
    values = deviation * jax.random.normal(key, dims, jnp.float32)
    if cuts:
        values = values * level_of(key, dims, cuts, -0.22, 0.18)
    return jnp.clip(values, -most, most).astype(kind)


def setup_inputs(seed: int = 0) -> dict:
    keys = jax.random.split(jax.random.key(seed), 7)
    return {
        "samples": centred(keys[0], (COILS, BLOCKS, 2 * BLOCK_LEN), 1.0, 6.0, ((0, 4), (1, 8))),
        "sample_pos": jnp.clip(64.0 * jax.random.uniform(keys[1], (BLOCKS, BLOCK_LEN), jnp.float32) ** level_of(keys[1], (BLOCKS, BLOCK_LEN), ((0, 8),), -0.2, 0.2), 0.0, 64.0).astype(jnp.bfloat16),
        "block_count": set_ends(jax.random.randint(keys[2], (BLOCKS,), 16, BLOCK_LEN + 1), jax.random.fold_in(keys[2], 1), 16, BLOCK_LEN).astype(jnp.int32),
        "grid_block": set_ends(jax.random.randint(keys[3], (BLOCKS,), 0, NGB), jax.random.fold_in(keys[3], 1), 0, NGB - 1).astype(jnp.int32),
        "block_slab": draw_block_slab(jax.random.fold_in(keys[6], 71), 0),
        "sensitivity": centred(keys[5], (COILS, Z, XW, 2 * KY), 0.5, 3.0, ((1, 8), (2, 4))),
    }


kernel_half = 2.5

def block_weights(positions, counts):
    cell_mid = jnp.arange(positions.shape[-1], dtype=jnp.int32).astype(jnp.float32) + 0.5
    offset = (positions.astype(jnp.float32)[..., :, None] - cell_mid) / kernel_half
    bump = jnp.maximum(1.0 - offset * offset, 0.0)
    live = jnp.arange(positions.shape[-1], dtype=jnp.int32)[:, None] < counts[..., None, None]
    return jnp.where(live, bump * bump, 0.0).astype(jnp.bfloat16)

def twiddle(first, second, length):
    phase = (first * second % length).astype(jnp.float32) * (2.0 * math.pi / length)
    scale = 1.0 / math.sqrt(length)
    return (jnp.cos(phase) * scale, jnp.sin(phase) * scale)

def choose(part_in, part_out, cosine, sine):
    upper = jnp.where(part_out == 0, cosine, sine)
    lower = jnp.where(part_out == 0, -sine, cosine)
    return jnp.where(part_in == 0, upper, lower).astype(jnp.bfloat16)

def across_table(kx_len, rows_out):
    index_in = jnp.arange(2 * kx_len, dtype=jnp.int32)
    segment = index_in // 128
    part_in = index_in // 64 % 2
    cell_at = segment * 64 + index_in % 64
    index_out = jnp.arange(2 * rows_out, dtype=jnp.int32)
    part_out = index_out // rows_out
    row_at = (kx_len - rows_out) // 2 + index_out % rows_out
    cosine, sine = twiddle(cell_at[:, None], row_at[None, :], kx_len)
    return choose(part_in[:, None], part_out[None, :], cosine, sine)

def square_table(length):
    index_in = jnp.arange(2 * length, dtype=jnp.int32)
    index_out = jnp.arange(2 * length, dtype=jnp.int32)
    cosine, sine = twiddle((index_in // 2)[:, None], (index_out % length)[None, :], length)
    return choose((index_in % 2)[:, None], (index_out // length)[None, :], cosine, sine)

def depth_table(positions, freqs, length):
    cosine, sine = twiddle(positions[:, None], freqs[None, :], length)
    upper = jnp.stack([cosine, -sine], axis=-1)
    lower = jnp.stack([sine, cosine], axis=-1)
    return jnp.stack([upper, lower], axis=1).astype(jnp.bfloat16)

def conj_term(coil_map, coil_image, half):
    map_re = coil_map[..., :half].astype(jnp.float32)
    map_im = coil_map[..., half:].astype(jnp.float32)
    img_re = coil_image[..., :half].astype(jnp.float32)
    img_im = coil_image[..., half:].astype(jnp.float32)
    return jnp.concatenate([map_re * img_re + map_im * img_im, map_re * img_im - map_im * img_re], axis=-1)

def reference(samples, sample_pos, block_count, grid_block, block_slab, sensitivity):
    seg_count = KX // 64
    target = (block_slab[:, 0] * (ZP * KY * seg_count) + grid_block).astype(jnp.int32)
    group_len = math.gcd(BLOCKS, 4096)
    group_count = BLOCKS // group_len

    def one_group(pieces):
        values, positions, counts = pieces
        weights = lax.optimization_barrier(block_weights(positions, counts)).astype(jnp.float32)
        shaped = values.astype(jnp.float32).reshape(COILS, group_len, 2, 64)
        result = jnp.einsum('mij,cmpi->cmpj', weights, shaped, precision=lax.Precision.HIGHEST)
        return result.reshape(COILS, group_len, 128).astype(jnp.bfloat16)
    grouped = (jnp.transpose(samples.reshape(COILS, group_count, group_len, 128), (1, 0, 2, 3)), sample_pos.reshape(group_count, group_len, 64), block_count.reshape(group_count, group_len))
    gridded = jnp.transpose(lax.map(one_group, grouped), (1, 0, 2, 3)).reshape(COILS, BLOCKS, 128)
    across = across_table(KX, XW)
    y_table = square_table(KY).reshape(KY, 2, 2 * KY).astype(jnp.float32)
    every_z = jnp.arange(Z, dtype=jnp.int32)
    depth_tab = depth_table(every_z, every_z, Z).astype(jnp.float32)

    def one_coil(running, pieces):
        cell_rows, coil_map = pieces
        cell_wide = lax.optimization_barrier(cell_rows).astype(jnp.float32)
        kspace = jnp.zeros((Z * KY * seg_count, 128), jnp.float32).at[target].add(cell_wide).astype(jnp.bfloat16)
        x_rows = jnp.dot(kspace.reshape(Z * KY, 2 * KX), across, preferred_element_type=jnp.float32).astype(jnp.bfloat16)
        x_rows = lax.optimization_barrier(x_rows).astype(jnp.float32).reshape(Z, KY, 2, XW)
        y_planes = jnp.einsum('zkqx,kqn->zxn', x_rows, y_table, precision=lax.Precision.HIGHEST).astype(jnp.bfloat16)
        y_planes = lax.optimization_barrier(y_planes).astype(jnp.float32).reshape(Z, XW, 2, KY)
        coil_image = jnp.einsum('zpkq,kxqy->zxpy', depth_tab, y_planes, precision=lax.Precision.HIGHEST)
        coil_image = coil_image.reshape(Z, XW, 2 * KY).astype(jnp.bfloat16)
        return (running + conj_term(coil_map, coil_image, KY), None)
    start_sum = jnp.zeros((Z, XW, 2 * KY), jnp.float32)
    image, _ = lax.scan(one_coil, start_sum, (gridded, sensitivity))
    return image
```

```python
import functools
import math

import jax
import jax.numpy as jnp
from jax import lax
from jax.experimental import pallas as pl
from jax.experimental.pallas import tpu as pltpu
from jax.sharding import PartitionSpec as P

KX = 256
CELLS = 64
CLASSES = 8
NT = (((1,), (1,)), ((), ()))


def twiddle(first, second, length):
    phase = (first * second % length).astype(jnp.float32) * (2.0 * math.pi / length)
    scale = 1.0 / math.sqrt(length)
    return (jnp.cos(phase) * scale, jnp.sin(phase) * scale)


def ints(count):
    return jnp.arange(count, dtype=jnp.int32)


def across_table(coils, rows_out, x_here):
    x0 = (KX - rows_out) // 2
    cosine, sine = twiddle(x0 + ints(rows_out)[:, None], ints(CELLS)[None, :], KX)
    upper = jnp.stack([cosine, -sine], axis=1)
    lower = jnp.stack([sine, cosine], axis=1)
    eye = jnp.eye(coils, dtype=jnp.float32)
    tables = []
    for one in (jnp.stack([upper, lower], axis=1), jnp.stack([-lower, upper], axis=1)):
        one = one.reshape(rows_out // x_here, 1, x_here, 2, 1, 2, CELLS)
        one = one * eye[None, :, None, None, :, None, None]
        tables.append(one.reshape(2 * coils * rows_out, 2 * coils * CELLS))
    return jnp.concatenate(tables, axis=0).astype(jnp.bfloat16)


def right_table(length):
    cosine, sine = twiddle(ints(length)[:, None], ints(length)[None, :], length)
    upper = jnp.concatenate([cosine, sine], axis=1)
    lower = jnp.concatenate([-sine, cosine], axis=1)
    return jnp.concatenate([upper, lower], axis=0).astype(jnp.bfloat16)


def left_table(length):
    cosine, sine = twiddle(ints(length)[:, None], ints(length)[None, :], length)
    upper = jnp.concatenate([cosine, -sine], axis=1)
    lower = jnp.concatenate([sine, cosine], axis=1)
    return jnp.concatenate([upper, lower], axis=0).astype(jnp.bfloat16)


def spread_table(table, values):
    at = ints(2 * CELLS) % CELLS
    cell = CLASSES * (at % CLASSES) + at // CLASSES
    table = table.reshape(table.shape[0], values, CELLS)[:, :, cell]
    return table.reshape(table.shape[0], values * 2 * CELLS)


def grid_kernel(
    coils, unroll, pos_ref, val_ref, seg_ref, x_ref, tab_ref, out_ref, cells, near, bump
):
    rows, tile = out_ref.shape
    block = lax.broadcasted_iota(jnp.int32, (16, 2 * CELLS), 0)
    upper = lax.broadcasted_iota(jnp.int32, (16, 2 * CELLS), 1) >= CELLS
    odd = block % 2 == 1
    own = [block % 4 // 2 == half for half in range(2)]
    mine = block // 4 % 2 == upper.astype(jnp.int32)
    level = lax.broadcasted_iota(jnp.int32, (CLASSES, 2 * CELLS), 0).astype(jnp.float32)

    def step(g, slot):
        at = pl.ds(pl.multiple_of(g * 16, 16), 16)
        left = []
        for c in range(coils):
            straight = val_ref[c, at, :].astype(jnp.float32)
            turned = pltpu.roll(straight, CELLS, 1)
            for low, high in ((straight, turned), (turned, straight)):
                placed = jnp.where(
                    odd, jnp.where(upper, high, 0.0), jnp.where(upper, 0.0, low)
                )
                halves = [jnp.where(own[half], placed, 0.0) for half in range(2)]
                left.append(jnp.concatenate(halves, axis=1).astype(jnp.bfloat16))
        place = pos_ref[pl.ds(pl.multiple_of(g * 8, 8), 8), :].astype(jnp.float32) * 0.125
        for r in range(CLASSES):
            offset = place - ((r + 0.5) * 0.125 - 0.5)
            seat = jnp.floor(offset)
            offset = (offset - seat) * 3.2 - 1.6
            rise = jnp.maximum(1.0 - offset * offset, 0.0)
            near[slot, r] = seat
            bump[slot, r] = rise * rise
        right = []
        for quad in range(4):
            halves = []
            for half in range(2):
                row = pl.ds(2 * quad + half, 1)
                parts = []
                for r in range(CLASSES):
                    seat = jnp.broadcast_to(near[slot, r, row, :], level.shape)
                    high = jnp.broadcast_to(bump[slot, r, row, :], level.shape)
                    parts.append(jnp.where(level == seat, high, 0.0))
                halves.append(jnp.concatenate(parts, axis=0).astype(jnp.bfloat16))
            right.append(jnp.concatenate(halves, axis=1))
        done = lax.dot_general(
            jnp.concatenate(left, axis=0),
            jnp.concatenate(right, axis=0),
            NT,
            preferred_element_type=jnp.float32,
        )
        for v in range(2 * coils):
            first = done[16 * v : 16 * v + 8, : 2 * CELLS]
            second = done[16 * v + 8 : 16 * v + 16, 2 * CELLS :]
            both = jnp.where(mine, jnp.concatenate([first, second], axis=0), 0.0)
            cells[at, 2 * CELLS * v : 2 * CELLS * (v + 1)] = both.astype(jnp.bfloat16)

    @pl.loop(0, tile // (16 * unroll))
    def _(outer):
        for slot in range(unroll):
            step(outer * unroll + slot, slot)

    moved = lax.dot_general(tab_ref[...], cells[...], NT, preferred_element_type=jnp.float32)
    turn = (x_ref[...] * seg_ref[...]) & 3
    turned = jnp.where((turn & 1) == 0, moved[:rows], moved[rows:])
    out_ref[...] = jnp.where(turn >= 2, -turned, turned).astype(jnp.bfloat16)


def sort_kernel(vals_ref, spot_ref, kz_ref, out_ref, spot_out_ref, before, rank):
    rows, group = vals_ref.shape
    depth = before.shape[0]
    piece = math.gcd(128, group)
    pieces = group // piece
    level = lax.broadcasted_iota(jnp.int32, (depth, piece), 0)
    src = lax.broadcasted_iota(jnp.int32, (piece, 2 * piece), 0)
    dst = lax.broadcasted_iota(jnp.int32, (piece, 2 * piece), 1)
    steps = jnp.where((src < dst) | (dst >= piece), 1.0, 0.0).astype(jnp.bfloat16)
    seen = jnp.zeros((depth, piece), jnp.float32)
    for at in range(pieces):
        cut = slice(at * piece, (at + 1) * piece)
        hot = jnp.where(level == kz_ref[:, cut], 1.0, 0.0)
        counts = jnp.dot(hot.astype(jnp.bfloat16), steps, preferred_element_type=jnp.float32)
        before[:, cut] = seen + counts[:, :piece]
        seen = seen + counts[:, piece:]
    high = jnp.floor(seen * (1.0 / 256.0))
    low = seen - 256.0 * high
    here = lax.broadcasted_iota(jnp.int32, (depth, depth), 0)
    under = lax.broadcasted_iota(jnp.int32, (depth, depth), 1)
    lower = jnp.where(under < here, 1.0, 0.0).astype(jnp.bfloat16)
    first = 256.0 * jnp.dot(lower, high.astype(jnp.bfloat16), preferred_element_type=jnp.float32)
    first = first + jnp.dot(lower, low.astype(jnp.bfloat16), preferred_element_type=jnp.float32)
    for at in range(pieces):
        cut = slice(at * piece, (at + 1) * piece)
        found = jnp.where(level == kz_ref[:, cut], before[:, cut] + first, 0.0)
        rank[:, cut] = jnp.sum(found, axis=0, keepdims=True).astype(jnp.int32)

    tile = math.gcd(256, group)
    slot = lax.broadcasted_iota(jnp.int32, (tile, group), 0)
    vals = jnp.concatenate([vals_ref[...], spot_ref[...]], axis=0)

    @pl.loop(0, group // tile)
    def _(at):
        start = pl.multiple_of(at * tile, tile)
        hot = jnp.where(slot == (rank[...] - start), 1.0, 0.0).astype(jnp.bfloat16)
        moved = lax.dot_general(vals, hot, NT, preferred_element_type=jnp.float32)
        moved = moved.astype(jnp.bfloat16)
        out_ref[:, pl.ds(start, tile)] = moved[:rows]
        spot_out_ref[:, pl.ds(start, tile)] = moved[rows:]


def add_kernel(
    chunk, span, lo_ref, more_ref, vals_ref, kz_ref, ky_ref, ytab_ref, ztab_ref, out_ref, total
):
    step = pl.program_id(0)
    rows = vals_ref.shape[1]
    width = vals_ref.shape[2]
    depth, freq = out_ref.shape[1], total.shape[2]
    parts = width // chunk
    spot = lax.broadcasted_iota(jnp.int32, (freq, chunk), 0)
    plane = lax.broadcasted_iota(jnp.int32, (span, chunk), 0)

    @pl.when(step == 0)
    def _():
        total[...] = jnp.zeros_like(total)

    def add(part, start):
        cut = slice(part * chunk, (part + 1) * chunk)
        hot = jnp.where(spot == ky_ref[0, :, cut], 1.0, 0.0).astype(jnp.bfloat16)
        mine = jnp.where(plane == (kz_ref[0, :, cut] - start), 1.0, 0.0).astype(jnp.bfloat16)
        left = []
        for v in range(rows):
            row = vals_ref[0, v : v + 1, cut].astype(jnp.float32)
            row = jnp.broadcast_to(row, (16, chunk)).astype(jnp.bfloat16)
            left.append(mine * jnp.concatenate([row] * (span // 16), axis=0))
        left = jnp.concatenate(left, axis=0)
        moved = lax.dot_general(left, hot, NT, preferred_element_type=jnp.float32)
        for v in range(rows):
            total[v, pl.ds(start, span), :] += moved[v * span : (v + 1) * span]

    for part in range(parts):
        add(part, pl.multiple_of(lo_ref[step * parts + part], 8))

    for part in range(parts):
        first = lo_ref[step * parts + part]

        def again(at, carry):
            add(part, pl.multiple_of(first + at * span, 8))
            return carry

        lax.fori_loop(1, more_ref[step * parts + part], again, 0)

    @pl.when(step == pl.num_programs(0) - 1)
    def _():
        pairs = rows // 2
        for pair in range(pairs):
            both = jnp.concatenate(
                [total[2 * pair, :depth, :], total[2 * pair + 1, :depth, :]], axis=1
            )
            planes = jnp.dot(
                both.astype(jnp.bfloat16), ytab_ref[...], preferred_element_type=jnp.float32
            ).astype(jnp.bfloat16)
            planes = jnp.concatenate([planes[:, :freq], planes[:, freq:]], axis=0)
            image = jnp.dot(ztab_ref[...], planes, preferred_element_type=jnp.float32)
            out_ref[pair, :, :freq] = image[:depth].astype(jnp.bfloat16)
            out_ref[pair, :, freq:] = image[depth:].astype(jnp.bfloat16)


def whole(memory=pltpu.VMEM):
    return pl.BlockSpec(memory_space=memory)


def per_device(samples, sample_pos, block_count, grid_block, block_slab, sensitivity):
    slab_total = lax.axis_size("slab")
    coil_total = lax.axis_size("coil")
    coils = samples.shape[0]
    blocks = samples.shape[1]
    planes = sensitivity.shape[1]
    rows_out = sensitivity.shape[2] * coil_total
    depth = planes * slab_total
    freq = sensitivity.shape[3] // 2
    x_here = rows_out // slab_total
    segments = KX // CELLS

    live = ints(CELLS)[None, :] < block_count[:, None]
    pos = jnp.where(live, sample_pos, 9984.0).reshape(blocks // 2, 2 * CELLS)
    seg = (grid_block % segments)[None, :]
    kz = block_slab[:, 0] * planes + grid_block // (segments * freq)
    ky = grid_block // segments % freq

    tile = math.gcd(blocks, 1024)
    unroll = math.gcd(tile // 16, 16)
    count = 2 * coils * rows_out
    table = spread_table(across_table(coils, rows_out, x_here), 2 * coils)
    x_at = (ints(count) // (2 * coils * x_here)) * x_here + ints(count) // 2 % x_here
    x_at = jnp.broadcast_to((x_at + (KX - rows_out) // 2)[:, None], (count, tile))
    lines = pl.pallas_call(
        functools.partial(grid_kernel, coils, unroll),
        grid=(blocks // tile,),
        in_specs=[
            pl.BlockSpec((tile // 2, 2 * CELLS), lambda b: (b, 0)),
            pl.BlockSpec((coils, tile, 2 * CELLS), lambda b: (0, b, 0)),
            pl.BlockSpec((1, tile), lambda b: (0, b)),
            pl.BlockSpec(x_at.shape, lambda b: (0, 0)),
            pl.BlockSpec(table.shape, lambda b: (0, 0)),
        ],
        out_specs=pl.BlockSpec((count, tile), lambda b: (0, b)),
        out_shape=jax.ShapeDtypeStruct((count, blocks), jnp.bfloat16),
        scratch_shapes=[
            pltpu.VMEM((tile, 4 * coils * CELLS), jnp.bfloat16),
            pltpu.VMEM((unroll, CLASSES, 8, 2 * CELLS), jnp.float32),
            pltpu.VMEM((unroll, CLASSES, 8, 2 * CELLS), jnp.float32),
        ],
        name="grid_x",
    )(pos, samples, seg, x_at, table)

    group = math.gcd(blocks, 2048)
    groups = blocks // group
    spots = jnp.pad(jnp.stack([kz, ky]).astype(jnp.bfloat16), ((0, 14), (0, 0)))
    ordered, spots = pl.pallas_call(
        sort_kernel,
        grid=(groups,),
        in_specs=[
            pl.BlockSpec((count, group), lambda b: (0, b)),
            pl.BlockSpec((16, group), lambda b: (0, b)),
            pl.BlockSpec((1, group), lambda b: (0, b)),
        ],
        out_specs=[
            pl.BlockSpec((count, group), lambda b: (0, b)),
            pl.BlockSpec((16, group), lambda b: (0, b)),
        ],
        out_shape=[
            jax.ShapeDtypeStruct((count, blocks), jnp.bfloat16),
            jax.ShapeDtypeStruct((16, blocks), jnp.bfloat16),
        ],
        scratch_shapes=[
            pltpu.VMEM((depth, group), jnp.float32),
            pltpu.VMEM((1, group), jnp.int32),
        ],
        name="order_kz",
    )(lines, spots, kz[None, :])
    each = 2 * coils * x_here
    tail = jnp.broadcast_to(spots[:2].reshape(1, each, -1), (slab_total, each, 2 * blocks // each))
    sent = lax.all_to_all(
        jnp.concatenate([ordered.reshape(slab_total, each, blocks), tail], axis=2),
        "slab",
        0,
        0,
        tiled=True,
    )
    spots = sent[:, :, blocks:].reshape(slab_total, 2, blocks).astype(jnp.int32)
    kz_all = spots[:, 0:1]
    ky_all = spots[:, 1:2]

    chunk = math.gcd(blocks, 256)
    span = 64
    width = math.gcd(blocks, 1024)
    per_row = blocks // width
    by_chunk = kz_all.reshape(slab_total * blocks // chunk, chunk)
    low = jnp.min(by_chunk, axis=1) // 8 * 8
    high = (jnp.max(by_chunk, axis=1) - low) // span + 1
    ytab, ztab = right_table(freq), left_table(depth)
    pairs = each // 2
    imaged = pl.pallas_call(
        functools.partial(add_kernel, chunk, span),
        grid_spec=pltpu.PrefetchScalarGridSpec(
            num_scalar_prefetch=2,
            grid=(slab_total * per_row,),
            in_specs=[
                pl.BlockSpec((1, each, width), lambda i, a, b: (i // per_row, 0, i % per_row)),
                pl.BlockSpec((1, 1, width), lambda i, a, b: (i // per_row, 0, i % per_row)),
                pl.BlockSpec((1, 1, width), lambda i, a, b: (i // per_row, 0, i % per_row)),
                pl.BlockSpec(ytab.shape, lambda i, a, b: (0, 0)),
                pl.BlockSpec(ztab.shape, lambda i, a, b: (0, 0)),
            ],
            out_specs=pl.BlockSpec((pairs, depth, 2 * freq), lambda i, a, b: (0, 0, 0)),
            scratch_shapes=[pltpu.VMEM((each, depth + span, freq), jnp.float32)],
        ),
        out_shape=jax.ShapeDtypeStruct((pairs, depth, 2 * freq), jnp.bfloat16),
        name="add_yz",
    )(low, high, sent, kz_all, ky_all, ytab, ztab)

    split = imaged.reshape(pairs, slab_total, planes, 2 * freq)
    split = lax.all_to_all(jnp.swapaxes(split, 0, 1), "slab", 0, 0, tiled=True)
    split = split.reshape(slab_total, coils, x_here, planes, 2 * freq)
    split = jnp.transpose(split, (0, 2, 1, 3, 4)).reshape(
        coil_total, rows_out // coil_total, coils, planes, 2 * freq
    )
    split = lax.all_to_all(split, "coil", 0, 0, tiled=True)
    mine = jnp.transpose(split, (0, 2, 3, 1, 4)).reshape(sensitivity.shape).astype(jnp.float32)
    maps = sensitivity.astype(jnp.float32)
    map_re, map_im = maps[..., :freq], maps[..., freq:]
    img_re, img_im = mine[..., :freq], mine[..., freq:]
    real_part = jnp.sum(map_re * img_re + map_im * img_im, axis=0)
    imag_part = jnp.sum(map_re * img_im - map_im * img_re, axis=0)
    return jnp.concatenate([real_part, imag_part], axis=-1)


def solution(mesh):
    return jax.shard_map(
        per_device,
        mesh=mesh,
        in_specs=(
            P("coil", "slab", None),
            P("slab", None),
            P("slab"),
            P("slab"),
            P("slab", None),
            P(None, "slab", "coil", None),
        ),
        out_specs=P("slab", "coil", None),
        check_vma=False,
    )
```

```python
import functools
import math

import jax
import jax.numpy as jnp
from jax import lax
from jax.experimental import pallas as pl
from jax.experimental.pallas import tpu as pltpu
from jax.sharding import PartitionSpec as P

KX = 256
CELLS = 64
CLASSES = 8
LANES = 128
RUNS = 4
NT = (((1,), (1,)), ((), ()))


def twiddle(first, second, length):
    phase = (first * second % length).astype(jnp.float32) * (2.0 * math.pi / length)
    scale = 1.0 / math.sqrt(length)
    return (jnp.cos(phase) * scale, jnp.sin(phase) * scale)


def ints(count):
    return jnp.arange(count, dtype=jnp.int32)


def across_table(coils, rows_out, x_here):
    x0 = (KX - rows_out) // 2
    cosine, sine = twiddle(x0 + ints(rows_out)[:, None], ints(CELLS)[None, :], KX)
    upper = jnp.stack([cosine, -sine], axis=1)
    lower = jnp.stack([sine, cosine], axis=1)
    eye = jnp.eye(coils, dtype=jnp.float32)
    tables = []
    for one in (jnp.stack([upper, lower], axis=1), jnp.stack([-lower, upper], axis=1)):
        one = one.reshape(rows_out // x_here, 1, x_here, 2, 1, 2, CELLS)
        one = one * eye[None, :, None, None, :, None, None]
        tables.append(one.reshape(2 * coils * rows_out, 2 * coils * CELLS))
    return jnp.concatenate(tables, axis=0).astype(jnp.bfloat16)


def right_table(length):
    cosine, sine = twiddle(ints(length)[:, None], ints(length)[None, :], length)
    upper = jnp.concatenate([cosine, sine], axis=1)
    lower = jnp.concatenate([-sine, cosine], axis=1)
    return jnp.concatenate([upper, lower], axis=0).astype(jnp.bfloat16)


def left_table(length):
    cosine, sine = twiddle(ints(length)[:, None], ints(length)[None, :], length)
    upper = jnp.concatenate([cosine, -sine], axis=1)
    lower = jnp.concatenate([sine, cosine], axis=1)
    return jnp.concatenate([upper, lower], axis=0).astype(jnp.bfloat16)


def spread_table(table, values):
    at = ints(2 * CELLS) % CELLS
    cell = CLASSES * (at % CLASSES) + at // CLASSES
    table = table.reshape(table.shape[0], values, CELLS)[:, :, cell]
    return table.reshape(table.shape[0], values * 2 * CELLS)


def hot_rows(spots, depth):
    level = lax.broadcasted_iota(jnp.int32, (16, spots.shape[1]), 0).astype(jnp.float32)
    spots = jnp.broadcast_to(spots, (16, spots.shape[1])).astype(jnp.bfloat16)
    one, none = jnp.bfloat16(1), jnp.bfloat16(0)
    return jnp.concatenate(
        [
            jnp.where((level + at).astype(jnp.bfloat16) == spots, one, none)
            for at in range(0, depth, 16)
        ],
        axis=0,
    )


def permute(values, spots):
    depth = spots.shape[1]
    level = lax.broadcasted_iota(jnp.int32, (depth, depth), 0).astype(jnp.float32)
    hot = jnp.where(level == spots, 1.0, 0.0).astype(jnp.bfloat16)
    return lax.dot_general(values, hot, NT, preferred_element_type=jnp.float32)


def regroup(runs):
    count = len(runs)
    rows, length = runs[0].shape
    wide = LANES // count
    place = lax.broadcasted_iota(jnp.int32, (rows, LANES), 1) // wide
    for at in range(length // wide):
        cut = slice(at // count * LANES, at // count * LANES + LANES)
        out = runs[0][:, cut]
        for run in range(1, count):
            out = jnp.where(place == (at + run) % count, runs[run][:, cut], out)
        yield at, out


def order_kernel(planes, freq, kz_ref, ky_ref, spot_ref, sorted_ref):
    tile = kz_ref.shape[1]
    length = tile // RUNS
    wide = LANES // RUNS
    pieces = length // LANES
    runs = []
    for run in range(RUNS):
        cut = slice(run * length, (run + 1) * length)
        kz, ky = kz_ref[:, cut], ky_ref[:, cut]
        lane = lax.broadcasted_iota(jnp.int32, (1, length), 1).astype(jnp.float32)
        key = kz * float(length) + lane
        rank = jnp.zeros((1, length), jnp.float32)
        for piece in range(pieces):
            part = key[:, piece * LANES : (piece + 1) * LANES]
            part = jnp.broadcast_to(part, (LANES, LANES)).T
            part = jnp.concatenate([part] * pieces, axis=1)
            rank = rank + jnp.sum(jnp.where(part < key, 1.0, 0.0), axis=0, keepdims=True)
        rank = rank.astype(jnp.int32)
        seat = rank // wide
        spot = (seat // RUNS) * LANES + (seat + run) % RUNS * wide + rank % wide
        spot = spot.astype(jnp.float32)
        spot_ref[:, cut] = spot
        both = jnp.concatenate([kz, ky, jnp.zeros((14, length), jnp.float32)], axis=0)
        runs.append(permute(both.astype(jnp.bfloat16), spot))
    for at, out in regroup(runs):
        sorted_ref[0, :, at * LANES : (at + 1) * LANES] = out[:2]


def grid_kernel(
    coils, unroll, pos_ref, val_ref, seg_ref, x_ref, tab_ref, spot_ref, out_ref,
    cells, near, bump, placed,
):
    slabs, _, each, tile = out_ref.shape
    rows = slabs * each
    length = tile // RUNS
    block = lax.broadcasted_iota(jnp.int32, (16, LANES), 0)
    upper = lax.broadcasted_iota(jnp.int32, (16, LANES), 1) >= CELLS
    odd = block % 2 == 1
    own = [block % 4 // 2 == half for half in range(2)]
    mine = block // 4 % 2 == upper.astype(jnp.int32)
    level = lax.broadcasted_iota(jnp.int32, (CLASSES, LANES), 0).astype(jnp.float32)

    def step(g, slot):
        at = pl.ds(pl.multiple_of(g * 16, 16), 16)
        left = []
        for c in range(coils):
            straight = val_ref[c, at, :].astype(jnp.float32)
            turned = pltpu.roll(straight, CELLS, 1)
            for low, high in ((straight, turned), (turned, straight)):
                placed_here = jnp.where(
                    odd, jnp.where(upper, high, 0.0), jnp.where(upper, 0.0, low)
                )
                halves = [jnp.where(own[half], placed_here, 0.0) for half in range(2)]
                left.append(jnp.concatenate(halves, axis=1).astype(jnp.bfloat16))
        place = pos_ref[pl.ds(pl.multiple_of(g * 8, 8), 8), :].astype(jnp.float32) * 0.125
        for r in range(CLASSES):
            offset = place - ((r + 0.5) * 0.125 - 0.5)
            seat = jnp.floor(offset)
            offset = (offset - seat) * 3.2 - 1.6
            rise = jnp.maximum(1.0 - offset * offset, 0.0)
            near[slot, r] = seat
            bump[slot, r] = rise * rise
        right = []
        for quad in range(4):
            halves = []
            for half in range(2):
                row = pl.ds(2 * quad + half, 1)
                parts = []
                for r in range(CLASSES):
                    seat = jnp.broadcast_to(near[slot, r, row, :], level.shape)
                    high = jnp.broadcast_to(bump[slot, r, row, :], level.shape)
                    parts.append(jnp.where(level == seat, high, 0.0))
                halves.append(jnp.concatenate(parts, axis=0).astype(jnp.bfloat16))
            right.append(jnp.concatenate(halves, axis=1))
        done = lax.dot_general(
            jnp.concatenate(left, axis=0),
            jnp.concatenate(right, axis=0),
            NT,
            preferred_element_type=jnp.float32,
        )
        for v in range(2 * coils):
            first = done[16 * v : 16 * v + 8, :LANES]
            second = done[16 * v + 8 : 16 * v + 16, LANES:]
            both = jnp.where(mine, jnp.concatenate([first, second], axis=0), 0.0)
            cells[at, LANES * v : LANES * (v + 1)] = both.astype(jnp.bfloat16)

    @pl.loop(0, tile // (16 * unroll))
    def _(outer):
        for slot in range(unroll):
            step(outer * unroll + slot, slot)

    for run in range(RUNS):
        cut = slice(run * length, (run + 1) * length)
        moved = lax.dot_general(
            tab_ref[...], cells[cut, :], NT, preferred_element_type=jnp.float32
        )
        turn = (x_ref[...] * seg_ref[:, cut]) & 3
        turned = jnp.where((turn & 1) == 0, moved[:rows], moved[rows:])
        turned = jnp.where(turn >= 2, -turned, turned).astype(jnp.bfloat16)
        placed[run] = permute(turned, spot_ref[:, cut]).astype(jnp.bfloat16)
    for at, out in regroup([placed.at[run] for run in range(RUNS)]):
        for slab in range(slabs):
            out_ref[slab, 0, :, at * LANES : (at + 1) * LANES] = out[
                slab * each : (slab + 1) * each
            ]


def add_kernel(
    span, per, lo_ref, more_ref, vals_ref, spot_ref, ytab_ref, ztab_ref, out_ref, total
):
    step = pl.program_id(0)
    tiles, rows = vals_ref.shape[1], vals_ref.shape[2]
    pairs, depth, freq = out_ref.shape[0], out_ref.shape[1], out_ref.shape[2] // 2
    deep = 16 // rows
    width = tiles * LANES
    inner = (lax.broadcasted_iota(jnp.int32, (16, width), 0) // rows).astype(jnp.float32)

    @pl.when(step == 0)
    def _():
        total[...] = jnp.zeros_like(total)

    def add(part, start):
        cut = slice(part * LANES, (part + 1) * LANES)
        across = [vals_ref[0, t, :, cut] for t in range(tiles)]
        vals = jnp.concatenate([jnp.concatenate(across, axis=1)] * deep, axis=0)
        kz = jnp.concatenate([spot_ref[0, t, 0:1, cut] for t in range(tiles)], axis=1)
        ky = jnp.concatenate([spot_ref[0, t, 1:2, cut] for t in range(tiles)], axis=1)
        base = jnp.full((16, width), start, jnp.int32).astype(jnp.float32)
        plane = (jnp.broadcast_to(kz, (16, width)) - base - inner).astype(jnp.bfloat16)
        left = [
            jnp.where(plane == jnp.bfloat16(at), vals, jnp.bfloat16(0))
            for at in range(0, span, deep)
        ]
        moved = lax.dot_general(
            jnp.concatenate(left, axis=0),
            hot_rows(ky, freq),
            NT,
            preferred_element_type=jnp.float32,
        )
        at = pl.ds(pl.multiple_of(start * rows, 8), span * rows)
        for half in range(freq // LANES):
            total[half, at, :] += moved[:, half * LANES : (half + 1) * LANES]

    for part in range(per):
        add(part, lo_ref[step * per + part])

    for part in range(per):
        first = lo_ref[step * per + part]

        def again(at, carry):
            add(part, first + at * span)
            return carry

        lax.fori_loop(1, more_ref[step * per + part], again, 0)

    @pl.when(step == pl.num_programs(0) - 1)
    def _():
        for pair in range(pairs):
            both = jnp.concatenate(
                [
                    total[half, pl.ds(2 * pair + part, depth, stride=rows), :]
                    for part in range(2)
                    for half in range(freq // LANES)
                ],
                axis=1,
            )
            planes = jnp.dot(
                both.astype(jnp.bfloat16), ytab_ref[...], preferred_element_type=jnp.float32
            ).astype(jnp.bfloat16)
            planes = jnp.concatenate([planes[:, :freq], planes[:, freq:]], axis=0)
            image = jnp.dot(ztab_ref[...], planes, preferred_element_type=jnp.float32)
            out_ref[pair, :, :freq] = image[:depth].astype(jnp.bfloat16)
            out_ref[pair, :, freq:] = image[depth:].astype(jnp.bfloat16)


def whole(memory=pltpu.VMEM):
    return pl.BlockSpec(memory_space=memory)


def per_device(samples, sample_pos, block_count, grid_block, block_slab, sensitivity):
    slab_total = lax.axis_size("slab")
    coil_total = lax.axis_size("coil")
    coils = samples.shape[0]
    blocks = samples.shape[1]
    planes = sensitivity.shape[1]
    rows_out = sensitivity.shape[2] * coil_total
    depth = planes * slab_total
    freq = sensitivity.shape[3] // 2
    x_here = rows_out // slab_total
    segments = KX // CELLS

    live = ints(CELLS)[None, :] < block_count[:, None]
    pos = jnp.where(live, sample_pos, 9984.0).reshape(blocks // 2, 2 * CELLS)
    seg = (grid_block % segments)[None, :]
    kz = block_slab[:, 0] * planes + grid_block // (segments * freq)
    ky = grid_block // segments % freq
    kz, ky = kz.astype(jnp.float32)[None, :], ky.astype(jnp.float32)[None, :]

    tile = math.gcd(blocks, 2048)
    tiles = blocks // tile
    chunks = tile // LANES
    unroll = math.gcd(tile // 16, 16)
    count = 2 * coils * rows_out
    each = 2 * coils * x_here

    row = pl.BlockSpec((1, tile), lambda b: (0, b))
    spot, spots = pl.pallas_call(
        functools.partial(order_kernel, planes, freq),
        grid=(tiles,),
        in_specs=[row, row],
        out_specs=[row, pl.BlockSpec((1, 2, tile), lambda b: (b, 0, 0))],
        out_shape=[
            jax.ShapeDtypeStruct((1, blocks), jnp.float32),
            jax.ShapeDtypeStruct((tiles, 2, tile), jnp.float32),
        ],
        name="order_kz",
    )(kz, ky)

    table = spread_table(across_table(coils, rows_out, x_here), 2 * coils)
    x_at = (ints(count) // (2 * coils * x_here)) * x_here + ints(count) // 2 % x_here
    x_at = jnp.broadcast_to((x_at + (KX - rows_out) // 2)[:, None], (count, tile // RUNS))
    lines = pl.pallas_call(
        functools.partial(grid_kernel, coils, unroll),
        grid=(tiles,),
        in_specs=[
            pl.BlockSpec((tile // 2, LANES), lambda b: (b, 0)),
            pl.BlockSpec((coils, tile, LANES), lambda b: (0, b, 0)),
            row,
            pl.BlockSpec(x_at.shape, lambda b: (0, 0)),
            pl.BlockSpec(table.shape, lambda b: (0, 0)),
            row,
        ],
        out_specs=pl.BlockSpec((slab_total, 1, each, tile), lambda b: (0, b, 0, 0)),
        out_shape=jax.ShapeDtypeStruct((slab_total, tiles, each, tile), jnp.bfloat16),
        scratch_shapes=[
            pltpu.VMEM((tile, 2 * coils * LANES), jnp.bfloat16),
            pltpu.VMEM((unroll, CLASSES, 8, LANES), jnp.float32),
            pltpu.VMEM((unroll, CLASSES, 8, LANES), jnp.float32),
            pltpu.VMEM((RUNS, count, tile // RUNS), jnp.bfloat16),
        ],
        name="grid_x",
    )(pos, samples, seg, x_at, table, spot)

    sent = lax.all_to_all(lines, "slab", 0, 0, tiled=True)
    spots = lax.all_gather(spots, "slab")

    span = 32
    per = math.gcd(chunks, 4)
    steps = chunks // per
    by_chunk = spots[:, :, 0].reshape(slab_total, tiles, chunks, LANES)
    step_down = max(8 // each, 1)
    low = jnp.min(by_chunk, axis=(1, 3)).astype(jnp.int32) // step_down * step_down
    high = (jnp.max(by_chunk, axis=(1, 3)).astype(jnp.int32) - low) // span + 1
    ytab, ztab = right_table(freq), left_table(depth)
    pairs = each // 2
    imaged = pl.pallas_call(
        functools.partial(add_kernel, span, per),
        grid_spec=pltpu.PrefetchScalarGridSpec(
            num_scalar_prefetch=2,
            grid=(slab_total * steps,),
            in_specs=[
                pl.BlockSpec(
                    (1, tiles, each, per * LANES), lambda i, a, b: (i // steps, 0, 0, i % steps)
                ),
                pl.BlockSpec(
                    (1, tiles, 2, per * LANES), lambda i, a, b: (i // steps, 0, 0, i % steps)
                ),
                pl.BlockSpec(ytab.shape, lambda i, a, b: (0, 0)),
                pl.BlockSpec(ztab.shape, lambda i, a, b: (0, 0)),
            ],
            out_specs=pl.BlockSpec((pairs, depth, 2 * freq), lambda i, a, b: (0, 0, 0)),
            scratch_shapes=[
                pltpu.VMEM((freq // LANES, (depth + span) * each, LANES), jnp.float32)
            ],
        ),
        out_shape=jax.ShapeDtypeStruct((pairs, depth, 2 * freq), jnp.bfloat16),
        name="add_yz",
    )(low.reshape(-1), high.reshape(-1), sent, spots, ytab, ztab)

    split = imaged.reshape(pairs, slab_total, planes, 2 * freq)
    split = lax.all_to_all(jnp.swapaxes(split, 0, 1), "slab", 0, 0, tiled=True)
    split = split.reshape(slab_total, coils, x_here, planes, 2 * freq)
    split = jnp.transpose(split, (0, 2, 1, 3, 4)).reshape(
        coil_total, rows_out // coil_total, coils, planes, 2 * freq
    )
    split = lax.all_to_all(split, "coil", 0, 0, tiled=True)
    mine = jnp.transpose(split, (0, 2, 3, 1, 4)).reshape(sensitivity.shape).astype(jnp.float32)
    maps = sensitivity.astype(jnp.float32)
    map_re, map_im = maps[..., :freq], maps[..., freq:]
    img_re, img_im = mine[..., :freq], mine[..., freq:]
    real_part = jnp.sum(map_re * img_re + map_im * img_im, axis=0)
    imag_part = jnp.sum(map_re * img_im - map_im * img_re, axis=0)
    return jnp.concatenate([real_part, imag_part], axis=-1)


def solution(mesh):
    return jax.shard_map(
        per_device,
        mesh=mesh,
        in_specs=(
            P("coil", "slab", None),
            P("slab", None),
            P("slab"),
            P("slab"),
            P("slab", None),
            P(None, "slab", "coil", None),
        ),
        out_specs=P("slab", "coil", None),
        check_vma=False,
    )
```

```python
import functools
import math

import jax
import jax.numpy as jnp
from jax import lax
from jax.experimental import pallas as pl
from jax.experimental.pallas import tpu as pltpu
from jax.sharding import PartitionSpec as P

KX = 256
CELLS = 64
CLASSES = 8
LANES = 128
HALF = LANES // 2
RUNS = 4
STRETCH = HALF // RUNS
SPAN = 40
NT = (((1,), (1,)), ((), ()))


def twiddle(first, second, length):
    phase = (first * second % length).astype(jnp.float32) * (2.0 * math.pi / length)
    scale = 1.0 / math.sqrt(length)
    return (jnp.cos(phase) * scale, jnp.sin(phase) * scale)


def ints(count):
    return jnp.arange(count, dtype=jnp.int32)


def across_table(coils, rows_out, x_here):
    x0 = (KX - rows_out) // 2
    cosine, sine = twiddle(x0 + ints(rows_out)[:, None], ints(CELLS)[None, :], KX)
    upper = jnp.stack([cosine, -sine], axis=1)
    lower = jnp.stack([sine, cosine], axis=1)
    eye = jnp.eye(coils, dtype=jnp.float32)
    tables = []
    for one in (jnp.stack([upper, lower], axis=1), jnp.stack([-lower, upper], axis=1)):
        one = one.reshape(rows_out // x_here, 1, x_here, 2, 1, 2, CELLS)
        one = one * eye[None, :, None, None, :, None, None]
        tables.append(one.reshape(2 * coils * rows_out, 2 * coils * CELLS))
    return jnp.concatenate(tables, axis=0).astype(jnp.bfloat16)


def right_table(length):
    cosine, sine = twiddle(ints(length)[:, None], ints(length)[None, :], length)
    upper = jnp.concatenate([cosine, sine], axis=1)
    lower = jnp.concatenate([-sine, cosine], axis=1)
    return jnp.concatenate([upper, lower], axis=0).astype(jnp.bfloat16)


def left_table(length):
    cosine, sine = twiddle(ints(length)[:, None], ints(length)[None, :], length)
    upper = jnp.concatenate([cosine, -sine], axis=1)
    lower = jnp.concatenate([sine, cosine], axis=1)
    return jnp.concatenate([upper, lower], axis=0).astype(jnp.bfloat16)


def spread_table(table, values):
    at = ints(2 * CELLS) % CELLS
    cell = CLASSES * (at % CLASSES) + at // CLASSES
    table = table.reshape(table.shape[0], values, CELLS)[:, :, cell]
    return table.reshape(table.shape[0], values * 2 * CELLS)


def hot_rows(spots, depth):
    level = lax.broadcasted_iota(jnp.int32, (16, spots.shape[1]), 0).astype(jnp.float32)
    spots = jnp.broadcast_to(spots, (16, spots.shape[1])).astype(jnp.bfloat16)
    one, none = jnp.bfloat16(1), jnp.bfloat16(0)
    return jnp.concatenate(
        [
            jnp.where((level + at).astype(jnp.bfloat16) == spots, one, none)
            for at in range(0, depth, 16)
        ],
        axis=0,
    )


def permute(values, spots):
    depth = spots.shape[1]
    level = lax.broadcasted_iota(jnp.int32, (depth, depth), 0).astype(jnp.float32)
    hot = jnp.where(level == spots, 1.0, 0.0).astype(jnp.bfloat16)
    return lax.dot_general(values, hot, NT, preferred_element_type=jnp.float32)


def regroup(runs):
    rows, length = runs[0].shape
    place = lax.broadcasted_iota(jnp.int32, (rows, LANES), 1) % HALF // STRETCH
    for at in range(length // (2 * STRETCH)):
        cut = slice(at // RUNS * LANES, at // RUNS * LANES + LANES)
        out = runs[0][:, cut]
        for run in range(1, RUNS):
            out = jnp.where(place == (at + run) % RUNS, runs[run][:, cut], out)
        yield at, out


def order_kernel(planes, freq, kz_ref, ky_ref, spot_ref, sorted_ref):
    tile = kz_ref.shape[1]
    length = tile // RUNS
    pieces = length // LANES
    runs = []
    for run in range(RUNS):
        cut = slice(run * length, (run + 1) * length)
        kz, ky = kz_ref[:, cut], ky_ref[:, cut]
        lane = lax.broadcasted_iota(jnp.int32, (1, length), 1).astype(jnp.float32)
        key = kz * float(length) + lane
        rank = jnp.zeros((1, length), jnp.float32)
        for piece in range(pieces):
            part = key[:, piece * LANES : (piece + 1) * LANES]
            part = jnp.broadcast_to(part, (LANES, LANES)).T
            part = jnp.concatenate([part] * pieces, axis=1)
            rank = rank + jnp.sum(jnp.where(part < key, 1.0, 0.0), axis=0, keepdims=True)
        rank = rank.astype(jnp.int32)
        seat = rank // (2 * STRETCH)
        spot = seat // RUNS * LANES + rank // STRETCH % 2 * HALF
        spot = spot + (seat + run) % RUNS * STRETCH + rank % STRETCH
        spot = spot.astype(jnp.float32)
        spot_ref[:, cut] = spot
        both = jnp.concatenate([kz, ky, jnp.zeros((14, length), jnp.float32)], axis=0)
        runs.append(permute(both.astype(jnp.bfloat16), spot))
    for at, out in regroup(runs):
        sorted_ref[0, :, at * LANES : (at + 1) * LANES] = out[:2]


def grid_kernel(
    coils, unroll, pos_ref, val_ref, seg_ref, x_ref, tab_ref, spot_ref, out_ref,
    cells, near, bump, placed,
):
    slabs, _, each, tile = out_ref.shape
    rows = slabs * each
    length = tile // RUNS
    block = lax.broadcasted_iota(jnp.int32, (16, LANES), 0)
    upper = lax.broadcasted_iota(jnp.int32, (16, LANES), 1) >= CELLS
    odd = block % 2 == 1
    own = [block % 4 // 2 == half for half in range(2)]
    mine = block // 4 % 2 == upper.astype(jnp.int32)
    level = lax.broadcasted_iota(jnp.int32, (CLASSES, LANES), 0).astype(jnp.float32)

    def step(g, slot):
        at = pl.ds(pl.multiple_of(g * 16, 16), 16)
        left = []
        for c in range(coils):
            straight = val_ref[c, at, :].astype(jnp.float32)
            turned = pltpu.roll(straight, CELLS, 1)
            for low, high in ((straight, turned), (turned, straight)):
                placed_here = jnp.where(
                    odd, jnp.where(upper, high, 0.0), jnp.where(upper, 0.0, low)
                )
                halves = [jnp.where(own[half], placed_here, 0.0) for half in range(2)]
                left.append(jnp.concatenate(halves, axis=1).astype(jnp.bfloat16))
        place = pos_ref[pl.ds(pl.multiple_of(g * 8, 8), 8), :].astype(jnp.float32) * 0.125
        for r in range(CLASSES):
            offset = place - ((r + 0.5) * 0.125 - 0.5)
            seat = jnp.floor(offset)
            offset = (offset - seat) * 3.2 - 1.6
            rise = jnp.maximum(1.0 - offset * offset, 0.0)
            near[slot, r] = seat
            bump[slot, r] = rise * rise
        right = []
        for quad in range(4):
            halves = []
            for half in range(2):
                row = pl.ds(2 * quad + half, 1)
                parts = []
                for r in range(CLASSES):
                    seat = jnp.broadcast_to(near[slot, r, row, :], level.shape)
                    high = jnp.broadcast_to(bump[slot, r, row, :], level.shape)
                    parts.append(jnp.where(level == seat, high, 0.0))
                halves.append(jnp.concatenate(parts, axis=0).astype(jnp.bfloat16))
            right.append(jnp.concatenate(halves, axis=1))
        done = lax.dot_general(
            jnp.concatenate(left, axis=0),
            jnp.concatenate(right, axis=0),
            NT,
            preferred_element_type=jnp.float32,
        )
        for v in range(2 * coils):
            first = done[16 * v : 16 * v + 8, :LANES]
            second = done[16 * v + 8 : 16 * v + 16, LANES:]
            both = jnp.where(mine, jnp.concatenate([first, second], axis=0), 0.0)
            cells[at, LANES * v : LANES * (v + 1)] = both.astype(jnp.bfloat16)

    @pl.loop(0, tile // (16 * unroll))
    def _(outer):
        for slot in range(unroll):
            step(outer * unroll + slot, slot)

    for run in range(RUNS):
        cut = slice(run * length, (run + 1) * length)
        moved = lax.dot_general(
            tab_ref[...], cells[cut, :], NT, preferred_element_type=jnp.float32
        )
        turn = (x_ref[...] * seg_ref[:, cut]) & 3
        turned = jnp.where((turn & 1) == 0, moved[:rows], moved[rows:])
        turned = jnp.where(turn >= 2, -turned, turned).astype(jnp.bfloat16)
        placed[run] = permute(turned, spot_ref[:, cut]).astype(jnp.bfloat16)
    for at, out in regroup([placed.at[run] for run in range(RUNS)]):
        for slab in range(slabs):
            out_ref[slab, 0, :, at * LANES : (at + 1) * LANES] = out[
                slab * each : (slab + 1) * each
            ]


def add_kernel(
    per, lo_ref, more_ref, vals_ref, spot_ref, ytab_ref, ztab_ref, out_ref, total
):
    step = pl.program_id(0)
    tiles, rows = vals_ref.shape[1], vals_ref.shape[2]
    pairs, depth, freq = out_ref.shape[0], out_ref.shape[1], out_ref.shape[2] // 2
    deep = 16 // rows
    width = tiles * HALF
    inner = (lax.broadcasted_iota(jnp.int32, (16, width), 0) // rows).astype(jnp.float32)

    @pl.when(step == 0)
    def _():
        total[...] = jnp.zeros_like(total)

    def pick(part, read):
        cut = slice(part // 2 * LANES, part // 2 * LANES + LANES)
        out = []
        for t in range(0, tiles, 2):
            first, second = read(t, cut), read(t + 1, cut)
            low = lax.broadcasted_iota(jnp.int32, first.shape, 1) < HALF
            if part % 2 == 0:
                second = pltpu.roll(second, HALF, 1)
            else:
                first = pltpu.roll(first, HALF, 1)
            out.append(jnp.where(low, first, second))
        return jnp.concatenate(out, axis=1)

    def add(part, start):
        vals = pick(part, lambda t, cut: vals_ref[0, t, :, cut].astype(jnp.float32))
        vals = jnp.concatenate([vals] * deep, axis=0).astype(jnp.bfloat16)
        both = pick(part, lambda t, cut: spot_ref[0, t, :, cut])
        base = jnp.full((16, width), start, jnp.int32).astype(jnp.float32)
        plane = jnp.broadcast_to(both[0:1], (16, width)) - base - inner
        plane = plane.astype(jnp.bfloat16)
        left = [
            jnp.where(plane == jnp.bfloat16(at), vals, jnp.bfloat16(0))
            for at in range(0, SPAN, deep)
        ]
        moved = lax.dot_general(
            jnp.concatenate(left, axis=0),
            hot_rows(both[1:2], freq),
            NT,
            preferred_element_type=jnp.float32,
        )
        at = pl.ds(pl.multiple_of(start * rows, 8), SPAN * rows)
        for half in range(freq // LANES):
            total[half, at, :] += moved[:, half * LANES : (half + 1) * LANES]

    for part in range(per):
        add(part, lo_ref[step * per + part])

    for part in range(per):
        first = lo_ref[step * per + part]

        def again(at, carry):
            add(part, first + at * SPAN)
            return carry

        lax.fori_loop(1, more_ref[step * per + part], again, 0)

    @pl.when(step == pl.num_programs(0) - 1)
    def _():
        for pair in range(pairs):
            both = jnp.concatenate(
                [
                    total[half, pl.ds(2 * pair + part, depth, stride=rows), :]
                    for part in range(2)
                    for half in range(freq // LANES)
                ],
                axis=1,
            )
            planes = jnp.dot(
                both.astype(jnp.bfloat16), ytab_ref[...], preferred_element_type=jnp.float32
            ).astype(jnp.bfloat16)
            planes = jnp.concatenate([planes[:, :freq], planes[:, freq:]], axis=0)
            image = jnp.dot(ztab_ref[...], planes, preferred_element_type=jnp.float32)
            out_ref[pair, :, :freq] = image[:depth].astype(jnp.bfloat16)
            out_ref[pair, :, freq:] = image[depth:].astype(jnp.bfloat16)


def whole(memory=pltpu.VMEM):
    return pl.BlockSpec(memory_space=memory)


def per_device(samples, sample_pos, block_count, grid_block, block_slab, sensitivity):
    slab_total = lax.axis_size("slab")
    coil_total = lax.axis_size("coil")
    coils = samples.shape[0]
    blocks = samples.shape[1]
    planes = sensitivity.shape[1]
    rows_out = sensitivity.shape[2] * coil_total
    depth = planes * slab_total
    freq = sensitivity.shape[3] // 2
    x_here = rows_out // slab_total
    segments = KX // CELLS

    live = ints(CELLS)[None, :] < block_count[:, None]
    pos = jnp.where(live, sample_pos, 9984.0).reshape(blocks // 2, 2 * CELLS)
    seg = (grid_block % segments)[None, :]
    kz = block_slab[:, 0] * planes + grid_block // (segments * freq)
    ky = grid_block // segments % freq
    kz, ky = kz.astype(jnp.float32)[None, :], ky.astype(jnp.float32)[None, :]

    tile = math.gcd(blocks, 2048)
    tiles = blocks // tile
    chunks = tile // LANES
    unroll = math.gcd(tile // 16, 16)
    count = 2 * coils * rows_out
    each = 2 * coils * x_here

    row = pl.BlockSpec((1, tile), lambda b: (0, b))
    spot, spots = pl.pallas_call(
        functools.partial(order_kernel, planes, freq),
        grid=(tiles,),
        in_specs=[row, row],
        out_specs=[row, pl.BlockSpec((1, 2, tile), lambda b: (b, 0, 0))],
        out_shape=[
            jax.ShapeDtypeStruct((1, blocks), jnp.float32),
            jax.ShapeDtypeStruct((tiles, 2, tile), jnp.float32),
        ],
        name="order_kz",
    )(kz, ky)

    table = spread_table(across_table(coils, rows_out, x_here), 2 * coils)
    x_at = (ints(count) // (2 * coils * x_here)) * x_here + ints(count) // 2 % x_here
    x_at = jnp.broadcast_to((x_at + (KX - rows_out) // 2)[:, None], (count, tile // RUNS))
    lines = pl.pallas_call(
        functools.partial(grid_kernel, coils, unroll),
        grid=(tiles,),
        in_specs=[
            pl.BlockSpec((tile // 2, LANES), lambda b: (b, 0)),
            pl.BlockSpec((coils, tile, LANES), lambda b: (0, b, 0)),
            row,
            pl.BlockSpec(x_at.shape, lambda b: (0, 0)),
            pl.BlockSpec(table.shape, lambda b: (0, 0)),
            row,
        ],
        out_specs=pl.BlockSpec((slab_total, 1, each, tile), lambda b: (0, b, 0, 0)),
        out_shape=jax.ShapeDtypeStruct((slab_total, tiles, each, tile), jnp.bfloat16),
        scratch_shapes=[
            pltpu.VMEM((tile, 2 * coils * LANES), jnp.bfloat16),
            pltpu.VMEM((unroll, CLASSES, 8, LANES), jnp.float32),
            pltpu.VMEM((unroll, CLASSES, 8, LANES), jnp.float32),
            pltpu.VMEM((RUNS, count, tile // RUNS), jnp.bfloat16),
        ],
        name="grid_x",
    )(pos, samples, seg, x_at, table, spot)

    sent = lax.all_to_all(lines, "slab", 0, 0, tiled=True)
    spots = lax.all_gather(spots, "slab")

    per = math.gcd(chunks, 4)
    steps = chunks // per
    by_chunk = spots[:, :, 0].reshape(slab_total, tiles, 2 * chunks, HALF)
    step_down = max(8 // each, 1)
    low = jnp.min(by_chunk, axis=(1, 3)).astype(jnp.int32) // step_down * step_down
    high = (jnp.max(by_chunk, axis=(1, 3)).astype(jnp.int32) - low) // SPAN + 1
    ytab, ztab = right_table(freq), left_table(depth)
    pairs = each // 2
    imaged = pl.pallas_call(
        functools.partial(add_kernel, 2 * per),
        grid_spec=pltpu.PrefetchScalarGridSpec(
            num_scalar_prefetch=2,
            grid=(slab_total * steps,),
            in_specs=[
                pl.BlockSpec(
                    (1, tiles, each, per * LANES), lambda i, a, b: (i // steps, 0, 0, i % steps)
                ),
                pl.BlockSpec(
                    (1, tiles, 2, per * LANES), lambda i, a, b: (i // steps, 0, 0, i % steps)
                ),
                pl.BlockSpec(ytab.shape, lambda i, a, b: (0, 0)),
                pl.BlockSpec(ztab.shape, lambda i, a, b: (0, 0)),
            ],
            out_specs=pl.BlockSpec((pairs, depth, 2 * freq), lambda i, a, b: (0, 0, 0)),
            scratch_shapes=[
                pltpu.VMEM((freq // LANES, (depth + SPAN) * each, LANES), jnp.float32)
            ],
        ),
        out_shape=jax.ShapeDtypeStruct((pairs, depth, 2 * freq), jnp.bfloat16),
        name="add_yz",
    )(low.reshape(-1), high.reshape(-1), sent, spots, ytab, ztab)

    split = imaged.reshape(pairs, slab_total, planes, 2 * freq)
    split = lax.all_to_all(jnp.swapaxes(split, 0, 1), "slab", 0, 0, tiled=True)
    split = split.reshape(slab_total, coils, x_here, planes, 2 * freq)
    split = jnp.transpose(split, (0, 2, 1, 3, 4)).reshape(
        coil_total, rows_out // coil_total, coils, planes, 2 * freq
    )
    split = lax.all_to_all(split, "coil", 0, 0, tiled=True)
    mine = jnp.transpose(split, (0, 2, 3, 1, 4)).reshape(sensitivity.shape).astype(jnp.float32)
    maps = sensitivity.astype(jnp.float32)
    map_re, map_im = maps[..., :freq], maps[..., freq:]
    img_re, img_im = mine[..., :freq], mine[..., freq:]
    real_part = jnp.sum(map_re * img_re + map_im * img_im, axis=0)
    imag_part = jnp.sum(map_re * img_im - map_im * img_re, axis=0)
    return jnp.concatenate([real_part, imag_part], axis=-1)


def solution(mesh):
    return jax.shard_map(
        per_device,
        mesh=mesh,
        in_specs=(
            P("coil", "slab", None),
            P("slab", None),
            P("slab"),
            P("slab"),
            P("slab", None),
            P(None, "slab", "coil", None),
        ),
        out_specs=P("slab", "coil", None),
        check_vma=False,
    )
```

```python
import functools
import math

import jax
import jax.numpy as jnp
from jax import lax
from jax.experimental import pallas as pl
from jax.experimental.pallas import tpu as pltpu
from jax.sharding import PartitionSpec as P

KX = 256
CELLS = 64
CLASSES = 8
LANES = 128
HALF = LANES // 2
RUNS = 4
STRETCH = HALF // RUNS
SPAN = 40
NT = (((1,), (1,)), ((), ()))
MESH = pl.DeviceIdType.MESH


def twiddle(first, second, length):
    phase = (first * second % length).astype(jnp.float32) * (2.0 * math.pi / length)
    scale = 1.0 / math.sqrt(length)
    return (jnp.cos(phase) * scale, jnp.sin(phase) * scale)


def ints(count):
    return jnp.arange(count, dtype=jnp.int32)


def across_table(coils, rows_out, x_here):
    x0 = (KX - rows_out) // 2
    cosine, sine = twiddle(x0 + ints(rows_out)[:, None], ints(CELLS)[None, :], KX)
    upper = jnp.stack([cosine, -sine], axis=1)
    lower = jnp.stack([sine, cosine], axis=1)
    eye = jnp.eye(coils, dtype=jnp.float32)
    tables = []
    for one in (jnp.stack([upper, lower], axis=1), jnp.stack([-lower, upper], axis=1)):
        one = one.reshape(rows_out // x_here, 1, x_here, 2, 1, 2, CELLS)
        one = one * eye[None, :, None, None, :, None, None]
        tables.append(one.reshape(2 * coils * rows_out, 2 * coils * CELLS))
    return jnp.concatenate(tables, axis=0).astype(jnp.bfloat16)


def right_table(length):
    cosine, sine = twiddle(ints(length)[:, None], ints(length)[None, :], length)
    upper = jnp.concatenate([cosine, sine], axis=1)
    lower = jnp.concatenate([-sine, cosine], axis=1)
    return jnp.concatenate([upper, lower], axis=0).astype(jnp.bfloat16)


def left_table(length):
    cosine, sine = twiddle(ints(length)[:, None], ints(length)[None, :], length)
    upper = jnp.concatenate([cosine, -sine], axis=1)
    lower = jnp.concatenate([sine, cosine], axis=1)
    return jnp.concatenate([upper, lower], axis=0).astype(jnp.bfloat16)


def spread_table(table, values):
    at = ints(2 * CELLS) % CELLS
    cell = CLASSES * (at % CLASSES) + at // CLASSES
    table = table.reshape(table.shape[0], values, CELLS)[:, :, cell]
    return table.reshape(table.shape[0], values * 2 * CELLS)


def hot_rows(spots, depth):
    level = lax.broadcasted_iota(jnp.int32, (16, spots.shape[1]), 0).astype(jnp.float32)
    spots = jnp.broadcast_to(spots, (16, spots.shape[1])).astype(jnp.bfloat16)
    one, none = jnp.bfloat16(1), jnp.bfloat16(0)
    return jnp.concatenate(
        [
            jnp.where((level + at).astype(jnp.bfloat16) == spots, one, none)
            for at in range(0, depth, 16)
        ],
        axis=0,
    )


def permute(values, spots):
    depth = spots.shape[1]
    level = lax.broadcasted_iota(jnp.int32, (depth, depth), 0).astype(jnp.float32)
    hot = jnp.where(level == spots, 1.0, 0.0).astype(jnp.bfloat16)
    return lax.dot_general(values, hot, NT, preferred_element_type=jnp.float32)


def regroup(runs):
    rows, length = runs[0].shape
    place = lax.broadcasted_iota(jnp.int32, (rows, LANES), 1) % HALF // STRETCH
    for at in range(length // (2 * STRETCH)):
        cut = slice(at // RUNS * LANES, at // RUNS * LANES + LANES)
        out = runs[0][:, cut]
        for run in range(1, RUNS):
            out = jnp.where(place == (at + run) % RUNS, runs[run][:, cut], out)
        yield at, out


def order_kernel(planes, freq, kz_ref, ky_ref, spot_ref, sorted_ref):
    tile = kz_ref.shape[1]
    length = tile // RUNS
    pieces = length // LANES
    runs = []
    for run in range(RUNS):
        cut = slice(run * length, (run + 1) * length)
        kz, ky = kz_ref[:, cut], ky_ref[:, cut]
        lane = lax.broadcasted_iota(jnp.int32, (1, length), 1).astype(jnp.float32)
        key = kz * float(length) + lane
        rank = jnp.zeros((1, length), jnp.float32)
        for piece in range(pieces):
            part = key[:, piece * LANES : (piece + 1) * LANES]
            part = jnp.broadcast_to(part, (LANES, LANES)).T
            part = jnp.concatenate([part] * pieces, axis=1)
            rank = rank + jnp.sum(jnp.where(part < key, 1.0, 0.0), axis=0, keepdims=True)
        rank = rank.astype(jnp.int32)
        seat = rank // (2 * STRETCH)
        spot = seat // RUNS * LANES + rank // STRETCH % 2 * HALF
        spot = spot + (seat + run) % RUNS * STRETCH + rank % STRETCH
        spot = spot.astype(jnp.float32)
        spot_ref[:, cut] = spot
        both = jnp.concatenate([kz, ky, jnp.zeros((14, length), jnp.float32)], axis=0)
        runs.append(permute(both.astype(jnp.bfloat16), spot))
    for at, out in regroup(runs):
        sorted_ref[0, :, at * LANES : (at + 1) * LANES] = out[:2]


def grid_kernel(
    coils, unroll, pos_ref, val_ref, seg_ref, x_ref, tab_ref, spot_ref, spots_ref, map_ref,
    lines_ref, every_ref, maps_ref,
    cells, near, bump, placed, ready, line_out, line_in, line_own,
    spots_out, spots_in, spots_own, map_out, map_in, map_own,
):
    turn_at = pl.program_id(0)
    tiles, slabs, each, tile = ready.shape
    rows = slabs * each
    deals, shares = map_ref.shape[0], map_ref.shape[1]
    slab, coil = lax.axis_index("slab"), lax.axis_index("coil")
    barrier = pltpu.get_barrier_semaphore()
    here = slab // shares == coil

    def line_copy(at, hop):
        peer = lax.rem(slab + hop, slabs)
        return pltpu.make_async_remote_copy(
            ready.at[at, peer], lines_ref.at[slab, at], line_out.at[at, hop], line_in.at[at, hop],
            device_id={"slab": peer}, device_id_type=MESH,
        )

    def line_keep(at):
        return pltpu.make_async_copy(
            ready.at[at, slab], lines_ref.at[slab, at], line_own.at[at]
        )

    def spots_copy(hop):
        peer = lax.rem(slab + hop, slabs)
        return pltpu.make_async_remote_copy(
            spots_ref, every_ref.at[slab], spots_out.at[hop], spots_in.at[hop],
            device_id={"slab": peer}, device_id_type=MESH,
        )

    def spots_keep():
        return pltpu.make_async_copy(spots_ref, every_ref.at[slab], spots_own)

    def map_copy(deal, share):
        return pltpu.make_async_remote_copy(
            map_ref.at[deal, share], maps_ref.at[slab],
            map_out.at[deal, share], map_in.at[slab],
            device_id={"slab": coil * shares + share, "coil": deal}, device_id_type=MESH,
        )

    def map_take(source):
        return pltpu.make_async_remote_copy(
            map_ref.at[0, 0], maps_ref.at[source], map_out.at[0, 0], map_in.at[source],
            device_id={"slab": slab, "coil": coil}, device_id_type=MESH,
        )

    def map_keep():
        return pltpu.make_async_copy(
            map_ref.at[coil, lax.rem(slab, shares)], maps_ref.at[slab], map_own
        )

    def is_me(deal, share):
        return jnp.logical_and(coil * shares + share == slab, coil == deal)

    @pl.when(turn_at == 0)
    def _():
        for hop in range(1, slabs):
            pl.semaphore_signal(
                barrier, 1, device_id={"slab": lax.rem(slab + hop, slabs)}, device_id_type=MESH
            )
        for source in range(slabs):
            @pl.when(jnp.logical_not(jnp.logical_and(here, source == slab)))
            def _():
                pl.semaphore_signal(
                    barrier, 1, device_id={"slab": source, "coil": slab // shares},
                    device_id_type=MESH,
                )
    length = tile // RUNS
    block = lax.broadcasted_iota(jnp.int32, (16, LANES), 0)
    upper = lax.broadcasted_iota(jnp.int32, (16, LANES), 1) >= CELLS
    odd = block % 2 == 1
    own = [block % 4 // 2 == half for half in range(2)]
    mine = block // 4 % 2 == upper.astype(jnp.int32)
    level = lax.broadcasted_iota(jnp.int32, (CLASSES, LANES), 0).astype(jnp.float32)

    def step(g, slot):
        at = pl.ds(pl.multiple_of(g * 16, 16), 16)
        left = []
        for c in range(coils):
            straight = val_ref[c, at, :].astype(jnp.float32)
            turned = pltpu.roll(straight, CELLS, 1)
            for low, high in ((straight, turned), (turned, straight)):
                placed_here = jnp.where(
                    odd, jnp.where(upper, high, 0.0), jnp.where(upper, 0.0, low)
                )
                halves = [jnp.where(own[half], placed_here, 0.0) for half in range(2)]
                left.append(jnp.concatenate(halves, axis=1).astype(jnp.bfloat16))
        place = pos_ref[pl.ds(pl.multiple_of(g * 8, 8), 8), :].astype(jnp.float32) * 0.125
        for r in range(CLASSES):
            offset = place - ((r + 0.5) * 0.125 - 0.5)
            seat = jnp.floor(offset)
            offset = (offset - seat) * 3.2 - 1.6
            rise = jnp.maximum(1.0 - offset * offset, 0.0)
            near[slot, r] = seat
            bump[slot, r] = rise * rise
        right = []
        for quad in range(4):
            halves = []
            for half in range(2):
                row = pl.ds(2 * quad + half, 1)
                parts = []
                for r in range(CLASSES):
                    seat = jnp.broadcast_to(near[slot, r, row, :], level.shape)
                    high = jnp.broadcast_to(bump[slot, r, row, :], level.shape)
                    parts.append(jnp.where(level == seat, high, 0.0))
                halves.append(jnp.concatenate(parts, axis=0).astype(jnp.bfloat16))
            right.append(jnp.concatenate(halves, axis=1))
        done = lax.dot_general(
            jnp.concatenate(left, axis=0),
            jnp.concatenate(right, axis=0),
            NT,
            preferred_element_type=jnp.float32,
        )
        for v in range(2 * coils):
            first = done[16 * v : 16 * v + 8, :LANES]
            second = done[16 * v + 8 : 16 * v + 16, LANES:]
            both = jnp.where(mine, jnp.concatenate([first, second], axis=0), 0.0)
            cells[at, LANES * v : LANES * (v + 1)] = both.astype(jnp.bfloat16)

    @pl.loop(0, tile // (16 * unroll))
    def _(outer):
        for slot in range(unroll):
            step(outer * unroll + slot, slot)

    for run in range(RUNS):
        cut = slice(run * length, (run + 1) * length)
        moved = lax.dot_general(
            tab_ref[...], cells[cut, :], NT, preferred_element_type=jnp.float32
        )
        turn = (x_ref[...] * seg_ref[:, cut]) & 3
        turned = jnp.where((turn & 1) == 0, moved[:rows], moved[rows:])
        turned = jnp.where(turn >= 2, -turned, turned).astype(jnp.bfloat16)
        placed[run] = permute(turned, spot_ref[:, cut]).astype(jnp.bfloat16)
    for at, out in regroup([placed.at[run] for run in range(RUNS)]):
        for owner in range(slabs):
            ready[turn_at, owner, :, at * LANES : (at + 1) * LANES] = out[
                owner * each : (owner + 1) * each
            ]

    @pl.when(turn_at == 0)
    def _():
        pl.semaphore_wait(barrier, slabs - 1 + deals * shares - here.astype(jnp.int32))
        spots_keep().start()
        for hop in range(1, slabs):
            spots_copy(hop).start()
        for deal in range(deals):
            for share in range(shares):
                @pl.when(jnp.logical_not(is_me(deal, share)))
                def _():
                    map_copy(deal, share).start()

        @pl.when(here)
        def _():
            map_keep().start()

    for hop in range(1, slabs):
        line_copy(turn_at, hop).start()
    line_keep(turn_at).start()

    @pl.when(turn_at == tiles - 1)
    def _():
        spots_keep().wait()
        for hop in range(1, slabs):
            spots_copy(hop).wait()
        for deal in range(deals):
            for share in range(shares):
                @pl.when(jnp.logical_not(is_me(deal, share)))
                def _():
                    map_copy(deal, share).wait_send()
        for source in range(slabs):
            @pl.when(jnp.logical_not(jnp.logical_and(here, source == slab)))
            def _():
                map_take(source).wait_recv()

        @pl.when(here)
        def _():
            map_keep().wait()

        for at in range(tiles):
            line_keep(at).wait()
            for hop in range(1, slabs):
                line_copy(at, hop).wait()


def add_kernel(
    per, lo_ref, more_ref, vals_ref, spot_ref, out_ref, total
):
    step = pl.program_id(0)
    tiles, rows = vals_ref.shape[1], vals_ref.shape[2]
    pairs, depth, freq = out_ref.shape[0], out_ref.shape[1], out_ref.shape[2] // 2
    deep = 16 // rows
    width = tiles * HALF
    inner = (lax.broadcasted_iota(jnp.int32, (16, width), 0) // rows).astype(jnp.float32)

    @pl.when(step == 0)
    def _():
        total[...] = jnp.zeros_like(total)

    def pick(part, read):
        cut = slice(part // 2 * LANES, part // 2 * LANES + LANES)
        out = []
        for t in range(0, tiles, 2):
            first, second = read(t, cut), read(t + 1, cut)
            low = lax.broadcasted_iota(jnp.int32, first.shape, 1) < HALF
            if part % 2 == 0:
                second = pltpu.roll(second, HALF, 1)
            else:
                first = pltpu.roll(first, HALF, 1)
            out.append(jnp.where(low, first, second))
        return jnp.concatenate(out, axis=1)

    def add(part, start):
        vals = pick(part, lambda t, cut: vals_ref[0, t, :, cut].astype(jnp.float32))
        vals = jnp.concatenate([vals] * deep, axis=0).astype(jnp.bfloat16)
        both = pick(part, lambda t, cut: spot_ref[0, t, :, cut])
        base = jnp.full((16, width), start, jnp.int32).astype(jnp.float32)
        plane = jnp.broadcast_to(both[0:1], (16, width)) - base - inner
        plane = plane.astype(jnp.bfloat16)
        left = [
            jnp.where(plane == jnp.bfloat16(at), vals, jnp.bfloat16(0))
            for at in range(0, SPAN, deep)
        ]
        moved = lax.dot_general(
            jnp.concatenate(left, axis=0),
            hot_rows(both[1:2], freq),
            NT,
            preferred_element_type=jnp.float32,
        )
        at = pl.ds(pl.multiple_of(start * rows, 8), SPAN * rows)
        for half in range(freq // LANES):
            total[half, at, :] += moved[:, half * LANES : (half + 1) * LANES]

    for part in range(per):
        add(part, lo_ref[step * per + part])

    for part in range(per):
        first = lo_ref[step * per + part]

        def again(at, carry):
            add(part, first + at * SPAN)
            return carry

        lax.fori_loop(1, more_ref[step * per + part], again, 0)

    @pl.when(step == pl.num_programs(0) - 1)
    def _():
        for pair in range(pairs):
            for part in range(2):
                for half in range(freq // LANES):
                    start = part * freq + half * LANES
                    found = total[half, pl.ds(2 * pair + part, depth, stride=rows), :]
                    out_ref[pair, :, start : start + LANES] = found.astype(jnp.bfloat16)


def image_kernel(
    rows_ref, map_ref, ytab_ref, ztab_ref, out_ref, ready, near, far,
    near_out, near_in, far_out, far_in,
):
    wide, slabs, planes, _ = ready.shape
    coils = rows_ref.shape[0] // wide
    deals, shares = far.shape[0], far.shape[1]
    depth, freq = rows_ref.shape[1], rows_ref.shape[2] // 2
    slab, coil = lax.axis_index("slab"), lax.axis_index("coil")
    barrier = pltpu.get_barrier_semaphore()
    for hop in range(1, slabs):
        peer = {"slab": lax.rem(slab + hop, slabs)}
        pl.semaphore_signal(barrier, 1, device_id=peer, device_id_type=MESH)
    for hop in range(1, deals):
        peer = {"coil": lax.rem(coil + hop, deals)}
        pl.semaphore_signal(barrier, 1, device_id=peer, device_id_type=MESH)

    def near_copy(x, hop):
        peer = lax.rem(slab + hop, slabs)
        return pltpu.make_async_remote_copy(
            ready.at[x, peer], near.at[x, slab], near_out.at[x, hop], near_in.at[x, hop],
            device_id={"slab": peer}, device_id_type=MESH,
        )

    def far_copy(x, source, hop):
        share = lax.rem(source, shares)
        return pltpu.make_async_remote_copy(
            near.at[x, source], far.at[hop, share, x],
            far_out.at[hop, share, x], far_in.at[hop, share, x],
            device_id={"coil": lax.rem(coil + hop, deals)}, device_id_type=MESH,
        )

    for x in range(wide):
        real = imag = 0.0
        for c in range(coils):
            planar = jnp.dot(
                rows_ref[c * wide + x], ytab_ref[...], preferred_element_type=jnp.float32
            ).astype(jnp.bfloat16)
            planar = jnp.concatenate([planar[:, :freq], planar[:, freq:]], axis=0)
            image = jnp.dot(ztab_ref[...], planar, preferred_element_type=jnp.float32)
            image = image.astype(jnp.bfloat16).astype(jnp.float32)
            img_re, img_im = image[:depth], image[depth:]
            maps = map_ref[:, c, x].reshape(depth, 2 * freq).astype(jnp.float32)
            map_re, map_im = maps[:, :freq], maps[:, freq:]
            real = real + (map_re * img_re + map_im * img_im)
            imag = imag + (map_re * img_im - map_im * img_re)
        both = jnp.concatenate([real, imag], axis=1).astype(jnp.bfloat16)
        ready[x] = both.reshape(slabs, planes, 2 * freq)
        near[x, pl.ds(slab, 1)] = ready[x, pl.ds(slab, 1)]
        if x == 0:
            pl.semaphore_wait(barrier, slabs - 1 + deals - 1)
        for hop in range(1, slabs):
            near_copy(x, hop).start()

    for x in range(wide):
        for hop in range(slabs):
            source = lax.rem(slab + slabs - hop, slabs)
            if hop > 0:
                near_copy(x, hop).wait_recv()
            leap = lax.rem(source // shares + deals - coil, deals)

            @pl.when(leap > 0)
            def _():
                far_copy(x, source, leap).start()

    for x in range(wide):
        for share in range(shares):
            value = near[x, coil * shares + share].astype(jnp.float32)
            for hop in range(1, deals):
                far_copy(x, share, hop).wait_recv()
                value = value + far[hop, share, x].astype(jnp.float32)
            out_ref[:, share * wide + x, :] = value
    for x in range(wide):
        for hop in range(1, slabs):
            near_copy(x, hop).wait_send()
        for share in range(shares):
            for hop in range(1, deals):
                far_copy(x, share, hop).wait_send()


def per_device(samples, sample_pos, block_count, grid_block, block_slab, sensitivity):
    slab_total = lax.axis_size("slab")
    coil_total = lax.axis_size("coil")
    coils = samples.shape[0]
    blocks = samples.shape[1]
    planes = sensitivity.shape[1]
    rows_out = sensitivity.shape[2] * coil_total
    depth = planes * slab_total
    freq = sensitivity.shape[3] // 2
    x_here = rows_out // slab_total
    segments = KX // CELLS

    live = ints(CELLS)[None, :] < block_count[:, None]
    pos = jnp.where(live, sample_pos, 9984.0).reshape(blocks // 2, 2 * CELLS)
    seg = (grid_block % segments)[None, :]
    kz = block_slab[:, 0] * planes + grid_block // (segments * freq)
    ky = grid_block // segments % freq
    kz, ky = kz.astype(jnp.float32)[None, :], ky.astype(jnp.float32)[None, :]

    tile = math.gcd(blocks, 2048)
    tiles = blocks // tile
    chunks = tile // LANES
    unroll = math.gcd(tile // 16, 16)
    count = 2 * coils * rows_out
    each = 2 * coils * x_here

    row = pl.BlockSpec((1, tile), lambda b: (0, b))
    spot, spots = pl.pallas_call(
        functools.partial(order_kernel, planes, freq),
        grid=(tiles,),
        in_specs=[row, row],
        out_specs=[row, pl.BlockSpec((1, 2, tile), lambda b: (b, 0, 0))],
        out_shape=[
            jax.ShapeDtypeStruct((1, blocks), jnp.float32),
            jax.ShapeDtypeStruct((tiles, 2, tile), jnp.float32),
        ],
        name="order_kz",
    )(kz, ky)

    table = spread_table(across_table(coils, rows_out, x_here), 2 * coils)
    x_at = (ints(count) // (2 * coils * x_here)) * x_here + ints(count) // 2 % x_here
    x_at = jnp.broadcast_to((x_at + (KX - rows_out) // 2)[:, None], (count, tile // RUNS))
    x_own = sensitivity.shape[2]
    maps = sensitivity.reshape(
        coil_total, coils, planes, x_own // x_here, x_here, 2 * freq
    ).transpose(0, 3, 1, 4, 2, 5)
    anywhere = pl.BlockSpec(memory_space=pl.ANY)
    sent, spots, maps = pl.pallas_call(
        functools.partial(grid_kernel, coils, unroll),
        grid=(tiles,),
        in_specs=[
            pl.BlockSpec((tile // 2, LANES), lambda b: (b, 0)),
            pl.BlockSpec((coils, tile, LANES), lambda b: (0, b, 0)),
            row,
            pl.BlockSpec(x_at.shape, lambda b: (0, 0)),
            pl.BlockSpec(table.shape, lambda b: (0, 0)),
            row,
            pl.BlockSpec(spots.shape, lambda b: (0, 0, 0)),
            anywhere,
        ],
        out_specs=[anywhere] * 3,
        out_shape=[
            jax.ShapeDtypeStruct((slab_total, tiles, each, tile), jnp.bfloat16),
            jax.ShapeDtypeStruct((slab_total,) + spots.shape, jnp.float32),
            jax.ShapeDtypeStruct((slab_total,) + maps.shape[2:], jnp.bfloat16),
        ],
        scratch_shapes=[
            pltpu.VMEM((tile, 2 * coils * LANES), jnp.bfloat16),
            pltpu.VMEM((unroll, CLASSES, 8, LANES), jnp.float32),
            pltpu.VMEM((unroll, CLASSES, 8, LANES), jnp.float32),
            pltpu.VMEM((RUNS, count, tile // RUNS), jnp.bfloat16),
            pltpu.VMEM((tiles, slab_total, each, tile), jnp.bfloat16),
            pltpu.SemaphoreType.DMA((tiles, slab_total)),
            pltpu.SemaphoreType.DMA((tiles, slab_total)),
            pltpu.SemaphoreType.DMA((tiles,)),
            pltpu.SemaphoreType.DMA((slab_total,)),
            pltpu.SemaphoreType.DMA((slab_total,)),
            pltpu.SemaphoreType.DMA,
            pltpu.SemaphoreType.DMA(maps.shape[:2]),
            pltpu.SemaphoreType.DMA((slab_total,)),
            pltpu.SemaphoreType.DMA,
        ],
        compiler_params=pltpu.CompilerParams(collective_id=0, has_side_effects=True),
        name="grid_x",
    )(pos, samples, seg, x_at, table, spot, spots, maps)

    per = math.gcd(chunks, 4)
    steps = chunks // per
    by_chunk = spots[:, :, 0].reshape(slab_total, tiles, 2 * chunks, HALF)
    step_down = max(8 // each, 1)
    low = jnp.min(by_chunk, axis=(1, 3)).astype(jnp.int32) // step_down * step_down
    high = (jnp.max(by_chunk, axis=(1, 3)).astype(jnp.int32) - low) // SPAN + 1
    ytab, ztab = right_table(freq), left_table(depth)
    pairs = each // 2
    imaged = pl.pallas_call(
        functools.partial(add_kernel, 2 * per),
        grid_spec=pltpu.PrefetchScalarGridSpec(
            num_scalar_prefetch=2,
            grid=(slab_total * steps,),
            in_specs=[
                pl.BlockSpec(
                    (1, tiles, each, per * LANES), lambda i, a, b: (i // steps, 0, 0, i % steps)
                ),
                pl.BlockSpec(
                    (1, tiles, 2, per * LANES), lambda i, a, b: (i // steps, 0, 0, i % steps)
                ),
            ],
            out_specs=pl.BlockSpec((pairs, depth, 2 * freq), lambda i, a, b: (0, 0, 0)),
            scratch_shapes=[
                pltpu.VMEM((freq // LANES, (depth + SPAN) * each, LANES), jnp.float32)
            ],
        ),
        out_shape=jax.ShapeDtypeStruct((pairs, depth, 2 * freq), jnp.bfloat16),
        name="add_yz",
    )(low.reshape(-1), high.reshape(-1), sent, spots)

    shares = x_own // x_here
    memory = pl.BlockSpec(memory_space=pltpu.VMEM)
    return pl.pallas_call(
        image_kernel,
        in_specs=[memory] * 4,
        out_specs=memory,
        out_shape=jax.ShapeDtypeStruct((planes, x_own, 2 * freq), jnp.float32),
        scratch_shapes=[
            pltpu.VMEM((x_here, slab_total, planes, 2 * freq), jnp.bfloat16),
            pltpu.VMEM((x_here, slab_total, planes, 2 * freq), jnp.bfloat16),
            pltpu.VMEM((coil_total, shares, x_here, planes, 2 * freq), jnp.bfloat16),
            pltpu.SemaphoreType.DMA((x_here, slab_total)),
            pltpu.SemaphoreType.DMA((x_here, slab_total)),
            pltpu.SemaphoreType.DMA((coil_total, shares, x_here)),
            pltpu.SemaphoreType.DMA((coil_total, shares, x_here)),
        ],
        compiler_params=pltpu.CompilerParams(collective_id=1, has_side_effects=True),
        name="image_sum",
    )(imaged, maps, ytab, ztab)


def solution(mesh):
    return jax.shard_map(
        per_device,
        mesh=mesh,
        in_specs=(
            P("coil", "slab", None),
            P("slab", None),
            P("slab"),
            P("slab"),
            P("slab", None),
            P(None, "slab", "coil", None),
        ),
        out_specs=P("slab", "coil", None),
        check_vma=False,
    )
```

```python
import functools
import math

import jax
import jax.numpy as jnp
import numpy as np
from jax import lax
from jax.experimental import pallas as pl
from jax.experimental.pallas import tpu as pltpu
from jax.sharding import PartitionSpec as P

KX = 256
CELLS = 64
CLASSES = 8
LANES = 128
HALF = LANES // 2
RUNS = 4
STRETCH = HALF // RUNS
SPAN = 40
PER = 8
NT = (((1,), (1,)), ((), ()))
MESH = pl.DeviceIdType.MESH


def ints(count):
    return jnp.arange(count, dtype=jnp.int32)


def twiddle(first, second, length):
    phase = (first * second % length).astype(np.float32) * np.float32(2.0 * math.pi / length)
    scale = np.float32(1.0 / math.sqrt(length))
    return np.cos(phase) * scale, np.sin(phase) * scale


def across_table(coils, rows_out, x_here):
    x0 = (KX - rows_out) // 2
    cosine, sine = twiddle(x0 + np.arange(rows_out)[:, None], np.arange(CELLS)[None, :], KX)
    upper = np.stack([cosine, -sine], axis=1)
    lower = np.stack([sine, cosine], axis=1)
    eye = np.eye(coils, dtype=np.float32)
    tables = []
    for one in (np.stack([upper, lower], axis=1), np.stack([-lower, upper], axis=1)):
        one = one.reshape(rows_out // x_here, 1, x_here, 2, 1, 2, CELLS)
        one = one * eye[None, :, None, None, :, None, None]
        tables.append(one.reshape(2 * coils * rows_out, 2 * coils * CELLS))
    return np.concatenate(tables, axis=0)


def right_table(length):
    cosine, sine = twiddle(np.arange(length)[:, None], np.arange(length)[None, :], length)
    upper = np.concatenate([cosine, sine], axis=1)
    lower = np.concatenate([-sine, cosine], axis=1)
    return jnp.asarray(np.concatenate([upper, lower], axis=0).astype(jnp.bfloat16))


def left_table(length):
    cosine, sine = twiddle(np.arange(length)[:, None], np.arange(length)[None, :], length)
    upper = np.concatenate([cosine, -sine], axis=1)
    lower = np.concatenate([sine, cosine], axis=1)
    return jnp.asarray(np.concatenate([upper, lower], axis=0).astype(jnp.bfloat16))


def spread_table(table, values):
    at = np.arange(2 * CELLS) % CELLS
    cell = CLASSES * (at % CLASSES) + at // CLASSES
    table = table.reshape(table.shape[0], values, CELLS)[:, :, cell]
    return jnp.asarray(table.reshape(table.shape[0], values * 2 * CELLS).astype(jnp.bfloat16))


def hot_rows(spots, depth):
    level = lax.broadcasted_iota(jnp.int32, (16, spots.shape[1]), 0).astype(jnp.float32)
    spots = jnp.broadcast_to(spots, (16, spots.shape[1])).astype(jnp.bfloat16)
    one, none = jnp.bfloat16(1), jnp.bfloat16(0)
    return jnp.concatenate(
        [
            jnp.where((level + at).astype(jnp.bfloat16) == spots, one, none)
            for at in range(0, depth, 16)
        ],
        axis=0,
    )


def permute(values, spots):
    depth = spots.shape[1]
    level = lax.broadcasted_iota(jnp.int32, (depth, depth), 0).astype(jnp.float32)
    hot = jnp.where(level == spots, 1.0, 0.0).astype(jnp.bfloat16)
    return lax.dot_general(values, hot, NT, preferred_element_type=jnp.float32)


def regroup(runs):
    rows, length = runs[0].shape
    place = lax.broadcasted_iota(jnp.int32, (rows, LANES), 1) % HALF // STRETCH
    for at in range(length // (2 * STRETCH)):
        cut = slice(at // RUNS * LANES, at // RUNS * LANES + LANES)
        out = runs[0][:, cut]
        for run in range(1, RUNS):
            out = jnp.where(place == (at + run) % RUNS, runs[run][:, cut], out)
        yield at, out


def order_kernel(planes, freq, kz_ref, ky_ref, spot_ref, sorted_ref):
    tile = kz_ref.shape[1]
    length = tile // RUNS
    pieces = length // LANES
    runs = []
    for run in range(RUNS):
        cut = slice(run * length, (run + 1) * length)
        kz, ky = kz_ref[:, cut], ky_ref[:, cut]
        lane = lax.broadcasted_iota(jnp.int32, (1, length), 1).astype(jnp.float32)
        key = kz * float(length) + lane
        rank = jnp.zeros((1, length), jnp.float32)
        for piece in range(pieces):
            part = key[:, piece * LANES : (piece + 1) * LANES]
            part = jnp.broadcast_to(part, (LANES, LANES)).T
            part = jnp.concatenate([part] * pieces, axis=1)
            rank = rank + jnp.sum(jnp.where(part < key, 1.0, 0.0), axis=0, keepdims=True)
        rank = rank.astype(jnp.int32)
        seat = rank // (2 * STRETCH)
        spot = seat // RUNS * LANES + rank // STRETCH % 2 * HALF
        spot = spot + (seat + run) % RUNS * STRETCH + rank % STRETCH
        spot = spot.astype(jnp.float32)
        spot_ref[:, cut] = spot
        both = jnp.concatenate([kz, ky, jnp.zeros((14, length), jnp.float32)], axis=0)
        runs.append(permute(both.astype(jnp.bfloat16), spot))
    for at, out in regroup(runs):
        sorted_ref[0, :, at * LANES : (at + 1) * LANES] = out[:2]


def grid_kernel(
    coils, unroll, pos_ref, val_ref, seg_ref, x_ref, tab_ref, spot_ref, spots_ref, map_ref,
    lines_ref, every_ref, maps_ref,
    cells, near, bump, placed, ready, line_out, line_in, line_own,
    spots_out, spots_in, spots_own, map_out, map_in, map_own,
):
    turn_at = pl.program_id(0)
    tiles, slabs, each, tile = ready.shape
    rows = slabs * each
    deals, shares = map_ref.shape[0], map_ref.shape[1]
    slab, coil = lax.axis_index("slab"), lax.axis_index("coil")
    barrier = pltpu.get_barrier_semaphore()
    here = slab // shares == coil

    def line_copy(at, hop):
        peer = lax.rem(slab + hop, slabs)
        return pltpu.make_async_remote_copy(
            ready.at[at, peer], lines_ref.at[slab, at], line_out.at[at, hop], line_in.at[at, hop],
            device_id={"slab": peer}, device_id_type=MESH,
        )

    def line_keep(at):
        return pltpu.make_async_copy(
            ready.at[at, slab], lines_ref.at[slab, at], line_own.at[at]
        )

    def spots_copy(hop):
        peer = lax.rem(slab + hop, slabs)
        return pltpu.make_async_remote_copy(
            spots_ref, every_ref.at[slab], spots_out.at[hop], spots_in.at[hop],
            device_id={"slab": peer}, device_id_type=MESH,
        )

    def spots_keep():
        return pltpu.make_async_copy(spots_ref, every_ref.at[slab], spots_own)

    def map_copy(deal, share):
        return pltpu.make_async_remote_copy(
            map_ref.at[deal, share], maps_ref.at[slab],
            map_out.at[deal, share], map_in.at[slab],
            device_id={"slab": coil * shares + share, "coil": deal}, device_id_type=MESH,
        )

    def map_take(source):
        return pltpu.make_async_remote_copy(
            map_ref.at[0, 0], maps_ref.at[source], map_out.at[0, 0], map_in.at[source],
            device_id={"slab": slab, "coil": coil}, device_id_type=MESH,
        )

    def map_keep():
        return pltpu.make_async_copy(
            map_ref.at[coil, lax.rem(slab, shares)], maps_ref.at[slab], map_own
        )

    def is_me(deal, share):
        return jnp.logical_and(coil * shares + share == slab, coil == deal)

    @pl.when(turn_at == 0)
    def _():
        for hop in range(1, slabs):
            pl.semaphore_signal(
                barrier, 1, device_id={"slab": lax.rem(slab + hop, slabs)}, device_id_type=MESH
            )
        for source in range(slabs):
            @pl.when(jnp.logical_not(jnp.logical_and(here, source == slab)))
            def _():
                pl.semaphore_signal(
                    barrier, 1, device_id={"slab": source, "coil": slab // shares},
                    device_id_type=MESH,
                )
    length = tile // RUNS
    block = lax.broadcasted_iota(jnp.int32, (16, LANES), 0)
    upper = lax.broadcasted_iota(jnp.int32, (16, LANES), 1) >= CELLS
    odd = block % 2 == 1
    own = [block % 4 // 2 == half for half in range(2)]
    mine = block // 4 % 2 == upper.astype(jnp.int32)
    level = lax.broadcasted_iota(jnp.int32, (CLASSES, LANES), 0).astype(jnp.float32)

    def step(g, slot):
        at = pl.ds(pl.multiple_of(g * 16, 16), 16)
        left = []
        for c in range(coils):
            straight = val_ref[c, at, :].astype(jnp.float32)
            turned = pltpu.roll(straight, CELLS, 1)
            for low, high in ((straight, turned), (turned, straight)):
                placed_here = jnp.where(
                    odd, jnp.where(upper, high, 0.0), jnp.where(upper, 0.0, low)
                )
                halves = [jnp.where(own[half], placed_here, 0.0) for half in range(2)]
                left.append(jnp.concatenate(halves, axis=1).astype(jnp.bfloat16))
        place = pos_ref[pl.ds(pl.multiple_of(g * 8, 8), 8), :].astype(jnp.float32) * 0.125
        for r in range(CLASSES):
            offset = place - ((r + 0.5) * 0.125 - 0.5)
            seat = jnp.floor(offset)
            offset = (offset - seat) * 3.2 - 1.6
            rise = jnp.maximum(1.0 - offset * offset, 0.0)
            near[slot, r] = seat
            bump[slot, r] = rise * rise
        right = []
        for quad in range(4):
            halves = []
            for half in range(2):
                row = pl.ds(2 * quad + half, 1)
                parts = []
                for r in range(CLASSES):
                    seat = jnp.broadcast_to(near[slot, r, row, :], level.shape)
                    high = jnp.broadcast_to(bump[slot, r, row, :], level.shape)
                    parts.append(jnp.where(level == seat, high, 0.0))
                halves.append(jnp.concatenate(parts, axis=0).astype(jnp.bfloat16))
            right.append(jnp.concatenate(halves, axis=1))
        done = lax.dot_general(
            jnp.concatenate(left, axis=0),
            jnp.concatenate(right, axis=0),
            NT,
            preferred_element_type=jnp.float32,
        )
        for v in range(2 * coils):
            first = done[16 * v : 16 * v + 8, :LANES]
            second = done[16 * v + 8 : 16 * v + 16, LANES:]
            both = jnp.where(mine, jnp.concatenate([first, second], axis=0), 0.0)
            cells[at, LANES * v : LANES * (v + 1)] = both.astype(jnp.bfloat16)

    @pl.loop(0, tile // (16 * unroll))
    def _(outer):
        for slot in range(unroll):
            step(outer * unroll + slot, slot)

    for run in range(RUNS):
        cut = slice(run * length, (run + 1) * length)
        moved = lax.dot_general(
            tab_ref[...], cells[cut, :], NT, preferred_element_type=jnp.float32
        )
        turn = (x_ref[...] * seg_ref[:, cut]) & 3
        turned = jnp.where((turn & 1) == 0, moved[:rows], moved[rows:])
        turned = jnp.where(turn >= 2, -turned, turned).astype(jnp.bfloat16)
        placed[run] = permute(turned, spot_ref[:, cut]).astype(jnp.bfloat16)
    for at, out in regroup([placed.at[run] for run in range(RUNS)]):
        for owner in range(slabs):
            ready[turn_at, owner, :, at * LANES : (at + 1) * LANES] = out[
                owner * each : (owner + 1) * each
            ]

    @pl.when(turn_at == 0)
    def _():
        pl.semaphore_wait(barrier, slabs - 1 + deals * shares - here.astype(jnp.int32))
        spots_keep().start()
        for hop in range(1, slabs):
            spots_copy(hop).start()
        for deal in range(deals):
            for share in range(shares):
                @pl.when(jnp.logical_not(is_me(deal, share)))
                def _():
                    map_copy(deal, share).start()

        @pl.when(here)
        def _():
            map_keep().start()

    for hop in range(1, slabs):
        line_copy(turn_at, hop).start()
    line_keep(turn_at).start()

    @pl.when(turn_at == tiles - 1)
    def _():
        spots_keep().wait()
        for hop in range(1, slabs):
            spots_copy(hop).wait()
        for deal in range(deals):
            for share in range(shares):
                @pl.when(jnp.logical_not(is_me(deal, share)))
                def _():
                    map_copy(deal, share).wait_send()
        for source in range(slabs):
            @pl.when(jnp.logical_not(jnp.logical_and(here, source == slab)))
            def _():
                map_take(source).wait_recv()

        @pl.when(here)
        def _():
            map_keep().wait()

        for at in range(tiles):
            line_keep(at).wait()
            for hop in range(1, slabs):
                line_copy(at, hop).wait()


def add_kernel(
    per, lo_ref, more_ref, vals_ref, spot_ref, out_ref, total
):
    step = pl.program_id(0)
    chunks = vals_ref.shape[3] // HALF
    tiles, rows = vals_ref.shape[1], vals_ref.shape[2]
    pairs, depth, freq = out_ref.shape[0], out_ref.shape[1], out_ref.shape[2] // 2
    deep = 16 // rows
    width = tiles * HALF
    inner = (lax.broadcasted_iota(jnp.int32, (16, width), 0) // rows).astype(jnp.float32)

    @pl.when(step == 0)
    def _():
        total[...] = jnp.zeros_like(total)

    def pick(outer, part, read):
        start = (outer * per + part // 2 * 2) * HALF
        cut = pl.ds(pl.multiple_of(start, LANES), LANES)
        out = []
        for t in range(0, tiles, 2):
            first, second = read(t, cut), read(t + 1, cut)
            low = lax.broadcasted_iota(jnp.int32, first.shape, 1) < HALF
            if part % 2 == 0:
                second = pltpu.roll(second, HALF, 1)
            else:
                first = pltpu.roll(first, HALF, 1)
            out.append(jnp.where(low, first, second))
        return jnp.concatenate(out, axis=1)

    def add(outer, part, start):
        vals = pick(outer, part, lambda t, cut: vals_ref[0, t, :, cut].astype(jnp.float32))
        vals = jnp.concatenate([vals] * deep, axis=0).astype(jnp.bfloat16)
        both = pick(outer, part, lambda t, cut: spot_ref[0, t, :, cut])
        base = jnp.full((16, width), start, jnp.int32).astype(jnp.float32)
        plane = jnp.broadcast_to(both[0:1], (16, width)) - base - inner
        plane = plane.astype(jnp.bfloat16)
        left = [
            jnp.where(plane == jnp.bfloat16(at), vals, jnp.bfloat16(0))
            for at in range(0, SPAN, deep)
        ]
        moved = lax.dot_general(
            jnp.concatenate(left, axis=0),
            hot_rows(both[1:2], freq),
            NT,
            preferred_element_type=jnp.float32,
        )
        at = pl.ds(pl.multiple_of(start * rows, 8), SPAN * rows)
        for half in range(freq // LANES):
            total[half, at, :] += moved[:, half * LANES : (half + 1) * LANES]

    @pl.loop(0, chunks // per)
    def _(outer):
        spot = step * chunks + outer * per
        for part in range(per):
            add(outer, part, lo_ref[spot + part])

        for part in range(per):
            first = lo_ref[spot + part]

            def again(at, carry):
                add(outer, part, first + at * SPAN)
                return carry

            lax.fori_loop(1, more_ref[spot + part], again, 0)

    @pl.when(step == pl.num_programs(0) - 1)
    def _():
        for pair in range(pairs):
            for part in range(2):
                for half in range(freq // LANES):
                    start = part * freq + half * LANES
                    found = total[half, pl.ds(2 * pair + part, depth, stride=rows), :]
                    out_ref[pair, :, start : start + LANES] = found.astype(jnp.bfloat16)


def image_kernel(
    rows_ref, map_ref, ytab_ref, ztab_ref, out_ref, ready, near, far,
    near_out, near_in, far_out, far_in,
):
    wide, slabs, planes, _ = ready.shape
    coils = rows_ref.shape[0] // wide
    deals, shares = far.shape[0], far.shape[1]
    depth, freq = rows_ref.shape[1], rows_ref.shape[2] // 2
    slab, coil = lax.axis_index("slab"), lax.axis_index("coil")
    barrier = pltpu.get_barrier_semaphore()
    for hop in range(1, slabs):
        peer = {"slab": lax.rem(slab + hop, slabs)}
        pl.semaphore_signal(barrier, 1, device_id=peer, device_id_type=MESH)
    for hop in range(1, deals):
        peer = {"coil": lax.rem(coil + hop, deals)}
        pl.semaphore_signal(barrier, 1, device_id=peer, device_id_type=MESH)

    def near_copy(x, hop):
        peer = lax.rem(slab + hop, slabs)
        return pltpu.make_async_remote_copy(
            ready.at[x, peer], near.at[x, slab], near_out.at[x, hop], near_in.at[x, hop],
            device_id={"slab": peer}, device_id_type=MESH,
        )

    def far_copy(x, source, hop):
        share = lax.rem(source, shares)
        return pltpu.make_async_remote_copy(
            near.at[x, source], far.at[hop, share, x],
            far_out.at[hop, share, x], far_in.at[hop, share, x],
            device_id={"coil": lax.rem(coil + hop, deals)}, device_id_type=MESH,
        )

    for x in range(wide):
        real = imag = 0.0
        for c in range(coils):
            planar = jnp.dot(
                rows_ref[c * wide + x], ytab_ref[...], preferred_element_type=jnp.float32
            ).astype(jnp.bfloat16)
            planar = jnp.concatenate([planar[:, :freq], planar[:, freq:]], axis=0)
            image = jnp.dot(ztab_ref[...], planar, preferred_element_type=jnp.float32)
            image = image.astype(jnp.bfloat16).astype(jnp.float32)
            img_re, img_im = image[:depth], image[depth:]
            maps = map_ref[:, c, x].reshape(depth, 2 * freq).astype(jnp.float32)
            map_re, map_im = maps[:, :freq], maps[:, freq:]
            real = real + (map_re * img_re + map_im * img_im)
            imag = imag + (map_re * img_im - map_im * img_re)
        both = jnp.concatenate([real, imag], axis=1).astype(jnp.bfloat16)
        ready[x] = both.reshape(slabs, planes, 2 * freq)
        near[x, pl.ds(slab, 1)] = ready[x, pl.ds(slab, 1)]
        if x == 0:
            pl.semaphore_wait(barrier, slabs - 1 + deals - 1)
        for hop in range(1, slabs):
            near_copy(x, hop).start()

    for x in range(wide):
        for hop in range(slabs):
            source = lax.rem(slab + slabs - hop, slabs)
            if hop > 0:
                near_copy(x, hop).wait_recv()
            leap = lax.rem(source // shares + deals - coil, deals)

            @pl.when(leap > 0)
            def _():
                far_copy(x, source, leap).start()

    for x in range(wide):
        for share in range(shares):
            value = near[x, coil * shares + share].astype(jnp.float32)
            for hop in range(1, deals):
                far_copy(x, share, hop).wait_recv()
                value = value + far[hop, share, x].astype(jnp.float32)
            out_ref[:, share * wide + x, :] = value
    for x in range(wide):
        for hop in range(1, slabs):
            near_copy(x, hop).wait_send()
        for share in range(shares):
            for hop in range(1, deals):
                far_copy(x, share, hop).wait_send()


def per_device(samples, sample_pos, block_count, grid_block, block_slab, sensitivity):
    slab_total = lax.axis_size("slab")
    coil_total = lax.axis_size("coil")
    coils = samples.shape[0]
    blocks = samples.shape[1]
    planes = sensitivity.shape[1]
    rows_out = sensitivity.shape[2] * coil_total
    depth = planes * slab_total
    freq = sensitivity.shape[3] // 2
    x_here = rows_out // slab_total
    segments = KX // CELLS

    live = ints(CELLS)[None, :] < block_count[:, None]
    pos = jnp.where(live, sample_pos, 9984.0).reshape(blocks // 2, 2 * CELLS)
    seg = (grid_block % segments)[None, :]
    kz = block_slab[:, 0] * planes + grid_block // (segments * freq)
    ky = grid_block // segments % freq
    kz, ky = kz.astype(jnp.float32)[None, :], ky.astype(jnp.float32)[None, :]

    tile = math.gcd(blocks, 2048)
    tiles = blocks // tile
    chunks = tile // LANES
    unroll = math.gcd(tile // 16, 16)
    count = 2 * coils * rows_out
    each = 2 * coils * x_here

    row = pl.BlockSpec((1, tile), lambda b: (0, b))
    spot, spots = pl.pallas_call(
        functools.partial(order_kernel, planes, freq),
        grid=(tiles,),
        in_specs=[row, row],
        out_specs=[row, pl.BlockSpec((1, 2, tile), lambda b: (b, 0, 0))],
        out_shape=[
            jax.ShapeDtypeStruct((1, blocks), jnp.float32),
            jax.ShapeDtypeStruct((tiles, 2, tile), jnp.float32),
        ],
        name="order_kz",
    )(kz, ky)

    table = spread_table(across_table(coils, rows_out, x_here), 2 * coils)
    x_at = (ints(count) // (2 * coils * x_here)) * x_here + ints(count) // 2 % x_here
    x_at = jnp.broadcast_to((x_at + (KX - rows_out) // 2)[:, None], (count, tile // RUNS))
    x_own = sensitivity.shape[2]
    maps = sensitivity.reshape(
        coil_total, coils, planes, x_own // x_here, x_here, 2 * freq
    ).transpose(0, 3, 1, 4, 2, 5)
    anywhere = pl.BlockSpec(memory_space=pl.ANY)
    sent, spots, maps = pl.pallas_call(
        functools.partial(grid_kernel, coils, unroll),
        grid=(tiles,),
        in_specs=[
            pl.BlockSpec((tile // 2, LANES), lambda b: (b, 0)),
            pl.BlockSpec((coils, tile, LANES), lambda b: (0, b, 0)),
            row,
            pl.BlockSpec(x_at.shape, lambda b: (0, 0)),
            pl.BlockSpec(table.shape, lambda b: (0, 0)),
            row,
            pl.BlockSpec(spots.shape, lambda b: (0, 0, 0)),
            anywhere,
        ],
        out_specs=[anywhere] * 3,
        out_shape=[
            jax.ShapeDtypeStruct((slab_total, tiles, each, tile), jnp.bfloat16),
            jax.ShapeDtypeStruct((slab_total,) + spots.shape, jnp.float32),
            jax.ShapeDtypeStruct((slab_total,) + maps.shape[2:], jnp.bfloat16),
        ],
        scratch_shapes=[
            pltpu.VMEM((tile, 2 * coils * LANES), jnp.bfloat16),
            pltpu.VMEM((unroll, CLASSES, 8, LANES), jnp.float32),
            pltpu.VMEM((unroll, CLASSES, 8, LANES), jnp.float32),
            pltpu.VMEM((RUNS, count, tile // RUNS), jnp.bfloat16),
            pltpu.VMEM((tiles, slab_total, each, tile), jnp.bfloat16),
            pltpu.SemaphoreType.DMA((tiles, slab_total)),
            pltpu.SemaphoreType.DMA((tiles, slab_total)),
            pltpu.SemaphoreType.DMA((tiles,)),
            pltpu.SemaphoreType.DMA((slab_total,)),
            pltpu.SemaphoreType.DMA((slab_total,)),
            pltpu.SemaphoreType.DMA,
            pltpu.SemaphoreType.DMA(maps.shape[:2]),
            pltpu.SemaphoreType.DMA((slab_total,)),
            pltpu.SemaphoreType.DMA,
        ],
        compiler_params=pltpu.CompilerParams(collective_id=0, has_side_effects=True),
        name="grid_x",
    )(pos, samples, seg, x_at, table, spot, spots, maps)

    per = math.gcd(2 * chunks, PER)
    by_chunk = spots[:, :, 0].reshape(slab_total, tiles, 2 * chunks, HALF)
    step_down = max(8 // each, 1)
    low = jnp.min(by_chunk, axis=(1, 3)).astype(jnp.int32) // step_down * step_down
    high = (jnp.max(by_chunk, axis=(1, 3)).astype(jnp.int32) - low) // SPAN + 1
    ytab, ztab = right_table(freq), left_table(depth)
    pairs = each // 2
    imaged = pl.pallas_call(
        functools.partial(add_kernel, per),
        grid_spec=pltpu.PrefetchScalarGridSpec(
            num_scalar_prefetch=2,
            grid=(slab_total,),
            in_specs=[
                pl.BlockSpec((1, tiles, each, tile), lambda i, a, b: (i, 0, 0, 0)),
                pl.BlockSpec((1, tiles, 2, tile), lambda i, a, b: (i, 0, 0, 0)),
            ],
            out_specs=pl.BlockSpec((pairs, depth, 2 * freq), lambda i, a, b: (0, 0, 0)),
            scratch_shapes=[
                pltpu.VMEM((freq // LANES, (depth + SPAN) * each, LANES), jnp.float32)
            ],
        ),
        out_shape=jax.ShapeDtypeStruct((pairs, depth, 2 * freq), jnp.bfloat16),
        name="add_yz",
    )(low.reshape(-1), high.reshape(-1), sent, spots)

    shares = x_own // x_here
    memory = pl.BlockSpec(memory_space=pltpu.VMEM)
    return pl.pallas_call(
        image_kernel,
        in_specs=[memory] * 4,
        out_specs=memory,
        out_shape=jax.ShapeDtypeStruct((planes, x_own, 2 * freq), jnp.float32),
        scratch_shapes=[
            pltpu.VMEM((x_here, slab_total, planes, 2 * freq), jnp.bfloat16),
            pltpu.VMEM((x_here, slab_total, planes, 2 * freq), jnp.bfloat16),
            pltpu.VMEM((coil_total, shares, x_here, planes, 2 * freq), jnp.bfloat16),
            pltpu.SemaphoreType.DMA((x_here, slab_total)),
            pltpu.SemaphoreType.DMA((x_here, slab_total)),
            pltpu.SemaphoreType.DMA((coil_total, shares, x_here)),
            pltpu.SemaphoreType.DMA((coil_total, shares, x_here)),
        ],
        compiler_params=pltpu.CompilerParams(collective_id=1, has_side_effects=True),
        name="image_sum",
    )(imaged, maps, ytab, ztab)


def solution(mesh):
    return jax.shard_map(
        per_device,
        mesh=mesh,
        in_specs=(
            P("coil", "slab", None),
            P("slab", None),
            P("slab"),
            P("slab"),
            P("slab", None),
            P(None, "slab", "coil", None),
        ),
        out_specs=P("slab", "coil", None),
        check_vma=False,
    )
```

```python
import functools
import math

import jax
import jax.numpy as jnp
import numpy as np
from jax import lax
from jax.experimental import pallas as pl
from jax.experimental.pallas import tpu as pltpu
from jax.sharding import PartitionSpec as P

KX = 256
CELLS = 64
CLASSES = 8
LANES = 128
RUNS = 4
STRETCH = LANES // RUNS
SPAN = 56
PER = 8
DEAD = 9984.0
NT = (((1,), (1,)), ((), ()))
MESH = pl.DeviceIdType.MESH


def twiddle(first, second, length):
    phase = (first * second % length).astype(np.float32) * np.float32(2.0 * math.pi / length)
    scale = np.float32(1.0 / math.sqrt(length))
    return np.cos(phase) * scale, np.sin(phase) * scale


def across_table(coils, rows_out, x_here):
    x0 = (KX - rows_out) // 2
    cosine, sine = twiddle(x0 + np.arange(rows_out)[:, None], np.arange(CELLS)[None, :], KX)
    upper = np.stack([cosine, -sine], axis=1)
    lower = np.stack([sine, cosine], axis=1)
    eye = np.eye(coils, dtype=np.float32)
    tables = []
    for one in (np.stack([upper, lower], axis=1), np.stack([-lower, upper], axis=1)):
        one = one.reshape(rows_out // x_here, 1, x_here, 2, 1, 2, CELLS)
        one = one * eye[None, :, None, None, :, None, None]
        tables.append(one.reshape(2 * coils * rows_out, 2 * coils * CELLS))
    return np.concatenate(tables, axis=0)


def right_table(length):
    cosine, sine = twiddle(np.arange(length)[:, None], np.arange(length)[None, :], length)
    upper = np.concatenate([cosine, sine], axis=1)
    lower = np.concatenate([-sine, cosine], axis=1)
    return jnp.asarray(np.concatenate([upper, lower], axis=0).astype(jnp.bfloat16))


def left_table(length):
    cosine, sine = twiddle(np.arange(length)[:, None], np.arange(length)[None, :], length)
    upper = np.concatenate([cosine, -sine], axis=1)
    lower = np.concatenate([sine, cosine], axis=1)
    return jnp.asarray(np.concatenate([upper, lower], axis=0).astype(jnp.bfloat16))


def spread_table(table, values):
    at = np.arange(2 * CELLS) % CELLS
    cell = CLASSES * (at % CLASSES) + at // CLASSES
    table = table.reshape(table.shape[0], values, CELLS)[:, :, cell]
    return jnp.asarray(table.reshape(table.shape[0], values * 2 * CELLS).astype(jnp.bfloat16))


def hot_rows(spots, depth):
    level = lax.broadcasted_iota(jnp.int32, (16, spots.shape[1]), 0).astype(jnp.float32)
    spots = jnp.broadcast_to(spots, (16, spots.shape[1])).astype(jnp.bfloat16)
    one, none = jnp.bfloat16(1), jnp.bfloat16(0)
    return jnp.concatenate(
        [
            jnp.where((level + at).astype(jnp.bfloat16) == spots, one, none)
            for at in range(0, depth, 16)
        ],
        axis=0,
    )


def permute(values, spots):
    depth = spots.shape[1]
    level = lax.broadcasted_iota(jnp.int32, (depth, depth), 0).astype(jnp.float32)
    hot = jnp.where(level == spots, 1.0, 0.0).astype(jnp.bfloat16)
    return lax.dot_general(values, hot, NT, preferred_element_type=jnp.float32)


def regroup(runs):
    rows, length = runs[0].shape
    place = lax.broadcasted_iota(jnp.int32, (rows, LANES), 1) // STRETCH
    for at in range(length // STRETCH):
        cut = slice(at // RUNS * LANES, at // RUNS * LANES + LANES)
        out = runs[0][:, cut]
        for run in range(1, RUNS):
            out = jnp.where(place == (at + run) % RUNS, runs[run][:, cut], out)
        yield at, out


def order(kz, run):
    length = kz.shape[1]
    pieces = length // LANES
    lane = lax.broadcasted_iota(jnp.int32, (1, length), 1).astype(jnp.float32)
    key = kz * float(length) + lane
    rank = jnp.zeros((1, length), jnp.float32)
    for piece in range(pieces):
        part = key[:, piece * LANES : (piece + 1) * LANES]
        part = jnp.broadcast_to(part, (LANES, LANES)).T
        part = jnp.concatenate([part] * pieces, axis=1)
        rank = rank + jnp.sum(jnp.where(part < key, 1.0, 0.0), axis=0, keepdims=True)
    rank = rank.astype(jnp.int32)
    seat = rank // STRETCH
    spot = seat // RUNS * LANES + (seat + run) % RUNS * STRETCH + rank % STRETCH
    return spot.astype(jnp.float32)


def grid_kernel(
    coils, unroll, planes, freq, pos_ref, count_ref, block_ref, slab_ref, val_ref, tab_ref, map_ref,
    lines_ref, every_ref, limits_ref, maps_ref,
    flat, cells, near, bump, placed, ready, spots, least, most, limits,
    line_out, line_in, line_own, spots_out, spots_in, spots_own,
    limit_out, limit_in, limit_own, map_out, map_in, map_own,
):
    turn_at = pl.program_id(0)
    tiles, slabs, each, tile = ready.shape
    rows = slabs * each
    deals, shares = map_ref.shape[0], map_ref.shape[1]
    slab, coil = lax.axis_index("slab"), lax.axis_index("coil")
    barrier = pltpu.get_barrier_semaphore()
    here = slab // shares == coil

    def line_copy(at, hop):
        peer = lax.rem(slab + hop, slabs)
        return pltpu.make_async_remote_copy(
            ready.at[at, peer], lines_ref.at[slab, at], line_out.at[at, hop], line_in.at[at, hop],
            device_id={"slab": peer}, device_id_type=MESH,
        )

    def line_keep(at):
        return pltpu.make_async_copy(
            ready.at[at, slab], lines_ref.at[slab, at], line_own.at[at]
        )

    def spots_copy(at, hop):
        peer = lax.rem(slab + hop, slabs)
        return pltpu.make_async_remote_copy(
            spots.at[at], every_ref.at[slab, at], spots_out.at[at, hop], spots_in.at[at, hop],
            device_id={"slab": peer}, device_id_type=MESH,
        )

    def spots_keep(at):
        return pltpu.make_async_copy(spots.at[at], every_ref.at[slab, at], spots_own.at[at])

    def limit_copy(hop):
        peer = lax.rem(slab + hop, slabs)
        return pltpu.make_async_remote_copy(
            limits, limits_ref.at[slab], limit_out.at[hop], limit_in.at[hop],
            device_id={"slab": peer}, device_id_type=MESH,
        )

    def limit_keep():
        return pltpu.make_async_copy(limits, limits_ref.at[slab], limit_own)

    def map_copy(deal, share):
        return pltpu.make_async_remote_copy(
            map_ref.at[deal, share], maps_ref.at[slab],
            map_out.at[deal, share], map_in.at[slab],
            device_id={"slab": coil * shares + share, "coil": deal}, device_id_type=MESH,
        )

    def map_take(source):
        return pltpu.make_async_remote_copy(
            map_ref.at[0, 0], maps_ref.at[source], map_out.at[0, 0], map_in.at[source],
            device_id={"slab": slab, "coil": coil}, device_id_type=MESH,
        )

    def map_keep():
        return pltpu.make_async_copy(
            map_ref.at[coil, lax.rem(slab, shares)], maps_ref.at[slab], map_own
        )

    def is_me(deal, share):
        return jnp.logical_and(coil * shares + share == slab, coil == deal)

    @pl.when(turn_at == 0)
    def _():
        for hop in range(1, slabs):
            pl.semaphore_signal(
                barrier, 1, device_id={"slab": lax.rem(slab + hop, slabs)}, device_id_type=MESH
            )
        for source in range(slabs):
            @pl.when(jnp.logical_not(jnp.logical_and(here, source == slab)))
            def _():
                pl.semaphore_signal(
                    barrier, 1, device_id={"slab": source, "coil": slab // shares},
                    device_id_type=MESH,
                )
    length = tile // RUNS
    chunks = tile // LANES

    for piece in range(chunks):
        cut = slice(piece * LANES, (piece + 1) * LANES)
        live = lax.broadcasted_iota(jnp.int32, (CELLS, LANES), 0) < count_ref[:, cut]
        place = jnp.where(live, pos_ref[:, cut].astype(jnp.float32), DEAD)
        both = jnp.concatenate([place, pltpu.roll(place, LANES - 8, 1)], axis=0)
        flat[cut, :] = both.T

    segments = KX // CELLS
    kz = slab_ref[...] * planes + block_ref[...] // (segments * freq)
    ky = block_ref[...] // segments % freq
    seg = block_ref[...] % segments
    kz, ky = kz.astype(jnp.float32), ky.astype(jnp.float32)

    block = lax.broadcasted_iota(jnp.int32, (16, LANES), 0)
    upper = lax.broadcasted_iota(jnp.int32, (16, LANES), 1) >= CELLS
    odd = block >= 8
    own = [block % 2 == half for half in range(2)]
    head = block % 8 < 4
    mine = block % 4 // 2 == upper.astype(jnp.int32)
    level = lax.broadcasted_iota(jnp.int32, (CLASSES, LANES), 0).astype(jnp.float32)

    def step(g, slot):
        at = pl.ds(pl.multiple_of(g * 16, 16), 16)
        left = []
        for c in range(coils):
            straight = val_ref[c, at, :].astype(jnp.float32)
            turned = pltpu.roll(straight, CELLS, 1)
            for low, high in ((straight, turned), (turned, straight)):
                placed_here = jnp.where(
                    odd, jnp.where(upper, high, 0.0), jnp.where(upper, 0.0, low)
                )
                halves = [jnp.where(own[half], placed_here, 0.0) for half in range(2)]
                left.append(jnp.concatenate(halves, axis=1).astype(jnp.bfloat16))
        place = flat[pl.ds(pl.multiple_of(g * 16, 16), 8), :] * 0.125
        for r in range(CLASSES):
            offset = place - ((r + 0.5) * 0.125 - 0.5)
            seat = jnp.floor(offset)
            offset = (offset - seat) * 3.2 - 1.6
            rise = jnp.maximum(1.0 - offset * offset, 0.0)
            near[slot, r] = seat
            bump[slot, r] = rise * rise
        right = []
        for quad in range(4):
            halves = []
            for half in range(2):
                row = pl.ds(2 * quad + half, 1)
                parts = []
                for r in range(CLASSES):
                    seat = jnp.broadcast_to(near[slot, r, row, :], level.shape)
                    high = jnp.broadcast_to(bump[slot, r, row, :], level.shape)
                    parts.append(jnp.where(level == seat, high, 0.0))
                halves.append(jnp.concatenate(parts, axis=0).astype(jnp.bfloat16))
            right.append(jnp.concatenate(halves, axis=1))
        done = lax.dot_general(
            jnp.concatenate(left, axis=0),
            jnp.concatenate(right, axis=0),
            NT,
            preferred_element_type=jnp.float32,
        )
        for v in range(2 * coils):
            rows16 = slice(16 * v, 16 * v + 16)
            both = jnp.where(head, done[rows16, :LANES], done[rows16, LANES:])
            both = jnp.where(mine, both, 0.0)
            cells[at, LANES * v : LANES * (v + 1)] = both.astype(jnp.bfloat16)

    @pl.loop(0, tile // (16 * unroll))
    def _(outer):
        for slot in range(unroll):
            step(outer * unroll + slot, slot)

    wide = 2 * coils
    x_here = each // wide
    line = lax.broadcasted_iota(jnp.int32, (rows, LANES), 0)
    x_at = line // each * x_here + line // 2 % x_here + (KX - rows // wide) // 2
    x_at = jnp.concatenate([x_at] * (length // LANES), axis=1)
    pad = jnp.zeros((14, length), jnp.float32)
    for run in range(RUNS):
        cut = slice(run * length, (run + 1) * length)
        moved = lax.dot_general(
            tab_ref[...], cells[cut, :], NT, preferred_element_type=jnp.float32
        )
        turn = (x_at * seg[:, cut]) & 3
        turned = jnp.where((turn & 1) == 0, moved[:rows], moved[rows:])
        turned = jnp.where(turn >= 2, -turned, turned)
        turned = jnp.concatenate([turned, kz[:, cut], ky[:, cut], pad], axis=0)
        spot = order(kz[:, cut], run)
        placed[run] = permute(turned.astype(jnp.bfloat16), spot).astype(jnp.bfloat16)

    @pl.when(turn_at == 0)
    def _():
        least[...] = jnp.full_like(least, 1.0e4)
        most[...] = jnp.zeros_like(most)

    for at, out in regroup([placed.at[run] for run in range(RUNS)]):
        for owner in range(slabs):
            ready[turn_at, owner, :, at * LANES : (at + 1) * LANES] = out[
                owner * each : (owner + 1) * each
            ]
        found = out[rows : rows + 2].astype(jnp.float32)
        spots[turn_at, :, at * LANES : (at + 1) * LANES] = found
        least[at : at + 1] = jnp.minimum(least[at : at + 1], found[0:1])
        most[at : at + 1] = jnp.maximum(most[at : at + 1], found[0:1])

    @pl.when(turn_at == tiles - 1)
    def _():
        step_down = max(8 // each, 1)
        low = jnp.min(least[...].T, axis=0, keepdims=True).astype(jnp.int32)
        low = low // step_down * step_down
        high = jnp.max(most[...].T, axis=0, keepdims=True).astype(jnp.int32)
        high = (high - low) // SPAN + 1
        limits[0:1] = low
        limits[1:2] = high
        limits[2:] = jnp.zeros((6, LANES), jnp.int32)

    @pl.when(turn_at == 0)
    def _():
        pl.semaphore_wait(barrier, slabs - 1 + deals * shares - here.astype(jnp.int32))
        for deal in range(deals):
            for share in range(shares):
                @pl.when(jnp.logical_not(is_me(deal, share)))
                def _():
                    map_copy(deal, share).start()

        @pl.when(here)
        def _():
            map_keep().start()

    for hop in range(1, slabs):
        line_copy(turn_at, hop).start()
        spots_copy(turn_at, hop).start()
    line_keep(turn_at).start()
    spots_keep(turn_at).start()

    @pl.when(turn_at == tiles - 1)
    def _():
        for hop in range(1, slabs):
            limit_copy(hop).start()
        limit_keep().start()
        for deal in range(deals):
            for share in range(shares):
                @pl.when(jnp.logical_not(is_me(deal, share)))
                def _():
                    map_copy(deal, share).wait_send()
        for source in range(slabs):
            @pl.when(jnp.logical_not(jnp.logical_and(here, source == slab)))
            def _():
                map_take(source).wait_recv()

        @pl.when(here)
        def _():
            map_keep().wait()

        for at in range(tiles):
            line_keep(at).wait()
            spots_keep(at).wait()
            for hop in range(1, slabs):
                line_copy(at, hop).wait()
                spots_copy(at, hop).wait()
        limit_keep().wait()
        for hop in range(1, slabs):
            limit_copy(hop).wait()


def add_kernel(
    per, limit_ref, vals_ref, spot_ref, out_ref, total
):
    step = pl.program_id(0)
    chunks = vals_ref.shape[3] // LANES
    tiles, rows = vals_ref.shape[1], vals_ref.shape[2]
    pairs, depth, freq = out_ref.shape[0], out_ref.shape[1], out_ref.shape[2] // 2
    deep = 16 // rows
    width = tiles * LANES
    inner = (lax.broadcasted_iota(jnp.int32, (16, width), 0) // rows).astype(jnp.float32)

    @pl.when(step == 0)
    def _():
        total[...] = jnp.zeros_like(total)

    def pick(outer, part, read):
        cut = pl.ds(pl.multiple_of((outer * per + part) * LANES, LANES), LANES)
        return jnp.concatenate([read(t, cut) for t in range(tiles)], axis=1)

    def add(outer, part, start):
        vals = pick(outer, part, lambda t, cut: vals_ref[0, t, :, cut])
        vals = jnp.concatenate([vals] * deep, axis=0)
        both = pick(outer, part, lambda t, cut: spot_ref[0, t, :, cut])
        base = jnp.full((16, width), start, jnp.int32).astype(jnp.float32)
        plane = jnp.broadcast_to(both[0:1], (16, width)) - base - inner
        plane = plane.astype(jnp.bfloat16)
        left = [
            jnp.where(plane == jnp.bfloat16(at), vals, jnp.bfloat16(0))
            for at in range(0, SPAN, deep)
        ]
        moved = lax.dot_general(
            jnp.concatenate(left, axis=0),
            hot_rows(both[1:2], freq),
            NT,
            preferred_element_type=jnp.float32,
        )
        at = pl.ds(pl.multiple_of(start * rows, 8), SPAN * rows)
        for half in range(freq // LANES):
            total[half, at, :] += moved[:, half * LANES : (half + 1) * LANES]

    @pl.loop(0, chunks // per)
    def _(outer):
        for part in range(per):
            add(outer, part, limit_ref[step, 0, outer * per + part])

        for part in range(per):
            first = limit_ref[step, 0, outer * per + part]

            def again(at, carry):
                add(outer, part, first + at * SPAN)
                return carry

            lax.fori_loop(1, limit_ref[step, 1, outer * per + part], again, 0)

    @pl.when(step == pl.num_programs(0) - 1)
    def _():
        for pair in range(pairs):
            for part in range(2):
                for half in range(freq // LANES):
                    start = part * freq + half * LANES
                    found = total[half, pl.ds(2 * pair + part, depth, stride=rows), :]
                    out_ref[pair, :, start : start + LANES] = found.astype(jnp.bfloat16)


def image_kernel(
    rows_ref, map_ref, ytab_ref, ztab_ref, out_ref, ready, near, far,
    near_out, near_in, far_out, far_in,
):
    wide, slabs, planes, _ = ready.shape
    coils = rows_ref.shape[0] // wide
    deals, shares = far.shape[0], far.shape[1]
    depth, freq = rows_ref.shape[1], rows_ref.shape[2] // 2
    slab, coil = lax.axis_index("slab"), lax.axis_index("coil")
    barrier = pltpu.get_barrier_semaphore()
    for hop in range(1, slabs):
        peer = {"slab": lax.rem(slab + hop, slabs)}
        pl.semaphore_signal(barrier, 1, device_id=peer, device_id_type=MESH)
    for hop in range(1, deals):
        peer = {"coil": lax.rem(coil + hop, deals)}
        pl.semaphore_signal(barrier, 1, device_id=peer, device_id_type=MESH)

    def near_copy(x, hop):
        peer = lax.rem(slab + hop, slabs)
        return pltpu.make_async_remote_copy(
            ready.at[x, peer], near.at[x, slab], near_out.at[x, hop], near_in.at[x, hop],
            device_id={"slab": peer}, device_id_type=MESH,
        )

    def far_copy(x, source, hop):
        share = lax.rem(source, shares)
        return pltpu.make_async_remote_copy(
            near.at[x, source], far.at[hop, share, x],
            far_out.at[hop, share, x], far_in.at[hop, share, x],
            device_id={"coil": lax.rem(coil + hop, deals)}, device_id_type=MESH,
        )

    for x in range(wide):
        real = imag = 0.0
        for c in range(coils):
            planar = jnp.dot(
                rows_ref[c * wide + x], ytab_ref[...], preferred_element_type=jnp.float32
            ).astype(jnp.bfloat16)
            planar = jnp.concatenate([planar[:, :freq], planar[:, freq:]], axis=0)
            image = jnp.dot(ztab_ref[...], planar, preferred_element_type=jnp.float32)
            image = image.astype(jnp.bfloat16).astype(jnp.float32)
            img_re, img_im = image[:depth], image[depth:]
            maps = map_ref[:, c, x].reshape(depth, 2 * freq).astype(jnp.float32)
            map_re, map_im = maps[:, :freq], maps[:, freq:]
            real = real + (map_re * img_re + map_im * img_im)
            imag = imag + (map_re * img_im - map_im * img_re)
        both = jnp.concatenate([real, imag], axis=1).astype(jnp.bfloat16)
        ready[x] = both.reshape(slabs, planes, 2 * freq)
        near[x, pl.ds(slab, 1)] = ready[x, pl.ds(slab, 1)]
        if x == 0:
            pl.semaphore_wait(barrier, slabs - 1 + deals - 1)
        for hop in range(1, slabs):
            near_copy(x, hop).start()

    for x in range(wide):
        for hop in range(slabs):
            source = lax.rem(slab + slabs - hop, slabs)
            if hop > 0:
                near_copy(x, hop).wait_recv()
            leap = lax.rem(source // shares + deals - coil, deals)

            @pl.when(leap > 0)
            def _():
                far_copy(x, source, leap).start()

    for x in range(wide):
        for share in range(shares):
            value = near[x, coil * shares + share].astype(jnp.float32)
            for hop in range(1, deals):
                far_copy(x, share, hop).wait_recv()
                value = value + far[hop, share, x].astype(jnp.float32)
            out_ref[:, share * wide + x, :] = value
    for x in range(wide):
        for hop in range(1, slabs):
            near_copy(x, hop).wait_send()
        for share in range(shares):
            for hop in range(1, deals):
                far_copy(x, share, hop).wait_send()


def per_device(samples, sample_pos, block_count, grid_block, block_slab, sensitivity):
    slab_total = lax.axis_size("slab")
    coil_total = lax.axis_size("coil")
    coils = samples.shape[0]
    blocks = samples.shape[1]
    planes = sensitivity.shape[1]
    rows_out = sensitivity.shape[2] * coil_total
    depth = planes * slab_total
    freq = sensitivity.shape[3] // 2
    x_here = rows_out // slab_total
    tile = math.gcd(blocks, 2048)
    tiles = blocks // tile
    chunks = tile // LANES
    unroll = math.gcd(tile // 16, 16)
    count = 2 * coils * rows_out
    each = 2 * coils * x_here

    row = pl.BlockSpec((1, tile), lambda b: (0, b))
    table = spread_table(across_table(coils, rows_out, x_here), 2 * coils)
    x_own = sensitivity.shape[2]
    maps = sensitivity.reshape(
        coil_total, coils, planes, x_own // x_here, x_here, 2 * freq
    ).transpose(0, 3, 1, 4, 2, 5)
    anywhere = pl.BlockSpec(memory_space=pl.ANY)
    sent, spots, limits, maps = pl.pallas_call(
        functools.partial(grid_kernel, coils, unroll, planes, freq),
        grid=(tiles,),
        in_specs=[
            pl.BlockSpec((CELLS, tile), lambda b: (0, b)),
            row,
            row,
            row,
            pl.BlockSpec((coils, tile, LANES), lambda b: (0, b, 0)),
            pl.BlockSpec(table.shape, lambda b: (0, 0)),
            anywhere,
        ],
        out_specs=[anywhere] * 4,
        out_shape=[
            jax.ShapeDtypeStruct((slab_total, tiles, each, tile), jnp.bfloat16),
            jax.ShapeDtypeStruct((slab_total, tiles, 2, tile), jnp.float32),
            jax.ShapeDtypeStruct((slab_total, 8, LANES), jnp.int32),
            jax.ShapeDtypeStruct((slab_total,) + maps.shape[2:], jnp.bfloat16),
        ],
        scratch_shapes=[
            pltpu.VMEM((tile, LANES), jnp.float32),
            pltpu.VMEM((tile, 2 * coils * LANES), jnp.bfloat16),
            pltpu.VMEM((unroll, CLASSES, 8, LANES), jnp.float32),
            pltpu.VMEM((unroll, CLASSES, 8, LANES), jnp.float32),
            pltpu.VMEM((RUNS, count + 16, tile // RUNS), jnp.bfloat16),
            pltpu.VMEM((tiles, slab_total, each, tile), jnp.bfloat16),
            pltpu.VMEM((tiles, 2, tile), jnp.float32),
            pltpu.VMEM((LANES, LANES), jnp.float32),
            pltpu.VMEM((LANES, LANES), jnp.float32),
            pltpu.VMEM((8, LANES), jnp.int32),
            pltpu.SemaphoreType.DMA((tiles, slab_total)),
            pltpu.SemaphoreType.DMA((tiles, slab_total)),
            pltpu.SemaphoreType.DMA((tiles,)),
            pltpu.SemaphoreType.DMA((tiles, slab_total)),
            pltpu.SemaphoreType.DMA((tiles, slab_total)),
            pltpu.SemaphoreType.DMA((tiles,)),
            pltpu.SemaphoreType.DMA((slab_total,)),
            pltpu.SemaphoreType.DMA((slab_total,)),
            pltpu.SemaphoreType.DMA,
            pltpu.SemaphoreType.DMA(maps.shape[:2]),
            pltpu.SemaphoreType.DMA((slab_total,)),
            pltpu.SemaphoreType.DMA,
        ],
        compiler_params=pltpu.CompilerParams(collective_id=0, has_side_effects=True),
        name="grid_x",
    )(
        sample_pos.T,
        block_count[None, :],
        grid_block[None, :],
        block_slab.reshape(1, blocks),
        samples,
        table,
        maps,
    )

    per = math.gcd(chunks, PER)
    ytab, ztab = right_table(freq), left_table(depth)
    pairs = each // 2
    imaged = pl.pallas_call(
        functools.partial(add_kernel, per),
        grid_spec=pltpu.PrefetchScalarGridSpec(
            num_scalar_prefetch=1,
            grid=(slab_total,),
            in_specs=[
                pl.BlockSpec((1, tiles, each, tile), lambda i, a: (i, 0, 0, 0)),
                pl.BlockSpec((1, tiles, 2, tile), lambda i, a: (i, 0, 0, 0)),
            ],
            out_specs=pl.BlockSpec((pairs, depth, 2 * freq), lambda i, a: (0, 0, 0)),
            scratch_shapes=[
                pltpu.VMEM((freq // LANES, (depth + SPAN) * each, LANES), jnp.float32)
            ],
        ),
        out_shape=jax.ShapeDtypeStruct((pairs, depth, 2 * freq), jnp.bfloat16),
        name="add_yz",
    )(limits, sent, spots)

    shares = x_own // x_here
    memory = pl.BlockSpec(memory_space=pltpu.VMEM)
    return pl.pallas_call(
        image_kernel,
        in_specs=[memory] * 4,
        out_specs=memory,
        out_shape=jax.ShapeDtypeStruct((planes, x_own, 2 * freq), jnp.float32),
        scratch_shapes=[
            pltpu.VMEM((x_here, slab_total, planes, 2 * freq), jnp.bfloat16),
            pltpu.VMEM((x_here, slab_total, planes, 2 * freq), jnp.bfloat16),
            pltpu.VMEM((coil_total, shares, x_here, planes, 2 * freq), jnp.bfloat16),
            pltpu.SemaphoreType.DMA((x_here, slab_total)),
            pltpu.SemaphoreType.DMA((x_here, slab_total)),
            pltpu.SemaphoreType.DMA((coil_total, shares, x_here)),
            pltpu.SemaphoreType.DMA((coil_total, shares, x_here)),
        ],
        compiler_params=pltpu.CompilerParams(collective_id=1, has_side_effects=True),
        name="image_sum",
    )(imaged, maps, ytab, ztab)


def solution(mesh):
    return jax.shard_map(
        per_device,
        mesh=mesh,
        in_specs=(
            P("coil", "slab", None),
            P("slab", None),
            P("slab"),
            P("slab"),
            P("slab", None),
            P(None, "slab", "coil", None),
        ),
        out_specs=P("slab", "coil", None),
        check_vma=False,
    )
```

```python
import functools
import math

import jax
import jax.numpy as jnp
import numpy as np
from jax import lax
from jax.experimental import pallas as pl
from jax.experimental.pallas import tpu as pltpu
from jax.sharding import PartitionSpec as P

KX = 256
CELLS = 64
CLASSES = 8
LANES = 128
RUNS = 4
STRETCH = LANES // RUNS
SPAN = 56
PER = 16
DEAD = 9984.0
NT = (((1,), (1,)), ((), ()))
MESH = pl.DeviceIdType.MESH


def twiddle(first, second, length):
    phase = (first * second % length).astype(np.float32) * np.float32(2.0 * math.pi / length)
    scale = np.float32(1.0 / math.sqrt(length))
    return np.cos(phase) * scale, np.sin(phase) * scale


def across_table(coils, rows_out, x_here):
    x0 = (KX - rows_out) // 2
    cosine, sine = twiddle(x0 + np.arange(rows_out)[:, None], np.arange(CELLS)[None, :], KX)
    upper = np.stack([cosine, -sine], axis=1)
    lower = np.stack([sine, cosine], axis=1)
    eye = np.eye(coils, dtype=np.float32)
    tables = []
    for one in (np.stack([upper, lower], axis=1), np.stack([-lower, upper], axis=1)):
        one = one.reshape(rows_out // x_here, 1, x_here, 2, 1, 2, CELLS)
        one = one * eye[None, :, None, None, :, None, None]
        tables.append(one.reshape(2 * coils * rows_out, 2 * coils * CELLS))
    return np.concatenate(tables, axis=0)


def right_table(length):
    cosine, sine = twiddle(np.arange(length)[:, None], np.arange(length)[None, :], length)
    upper = np.concatenate([cosine, sine], axis=1)
    lower = np.concatenate([-sine, cosine], axis=1)
    return jnp.asarray(np.concatenate([upper, lower], axis=0).astype(jnp.bfloat16))


def left_table(length):
    cosine, sine = twiddle(np.arange(length)[:, None], np.arange(length)[None, :], length)
    upper = np.concatenate([cosine, -sine], axis=1)
    lower = np.concatenate([sine, cosine], axis=1)
    return jnp.asarray(np.concatenate([upper, lower], axis=0).astype(jnp.bfloat16))


def spread_table(table, values):
    at = np.arange(2 * CELLS) % CELLS
    cell = CLASSES * (at % CLASSES) + at // CLASSES
    table = table.reshape(table.shape[0], values, CELLS)[:, :, cell]
    return jnp.asarray(table.reshape(table.shape[0], values * 2 * CELLS).astype(jnp.bfloat16))


def hot_rows(spots, depth):
    level = lax.broadcasted_iota(jnp.int32, (16, spots.shape[1]), 0).astype(jnp.float32)
    spots = jnp.broadcast_to(spots, (16, spots.shape[1])).astype(jnp.bfloat16)
    one, none = jnp.bfloat16(1), jnp.bfloat16(0)
    return jnp.concatenate(
        [
            jnp.where((level + at).astype(jnp.bfloat16) == spots, one, none)
            for at in range(0, depth, 16)
        ],
        axis=0,
    )


def permute(values, spots):
    depth = spots.shape[1]
    level = lax.broadcasted_iota(jnp.int32, (depth, depth), 0).astype(jnp.float32)
    hot = jnp.where(level == spots, 1.0, 0.0).astype(jnp.bfloat16)
    return lax.dot_general(values, hot, NT, preferred_element_type=jnp.float32)


def regroup(runs):
    rows, length = runs[0].shape
    place = lax.broadcasted_iota(jnp.int32, (rows, LANES), 1) // STRETCH
    for at in range(length // STRETCH):
        cut = slice(at // RUNS * LANES, at // RUNS * LANES + LANES)
        out = runs[0][:, cut]
        for run in range(1, RUNS):
            out = jnp.where(place == (at + run) % RUNS, runs[run][:, cut], out)
        yield at, out


def order(kz, run):
    length = kz.shape[1]
    pieces = length // LANES
    lane = lax.broadcasted_iota(jnp.int32, (1, length), 1).astype(jnp.float32)
    key = kz * float(length) + lane
    rank = jnp.zeros((1, length), jnp.float32)
    for piece in range(pieces):
        part = key[:, piece * LANES : (piece + 1) * LANES]
        part = jnp.broadcast_to(part, (LANES, LANES)).T
        part = jnp.concatenate([part] * pieces, axis=1)
        rank = rank + jnp.sum(jnp.where(part < key, 1.0, 0.0), axis=0, keepdims=True)
    rank = rank.astype(jnp.int32)
    seat = rank // STRETCH
    spot = seat // RUNS * LANES + (seat + run) % RUNS * STRETCH + rank % STRETCH
    return spot.astype(jnp.float32)


def grid_kernel(
    coils, unroll, planes, freq, pos_ref, count_ref, block_ref, slab_ref, val_ref, tab_ref, map_ref,
    lines_ref, every_ref, limits_ref, maps_ref,
    flat, cells, near, bump, placed, ready, spots, least, most, limits,
    line_out, line_in, line_own, spots_out, spots_in, spots_own,
    limit_out, limit_in, limit_own, map_out, map_in, map_own,
):
    turn_at = pl.program_id(0)
    tiles, slabs, each, tile = ready.shape
    rows = slabs * each
    deals, shares = map_ref.shape[0], map_ref.shape[2]
    slab, coil = lax.axis_index("slab"), lax.axis_index("coil")
    barrier = pltpu.get_barrier_semaphore()
    here = slab // shares == coil

    def line_copy(at, hop):
        peer = lax.rem(slab + hop, slabs)
        return pltpu.make_async_remote_copy(
            ready.at[at, peer], lines_ref.at[slab, at], line_out.at[at, hop], line_in.at[at, hop],
            device_id={"slab": peer}, device_id_type=MESH,
        )

    def line_keep(at):
        return pltpu.make_async_copy(
            ready.at[at, slab], lines_ref.at[slab, at], line_own.at[at]
        )

    def spots_copy(at, hop):
        peer = lax.rem(slab + hop, slabs)
        return pltpu.make_async_remote_copy(
            spots.at[at], every_ref.at[slab, at], spots_out.at[at, hop], spots_in.at[at, hop],
            device_id={"slab": peer}, device_id_type=MESH,
        )

    def spots_keep(at):
        return pltpu.make_async_copy(spots.at[at], every_ref.at[slab, at], spots_own.at[at])

    def limit_copy(hop):
        peer = lax.rem(slab + hop, slabs)
        return pltpu.make_async_remote_copy(
            limits, limits_ref.at[slab], limit_out.at[hop], limit_in.at[hop],
            device_id={"slab": peer}, device_id_type=MESH,
        )

    def limit_keep():
        return pltpu.make_async_copy(limits, limits_ref.at[slab], limit_own)

    def map_copy(deal, share):
        return pltpu.make_async_remote_copy(
            map_ref.at[deal, :, share], maps_ref.at[slab],
            map_out.at[deal, share], map_in.at[slab],
            device_id={"slab": coil * shares + share, "coil": deal}, device_id_type=MESH,
        )

    def map_take(source):
        return pltpu.make_async_remote_copy(
            map_ref.at[0, :, 0], maps_ref.at[source], map_out.at[0, 0], map_in.at[source],
            device_id={"slab": slab, "coil": coil}, device_id_type=MESH,
        )

    def map_keep():
        return pltpu.make_async_copy(
            map_ref.at[coil, :, lax.rem(slab, shares)], maps_ref.at[slab], map_own
        )

    def is_me(deal, share):
        return jnp.logical_and(coil * shares + share == slab, coil == deal)

    @pl.when(turn_at == 0)
    def _():
        for hop in range(1, slabs):
            pl.semaphore_signal(
                barrier, 1, device_id={"slab": lax.rem(slab + hop, slabs)}, device_id_type=MESH
            )
        for source in range(slabs):
            @pl.when(jnp.logical_not(jnp.logical_and(here, source == slab)))
            def _():
                pl.semaphore_signal(
                    barrier, 1, device_id={"slab": source, "coil": slab // shares},
                    device_id_type=MESH,
                )
    length = tile // RUNS
    chunks = tile // LANES

    for piece in range(chunks):
        cut = slice(piece * LANES, (piece + 1) * LANES)
        live = lax.broadcasted_iota(jnp.int32, (CELLS, LANES), 0) < count_ref[:, cut]
        place = jnp.where(live, pos_ref[:, cut].astype(jnp.float32), DEAD)
        both = jnp.concatenate([place, pltpu.roll(place, LANES - 8, 1)], axis=0)
        flat[cut, :] = both.T

    segments = KX // CELLS
    kz = slab_ref[...] * planes + block_ref[...] // (segments * freq)
    ky = block_ref[...] // segments % freq
    seg = block_ref[...] % segments
    kz, ky = kz.astype(jnp.float32), ky.astype(jnp.float32)

    block = lax.broadcasted_iota(jnp.int32, (16, LANES), 0)
    upper = lax.broadcasted_iota(jnp.int32, (16, LANES), 1) >= CELLS
    odd = block >= 8
    own = [block % 2 == half for half in range(2)]
    head = block % 8 < 4
    mine = block % 4 // 2 == upper.astype(jnp.int32)
    level = lax.broadcasted_iota(jnp.int32, (CLASSES, LANES), 0).astype(jnp.float32)

    def step(g, slot):
        at = pl.ds(pl.multiple_of(g * 16, 16), 16)
        left = []
        for c in range(coils):
            straight = val_ref[c, at, :].astype(jnp.float32)
            turned = pltpu.roll(straight, CELLS, 1)
            for low, high in ((straight, turned), (turned, straight)):
                placed_here = jnp.where(
                    odd, jnp.where(upper, high, 0.0), jnp.where(upper, 0.0, low)
                )
                halves = [jnp.where(own[half], placed_here, 0.0) for half in range(2)]
                left.append(jnp.concatenate(halves, axis=1).astype(jnp.bfloat16))
        place = flat[pl.ds(pl.multiple_of(g * 16, 16), 8), :] * 0.125
        for r in range(CLASSES):
            offset = place - ((r + 0.5) * 0.125 - 0.5)
            seat = jnp.floor(offset)
            offset = (offset - seat) * 3.2 - 1.6
            rise = jnp.maximum(1.0 - offset * offset, 0.0)
            near[slot, r] = seat
            bump[slot, r] = rise * rise
        right = []
        for quad in range(4):
            halves = []
            for half in range(2):
                row = pl.ds(2 * quad + half, 1)
                parts = []
                for r in range(CLASSES):
                    seat = jnp.broadcast_to(near[slot, r, row, :], level.shape)
                    high = jnp.broadcast_to(bump[slot, r, row, :], level.shape)
                    parts.append(jnp.where(level == seat, high, 0.0))
                halves.append(jnp.concatenate(parts, axis=0).astype(jnp.bfloat16))
            right.append(jnp.concatenate(halves, axis=1))
        done = lax.dot_general(
            jnp.concatenate(left, axis=0),
            jnp.concatenate(right, axis=0),
            NT,
            preferred_element_type=jnp.float32,
        )
        for v in range(2 * coils):
            rows16 = slice(16 * v, 16 * v + 16)
            both = jnp.where(head, done[rows16, :LANES], done[rows16, LANES:])
            both = jnp.where(mine, both, 0.0)
            cells[at, LANES * v : LANES * (v + 1)] = both.astype(jnp.bfloat16)

    @pl.loop(0, tile // (16 * unroll))
    def _(outer):
        for slot in range(unroll):
            step(outer * unroll + slot, slot)

        @pl.when(jnp.logical_and(turn_at == 0, outer == 0))
        def _():
            pl.semaphore_wait(barrier, slabs - 1 + deals * shares - here.astype(jnp.int32))
            for deal in range(deals):
                for share in range(shares):
                    @pl.when(jnp.logical_not(is_me(deal, share)))
                    def _():
                        map_copy(deal, share).start()

            @pl.when(here)
            def _():
                map_keep().start()

    wide = 2 * coils
    x_here = each // wide
    line = lax.broadcasted_iota(jnp.int32, (rows, LANES), 0)
    x_at = line // each * x_here + line // 2 % x_here + (KX - rows // wide) // 2
    x_at = jnp.concatenate([x_at] * (length // LANES), axis=1)
    pad = jnp.zeros((14, length), jnp.float32)
    for run in range(RUNS):
        cut = slice(run * length, (run + 1) * length)
        moved = lax.dot_general(
            tab_ref[...], cells[cut, :], NT, preferred_element_type=jnp.float32
        )
        turn = (x_at * seg[:, cut]) & 3
        turned = jnp.where((turn & 1) == 0, moved[:rows], moved[rows:])
        turned = jnp.where(turn >= 2, -turned, turned)
        turned = jnp.concatenate([turned, kz[:, cut], ky[:, cut], pad], axis=0)
        spot = order(kz[:, cut], run)
        placed[run] = permute(turned.astype(jnp.bfloat16), spot).astype(jnp.bfloat16)

    @pl.when(turn_at == 0)
    def _():
        least[...] = jnp.full_like(least, 1.0e4)
        most[...] = jnp.zeros_like(most)

    for at, out in regroup([placed.at[run] for run in range(RUNS)]):
        for owner in range(slabs):
            ready[turn_at, owner, :, at * LANES : (at + 1) * LANES] = out[
                owner * each : (owner + 1) * each
            ]
        found = out[rows : rows + 2]
        spots[turn_at, :, at * LANES : (at + 1) * LANES] = found
        found = found.astype(jnp.float32)
        least[at : at + 1] = jnp.minimum(least[at : at + 1], found[0:1])
        most[at : at + 1] = jnp.maximum(most[at : at + 1], found[0:1])

    @pl.when(turn_at == tiles - 1)
    def _():
        step_down = max(8 // each, 1)
        low = jnp.min(least[...].T, axis=0, keepdims=True).astype(jnp.int32)
        low = low // step_down * step_down
        high = jnp.max(most[...].T, axis=0, keepdims=True).astype(jnp.int32)
        high = (high - low) // SPAN + 1
        limits[0:1] = low
        limits[1:2] = high
        limits[2:] = jnp.zeros((6, LANES), jnp.int32)

    for hop in range(1, slabs):
        line_copy(turn_at, hop).start()
        spots_copy(turn_at, hop).start()
    line_keep(turn_at).start()
    spots_keep(turn_at).start()

    @pl.when(turn_at == tiles - 1)
    def _():
        for hop in range(1, slabs):
            limit_copy(hop).start()
        limit_keep().start()
        for deal in range(deals):
            for share in range(shares):
                @pl.when(jnp.logical_not(is_me(deal, share)))
                def _():
                    map_copy(deal, share).wait_send()
        for source in range(slabs):
            @pl.when(jnp.logical_not(jnp.logical_and(here, source == slab)))
            def _():
                map_take(source).wait_recv()

        @pl.when(here)
        def _():
            map_keep().wait()

        for at in range(tiles):
            line_keep(at).wait()
            spots_keep(at).wait()
            for hop in range(1, slabs):
                line_copy(at, hop).wait()
                spots_copy(at, hop).wait()
        limit_keep().wait()
        for hop in range(1, slabs):
            limit_copy(hop).wait()


def add_kernel(
    per, limit_ref, vals_ref, spot_ref, out_ref, total
):
    step = pl.program_id(0)
    chunks = vals_ref.shape[3] // LANES
    tiles, rows = vals_ref.shape[1], vals_ref.shape[2]
    pairs, depth, freq = out_ref.shape[0], out_ref.shape[1], out_ref.shape[2] // 2
    deep = 16 // rows
    width = tiles * LANES
    inner = (lax.broadcasted_iota(jnp.int32, (16, width), 0) // rows).astype(jnp.float32)

    @pl.when(step == 0)
    def _():
        total[...] = jnp.zeros_like(total)

    def pick(outer, part, read):
        cut = pl.ds(pl.multiple_of((outer * per + part) * LANES, LANES), LANES)
        return jnp.concatenate([read(t, cut) for t in range(tiles)], axis=1)

    def add(outer, part, start):
        vals = pick(outer, part, lambda t, cut: vals_ref[0, t, :, cut])
        vals = jnp.concatenate([vals] * deep, axis=0)
        both = pick(outer, part, lambda t, cut: spot_ref[0, t, :, cut].astype(jnp.float32))
        base = jnp.full((16, width), start, jnp.int32).astype(jnp.float32)
        plane = jnp.broadcast_to(both[0:1], (16, width)) - base - inner
        plane = plane.astype(jnp.bfloat16)
        left = [
            jnp.where(plane == jnp.bfloat16(at), vals, jnp.bfloat16(0))
            for at in range(0, SPAN, deep)
        ]
        moved = lax.dot_general(
            jnp.concatenate(left, axis=0),
            hot_rows(both[1:2], freq),
            NT,
            preferred_element_type=jnp.float32,
        )
        at = pl.ds(pl.multiple_of(start * rows, 8), SPAN * rows)
        for half in range(freq // LANES):
            total[half, at, :] += moved[:, half * LANES : (half + 1) * LANES]

    @pl.loop(0, chunks // per)
    def _(outer):
        for part in range(per):
            add(outer, part, limit_ref[step, 0, outer * per + part])

        def extra(part, carry):
            first = limit_ref[step, 0, outer * per + part]

            def again(at, carry):
                add(outer, part, first + at * SPAN)
                return carry

            return lax.fori_loop(1, limit_ref[step, 1, outer * per + part], again, carry)

        lax.fori_loop(0, per, extra, 0)

    @pl.when(step == pl.num_programs(0) - 1)
    def _():
        for pair in range(pairs):
            for part in range(2):
                for half in range(freq // LANES):
                    start = part * freq + half * LANES
                    found = total[half, pl.ds(2 * pair + part, depth, stride=rows), :]
                    out_ref[pair, :, start : start + LANES] = found.astype(jnp.bfloat16)


def image_kernel(
    rows_ref, map_ref, ytab_ref, ztab_ref, out_ref, ready, near, far,
    near_out, near_in, far_out, far_in,
):
    wide, slabs, planes, _ = ready.shape
    coils = rows_ref.shape[0] // wide
    deals, shares = far.shape[0], far.shape[1]
    depth, freq = rows_ref.shape[1], rows_ref.shape[2] // 2
    slab, coil = lax.axis_index("slab"), lax.axis_index("coil")
    barrier = pltpu.get_barrier_semaphore()
    for hop in range(1, slabs):
        peer = {"slab": lax.rem(slab + hop, slabs)}
        pl.semaphore_signal(barrier, 1, device_id=peer, device_id_type=MESH)
    for hop in range(1, deals):
        peer = {"coil": lax.rem(coil + hop, deals)}
        pl.semaphore_signal(barrier, 1, device_id=peer, device_id_type=MESH)

    def near_copy(x, hop):
        peer = lax.rem(slab + hop, slabs)
        return pltpu.make_async_remote_copy(
            ready.at[x, peer], near.at[x, slab], near_out.at[x, hop], near_in.at[x, hop],
            device_id={"slab": peer}, device_id_type=MESH,
        )

    def far_copy(x, source, hop):
        share = lax.rem(source, shares)
        return pltpu.make_async_remote_copy(
            near.at[x, source], far.at[hop, share, x],
            far_out.at[hop, share, x], far_in.at[hop, share, x],
            device_id={"coil": lax.rem(coil + hop, deals)}, device_id_type=MESH,
        )

    for x in range(wide):
        real = imag = 0.0
        for c in range(coils):
            planar = jnp.dot(
                rows_ref[c * wide + x], ytab_ref[...], preferred_element_type=jnp.float32
            ).astype(jnp.bfloat16)
            planar = jnp.concatenate([planar[:, :freq], planar[:, freq:]], axis=0)
            image = jnp.dot(ztab_ref[...], planar, preferred_element_type=jnp.float32)
            image = image.astype(jnp.bfloat16).astype(jnp.float32)
            img_re, img_im = image[:depth], image[depth:]
            maps = map_ref[:, c, x].reshape(depth, 2 * freq).astype(jnp.float32)
            map_re, map_im = maps[:, :freq], maps[:, freq:]
            real = real + (map_re * img_re + map_im * img_im)
            imag = imag + (map_re * img_im - map_im * img_re)
        both = jnp.concatenate([real, imag], axis=1).astype(jnp.bfloat16)
        ready[x] = both.reshape(slabs, planes, 2 * freq)
        near[x, pl.ds(slab, 1)] = ready[x, pl.ds(slab, 1)]
        if x == 0:
            pl.semaphore_wait(barrier, slabs - 1 + deals - 1)
        for hop in range(1, slabs):
            near_copy(x, hop).start()

    for x in range(wide):
        for hop in range(slabs):
            source = lax.rem(slab + slabs - hop, slabs)
            if hop > 0:
                near_copy(x, hop).wait_recv()
            leap = lax.rem(source // shares + deals - coil, deals)

            @pl.when(leap > 0)
            def _():
                far_copy(x, source, leap).start()

    for x in range(wide):
        for share in range(shares):
            value = near[x, coil * shares + share].astype(jnp.float32)
            for hop in range(1, deals):
                far_copy(x, share, hop).wait_recv()
                value = value + far[hop, share, x].astype(jnp.float32)
            out_ref[:, share * wide + x, :] = value
    for x in range(wide):
        for hop in range(1, slabs):
            near_copy(x, hop).wait_send()
        for share in range(shares):
            for hop in range(1, deals):
                far_copy(x, share, hop).wait_send()


def per_device(samples, sample_pos, block_count, grid_block, block_slab, sensitivity):
    slab_total = lax.axis_size("slab")
    coil_total = lax.axis_size("coil")
    coils = samples.shape[0]
    blocks = samples.shape[1]
    planes = sensitivity.shape[1]
    rows_out = sensitivity.shape[2] * coil_total
    depth = planes * slab_total
    freq = sensitivity.shape[3] // 2
    x_here = rows_out // slab_total
    tile = math.gcd(blocks, 2048)
    tiles = blocks // tile
    chunks = tile // LANES
    unroll = math.gcd(tile // 16, 16)
    count = 2 * coils * rows_out
    each = 2 * coils * x_here

    row = pl.BlockSpec((1, tile), lambda b: (0, b))
    table = spread_table(across_table(coils, rows_out, x_here), 2 * coils)
    x_own = sensitivity.shape[2]
    maps = sensitivity.reshape(
        coil_total, coils, planes, x_own // x_here, x_here, 2 * freq
    ).transpose(0, 1, 3, 4, 2, 5)
    anywhere = pl.BlockSpec(memory_space=pl.ANY)
    sent, spots, limits, maps = pl.pallas_call(
        functools.partial(grid_kernel, coils, unroll, planes, freq),
        grid=(tiles,),
        in_specs=[
            pl.BlockSpec((CELLS, tile), lambda b: (0, b)),
            row,
            row,
            row,
            pl.BlockSpec((coils, tile, LANES), lambda b: (0, b, 0)),
            pl.BlockSpec(table.shape, lambda b: (0, 0)),
            anywhere,
        ],
        out_specs=[anywhere] * 4,
        out_shape=[
            jax.ShapeDtypeStruct((slab_total, tiles, each, tile), jnp.bfloat16),
            jax.ShapeDtypeStruct((slab_total, tiles, 2, tile), jnp.bfloat16),
            jax.ShapeDtypeStruct((slab_total, 8, LANES), jnp.int32),
            jax.ShapeDtypeStruct((slab_total, coils) + maps.shape[3:], jnp.bfloat16),
        ],
        scratch_shapes=[
            pltpu.VMEM((tile, LANES), jnp.float32),
            pltpu.VMEM((tile, 2 * coils * LANES), jnp.bfloat16),
            pltpu.VMEM((unroll, CLASSES, 8, LANES), jnp.float32),
            pltpu.VMEM((unroll, CLASSES, 8, LANES), jnp.float32),
            pltpu.VMEM((RUNS, count + 16, tile // RUNS), jnp.bfloat16),
            pltpu.VMEM((tiles, slab_total, each, tile), jnp.bfloat16),
            pltpu.VMEM((tiles, 2, tile), jnp.bfloat16),
            pltpu.VMEM((LANES, LANES), jnp.float32),
            pltpu.VMEM((LANES, LANES), jnp.float32),
            pltpu.VMEM((8, LANES), jnp.int32),
            pltpu.SemaphoreType.DMA((tiles, slab_total)),
            pltpu.SemaphoreType.DMA((tiles, slab_total)),
            pltpu.SemaphoreType.DMA((tiles,)),
            pltpu.SemaphoreType.DMA((tiles, slab_total)),
            pltpu.SemaphoreType.DMA((tiles, slab_total)),
            pltpu.SemaphoreType.DMA((tiles,)),
            pltpu.SemaphoreType.DMA((slab_total,)),
            pltpu.SemaphoreType.DMA((slab_total,)),
            pltpu.SemaphoreType.DMA,
            pltpu.SemaphoreType.DMA((coil_total, x_own // x_here)),
            pltpu.SemaphoreType.DMA((slab_total,)),
            pltpu.SemaphoreType.DMA,
        ],
        compiler_params=pltpu.CompilerParams(collective_id=0, has_side_effects=True),
        name="grid_x",
    )(
        sample_pos.T,
        block_count[None, :],
        grid_block[None, :],
        block_slab.reshape(1, blocks),
        samples,
        table,
        maps,
    )

    per = math.gcd(chunks, PER)
    ytab, ztab = right_table(freq), left_table(depth)
    pairs = each // 2
    imaged = pl.pallas_call(
        functools.partial(add_kernel, per),
        grid_spec=pltpu.PrefetchScalarGridSpec(
            num_scalar_prefetch=1,
            grid=(slab_total,),
            in_specs=[
                pl.BlockSpec((1, tiles, each, tile), lambda i, a: (i, 0, 0, 0)),
                pl.BlockSpec((1, tiles, 2, tile), lambda i, a: (i, 0, 0, 0)),
            ],
            out_specs=pl.BlockSpec((pairs, depth, 2 * freq), lambda i, a: (0, 0, 0)),
            scratch_shapes=[
                pltpu.VMEM((freq // LANES, (depth + SPAN) * each, LANES), jnp.float32)
            ],
        ),
        out_shape=jax.ShapeDtypeStruct((pairs, depth, 2 * freq), jnp.bfloat16),
        name="add_yz",
    )(limits, sent, spots)

    shares = x_own // x_here
    memory = pl.BlockSpec(memory_space=pltpu.VMEM)
    return pl.pallas_call(
        image_kernel,
        in_specs=[memory] * 4,
        out_specs=memory,
        out_shape=jax.ShapeDtypeStruct((planes, x_own, 2 * freq), jnp.float32),
        scratch_shapes=[
            pltpu.VMEM((x_here, slab_total, planes, 2 * freq), jnp.bfloat16),
            pltpu.VMEM((x_here, slab_total, planes, 2 * freq), jnp.bfloat16),
            pltpu.VMEM((coil_total, shares, x_here, planes, 2 * freq), jnp.bfloat16),
            pltpu.SemaphoreType.DMA((x_here, slab_total)),
            pltpu.SemaphoreType.DMA((x_here, slab_total)),
            pltpu.SemaphoreType.DMA((coil_total, shares, x_here)),
            pltpu.SemaphoreType.DMA((coil_total, shares, x_here)),
        ],
        compiler_params=pltpu.CompilerParams(collective_id=1, has_side_effects=True),
        name="image_sum",
    )(imaged, maps, ytab, ztab)


def solution(mesh):
    return jax.shard_map(
        per_device,
        mesh=mesh,
        in_specs=(
            P("coil", "slab", None),
            P("slab", None),
            P("slab"),
            P("slab"),
            P("slab", None),
            P(None, "slab", "coil", None),
        ),
        out_specs=P("slab", "coil", None),
        check_vma=False,
    )
```

```python
import functools
import math

import jax
import jax.numpy as jnp
import numpy as np
from jax import lax
from jax.experimental import pallas as pl
from jax.experimental.pallas import tpu as pltpu
from jax.sharding import PartitionSpec as P

KX = 256
CELLS = 64
CLASSES = 8
LANES = 128
RUNS = 4
STRETCH = LANES // RUNS
SPAN = 56
PER = 16
DEAD = 9984.0
NT = (((1,), (1,)), ((), ()))
MESH = pl.DeviceIdType.MESH


def twiddle(first, second, length):
    phase = (first * second % length).astype(np.float32) * np.float32(2.0 * math.pi / length)
    scale = np.float32(1.0 / math.sqrt(length))
    return np.cos(phase) * scale, np.sin(phase) * scale


def across_table(coils, rows_out, x_here):
    x0 = (KX - rows_out) // 2
    cosine, sine = twiddle(x0 + np.arange(rows_out)[:, None], np.arange(CELLS)[None, :], KX)
    upper = np.stack([cosine, -sine], axis=1)
    lower = np.stack([sine, cosine], axis=1)
    eye = np.eye(coils, dtype=np.float32)
    tables = []
    for one in (np.stack([upper, lower], axis=1), np.stack([-lower, upper], axis=1)):
        one = one.reshape(rows_out // x_here, 1, x_here, 2, 1, 2, CELLS)
        one = one * eye[None, :, None, None, :, None, None]
        tables.append(one.reshape(2 * coils * rows_out, 2 * coils * CELLS))
    return np.concatenate(tables, axis=0)


def right_table(length):
    cosine, sine = twiddle(np.arange(length)[:, None], np.arange(length)[None, :], length)
    upper = np.concatenate([cosine, sine], axis=1)
    lower = np.concatenate([-sine, cosine], axis=1)
    return jnp.asarray(np.concatenate([upper, lower], axis=0).astype(jnp.bfloat16))


def left_table(length):
    cosine, sine = twiddle(np.arange(length)[:, None], np.arange(length)[None, :], length)
    upper = np.concatenate([cosine, -sine], axis=1)
    lower = np.concatenate([sine, cosine], axis=1)
    return jnp.asarray(np.concatenate([upper, lower], axis=0).astype(jnp.bfloat16))


def spread_table(table, values):
    at = np.arange(2 * CELLS) % CELLS
    cell = CLASSES * (at % CLASSES) + at // CLASSES
    table = table.reshape(table.shape[0], values, CELLS)[:, :, cell]
    return jnp.asarray(table.reshape(table.shape[0], values * 2 * CELLS).astype(jnp.bfloat16))


def hot_rows(spots, depth):
    level = lax.broadcasted_iota(jnp.int32, (16, spots.shape[1]), 0).astype(jnp.float32)
    spots = jnp.broadcast_to(spots, (16, spots.shape[1])).astype(jnp.bfloat16)
    one, none = jnp.bfloat16(1), jnp.bfloat16(0)
    return jnp.concatenate(
        [
            jnp.where((level + at).astype(jnp.bfloat16) == spots, one, none)
            for at in range(0, depth, 16)
        ],
        axis=0,
    )


def permute(values, spots):
    length = spots.shape[1]
    deep = math.gcd(length, 256)
    hot = [hot_rows(spots - float(at), deep) for at in range(0, length, deep)]
    hot = jnp.concatenate(hot, axis=0)
    return lax.dot_general(values, hot, NT, preferred_element_type=jnp.float32)


def regroup(runs):
    rows, length = runs[0].shape
    place = lax.broadcasted_iota(jnp.int32, (rows, LANES), 1) // STRETCH
    for at in range(length // STRETCH):
        cut = slice(at // RUNS * LANES, at // RUNS * LANES + LANES)
        out = runs[0][:, cut]
        for run in range(1, RUNS):
            out = jnp.where(place == (at + run) % RUNS, runs[run][:, cut], out)
        yield at, out


def order(kz, run):
    length = kz.shape[1]
    pieces = length // LANES
    lane = lax.broadcasted_iota(jnp.int32, (1, length), 1).astype(jnp.float32)
    key = kz * float(length) + lane
    rank = jnp.zeros((1, length), jnp.float32)
    for piece in range(pieces):
        part = key[:, piece * LANES : (piece + 1) * LANES]
        part = jnp.broadcast_to(part, (LANES, LANES)).T
        part = jnp.concatenate([part] * pieces, axis=1)
        rank = rank + jnp.sum(jnp.where(part < key, 1.0, 0.0), axis=0, keepdims=True)
    rank = rank.astype(jnp.int32)
    seat = rank // STRETCH
    spot = seat // RUNS * LANES + (seat + run) % RUNS * STRETCH + rank % STRETCH
    return spot.astype(jnp.float32)


def grid_kernel(
    coils, unroll, planes, freq, pos_ref, count_ref, block_ref, slab_ref, val_ref, tab_ref, map_ref,
    lines_ref, every_ref, limits_ref, maps_ref,
    flat, cells, near, bump, placed, ready, spots, least, most, limits,
    line_out, line_in, line_own, spots_out, spots_in, spots_own,
    limit_out, limit_in, limit_own, map_out, map_in, map_own,
):
    turn_at = pl.program_id(0)
    tiles, slabs, each, tile = ready.shape
    rows = slabs * each
    deals, shares = map_ref.shape[0], map_ref.shape[2]
    slab, coil = lax.axis_index("slab"), lax.axis_index("coil")
    barrier = pltpu.get_barrier_semaphore()
    here = slab // shares == coil

    def line_copy(at, hop):
        peer = lax.rem(slab + hop, slabs)
        return pltpu.make_async_remote_copy(
            ready.at[at, peer], lines_ref.at[slab, at], line_out.at[at, hop], line_in.at[at, hop],
            device_id={"slab": peer}, device_id_type=MESH,
        )

    def line_keep(at):
        return pltpu.make_async_copy(
            ready.at[at, slab], lines_ref.at[slab, at], line_own.at[at]
        )

    def spots_copy(at, hop):
        peer = lax.rem(slab + hop, slabs)
        return pltpu.make_async_remote_copy(
            spots.at[at], every_ref.at[slab, at], spots_out.at[at, hop], spots_in.at[at, hop],
            device_id={"slab": peer}, device_id_type=MESH,
        )

    def spots_keep(at):
        return pltpu.make_async_copy(spots.at[at], every_ref.at[slab, at], spots_own.at[at])

    def limit_copy(hop):
        peer = lax.rem(slab + hop, slabs)
        return pltpu.make_async_remote_copy(
            limits, limits_ref.at[slab], limit_out.at[hop], limit_in.at[hop],
            device_id={"slab": peer}, device_id_type=MESH,
        )

    def limit_keep():
        return pltpu.make_async_copy(limits, limits_ref.at[slab], limit_own)

    def map_copy(deal, share):
        return pltpu.make_async_remote_copy(
            map_ref.at[deal, :, share], maps_ref.at[slab],
            map_out.at[deal, share], map_in.at[slab],
            device_id={"slab": coil * shares + share, "coil": deal}, device_id_type=MESH,
        )

    def map_take(source):
        return pltpu.make_async_remote_copy(
            map_ref.at[0, :, 0], maps_ref.at[source], map_out.at[0, 0], map_in.at[source],
            device_id={"slab": slab, "coil": coil}, device_id_type=MESH,
        )

    def map_keep():
        return pltpu.make_async_copy(
            map_ref.at[coil, :, lax.rem(slab, shares)], maps_ref.at[slab], map_own
        )

    def is_me(deal, share):
        return jnp.logical_and(coil * shares + share == slab, coil == deal)

    @pl.when(turn_at == 0)
    def _():
        for hop in range(1, slabs):
            pl.semaphore_signal(
                barrier, 1, device_id={"slab": lax.rem(slab + hop, slabs)}, device_id_type=MESH
            )
        for source in range(slabs):
            @pl.when(jnp.logical_not(jnp.logical_and(here, source == slab)))
            def _():
                pl.semaphore_signal(
                    barrier, 1, device_id={"slab": source, "coil": slab // shares},
                    device_id_type=MESH,
                )
    length = tile // RUNS
    chunks = tile // LANES

    for piece in range(chunks):
        cut = slice(piece * LANES, (piece + 1) * LANES)
        live = lax.broadcasted_iota(jnp.int32, (CELLS, LANES), 0) < count_ref[:, cut]
        place = jnp.where(live, pos_ref[:, cut].astype(jnp.float32), DEAD)
        both = jnp.concatenate([place, pltpu.roll(place, LANES - 8, 1)], axis=0)
        flat[cut, :] = both.T

    segments = KX // CELLS
    kz = slab_ref[...] * planes + block_ref[...] // (segments * freq)
    ky = block_ref[...] // segments % freq
    seg = block_ref[...] % segments
    kz, ky = kz.astype(jnp.float32), ky.astype(jnp.float32)

    block = lax.broadcasted_iota(jnp.int32, (16, LANES), 0)
    upper = lax.broadcasted_iota(jnp.int32, (16, LANES), 1) >= CELLS
    odd = block >= 8
    own = [block % 2 == half for half in range(2)]
    head = block % 8 < 4
    mine = block % 4 // 2 == upper.astype(jnp.int32)
    level = lax.broadcasted_iota(jnp.int32, (CLASSES, LANES), 0).astype(jnp.float32)

    def step(g, slot):
        at = pl.ds(pl.multiple_of(g * 16, 16), 16)
        left = []
        for c in range(coils):
            straight = val_ref[c, at, :].astype(jnp.float32)
            turned = pltpu.roll(straight, CELLS, 1)
            for low, high in ((straight, turned), (turned, straight)):
                placed_here = jnp.where(
                    odd, jnp.where(upper, high, 0.0), jnp.where(upper, 0.0, low)
                )
                halves = [jnp.where(own[half], placed_here, 0.0) for half in range(2)]
                left.append(jnp.concatenate(halves, axis=1).astype(jnp.bfloat16))
        place = flat[pl.ds(pl.multiple_of(g * 16, 16), 8), :] * 0.125
        for r in range(CLASSES):
            offset = place - ((r + 0.5) * 0.125 - 0.5)
            seat = jnp.floor(offset)
            offset = (offset - seat) * 3.2 - 1.6
            rise = jnp.maximum(1.0 - offset * offset, 0.0)
            near[slot, r] = seat
            bump[slot, r] = rise * rise
        right = []
        for quad in range(4):
            halves = []
            for half in range(2):
                row = pl.ds(2 * quad + half, 1)
                parts = []
                for r in range(CLASSES):
                    seat = jnp.broadcast_to(near[slot, r, row, :], level.shape)
                    high = jnp.broadcast_to(bump[slot, r, row, :], level.shape)
                    parts.append(jnp.where(level == seat, high, 0.0))
                halves.append(jnp.concatenate(parts, axis=0).astype(jnp.bfloat16))
            right.append(jnp.concatenate(halves, axis=1))
        done = lax.dot_general(
            jnp.concatenate(left, axis=0),
            jnp.concatenate(right, axis=0),
            NT,
            preferred_element_type=jnp.float32,
        )
        for v in range(2 * coils):
            rows16 = slice(16 * v, 16 * v + 16)
            both = jnp.where(head, done[rows16, :LANES], done[rows16, LANES:])
            both = jnp.where(mine, both, 0.0)
            cells[at, LANES * v : LANES * (v + 1)] = both.astype(jnp.bfloat16)

    @pl.loop(0, tile // (16 * unroll))
    def _(outer):
        for slot in range(unroll):
            step(outer * unroll + slot, slot)

        @pl.when(jnp.logical_and(turn_at == 0, outer == 0))
        def _():
            pl.semaphore_wait(barrier, slabs - 1 + deals * shares - here.astype(jnp.int32))
            for deal in range(deals):
                for share in range(shares):
                    @pl.when(jnp.logical_not(is_me(deal, share)))
                    def _():
                        map_copy(deal, share).start()

            @pl.when(here)
            def _():
                map_keep().start()

    wide = 2 * coils
    x_here = each // wide
    line = lax.broadcasted_iota(jnp.int32, (rows, LANES), 0)
    x_at = line // each * x_here + line // 2 % x_here + (KX - rows // wide) // 2
    x_at = jnp.concatenate([x_at] * (length // LANES), axis=1)
    pad = jnp.zeros((14, length), jnp.float32)
    for run in range(RUNS):
        cut = slice(run * length, (run + 1) * length)
        moved = lax.dot_general(
            tab_ref[...], cells[cut, :], NT, preferred_element_type=jnp.float32
        )
        turn = (x_at * seg[:, cut]) & 3
        turned = jnp.where((turn & 1) == 0, moved[:rows], moved[rows:])
        turned = jnp.where(turn >= 2, -turned, turned)
        turned = jnp.concatenate([turned, kz[:, cut], ky[:, cut], pad], axis=0)
        spot = order(kz[:, cut], run)
        placed[run] = permute(turned.astype(jnp.bfloat16), spot).astype(jnp.bfloat16)

    @pl.when(turn_at == 0)
    def _():
        least[...] = jnp.full_like(least, 1.0e4)
        most[...] = jnp.zeros_like(most)

    for at, out in regroup([placed.at[run] for run in range(RUNS)]):
        for owner in range(slabs):
            ready[turn_at, owner, :, at * LANES : (at + 1) * LANES] = out[
                owner * each : (owner + 1) * each
            ]
        found = out[rows : rows + 2]
        spots[turn_at, :, at * LANES : (at + 1) * LANES] = found
        found = found.astype(jnp.float32)
        least[at : at + 1] = jnp.minimum(least[at : at + 1], found[0:1])
        most[at : at + 1] = jnp.maximum(most[at : at + 1], found[0:1])

    @pl.when(turn_at == tiles - 1)
    def _():
        step_down = max(8 // each, 1)
        low = jnp.min(least[...].T, axis=0, keepdims=True).astype(jnp.int32)
        low = low // step_down * step_down
        high = jnp.max(most[...].T, axis=0, keepdims=True).astype(jnp.int32)
        high = (high - low) // SPAN + 1
        limits[0:1] = low
        limits[1:2] = high
        limits[2:] = jnp.zeros((6, LANES), jnp.int32)

    for hop in range(1, slabs):
        line_copy(turn_at, hop).start()
        spots_copy(turn_at, hop).start()
    line_keep(turn_at).start()
    spots_keep(turn_at).start()

    @pl.when(turn_at == tiles - 1)
    def _():
        for hop in range(1, slabs):
            limit_copy(hop).start()
        limit_keep().start()
        for deal in range(deals):
            for share in range(shares):
                @pl.when(jnp.logical_not(is_me(deal, share)))
                def _():
                    map_copy(deal, share).wait_send()
        for source in range(slabs):
            @pl.when(jnp.logical_not(jnp.logical_and(here, source == slab)))
            def _():
                map_take(source).wait_recv()

        @pl.when(here)
        def _():
            map_keep().wait()

        for at in range(tiles):
            line_keep(at).wait()
            spots_keep(at).wait()
            for hop in range(1, slabs):
                line_copy(at, hop).wait()
                spots_copy(at, hop).wait()
        limit_keep().wait()
        for hop in range(1, slabs):
            limit_copy(hop).wait()


def add_kernel(
    per, limit_ref, vals_ref, spot_ref, out_ref, total
):
    step = pl.program_id(0)
    chunks = vals_ref.shape[3] // LANES
    tiles, rows = vals_ref.shape[1], vals_ref.shape[2]
    pairs, depth, freq = out_ref.shape[0], out_ref.shape[1], out_ref.shape[2] // 2
    deep = 16 // rows
    width = tiles * LANES
    inner = (lax.broadcasted_iota(jnp.int32, (16, width), 0) // rows).astype(jnp.float32)

    @pl.when(step == 0)
    def _():
        total[...] = jnp.zeros_like(total)

    def pick(outer, part, read):
        cut = pl.ds(pl.multiple_of((outer * per + part) * LANES, LANES), LANES)
        return jnp.concatenate([read(t, cut) for t in range(tiles)], axis=1)

    def add(outer, part, start):
        vals = pick(outer, part, lambda t, cut: vals_ref[0, t, :, cut])
        vals = jnp.concatenate([vals] * deep, axis=0)
        both = pick(outer, part, lambda t, cut: spot_ref[0, t, :, cut].astype(jnp.float32))
        base = jnp.full((16, width), start, jnp.int32).astype(jnp.float32)
        plane = jnp.broadcast_to(both[0:1], (16, width)) - base - inner
        plane = plane.astype(jnp.bfloat16)
        left = [
            jnp.where(plane == jnp.bfloat16(at), vals, jnp.bfloat16(0))
            for at in range(0, SPAN, deep)
        ]
        moved = lax.dot_general(
            jnp.concatenate(left, axis=0),
            hot_rows(both[1:2], freq),
            NT,
            preferred_element_type=jnp.float32,
        )
        at = pl.ds(pl.multiple_of(start * rows, 8), SPAN * rows)
        for half in range(freq // LANES):
            total[half, at, :] += moved[:, half * LANES : (half + 1) * LANES]

    @pl.loop(0, chunks // per)
    def _(outer):
        for part in range(per):
            add(outer, part, limit_ref[step, 0, outer * per + part])

        def extra(part, carry):
            first = limit_ref[step, 0, outer * per + part]

            def again(at, carry):
                add(outer, part, first + at * SPAN)
                return carry

            return lax.fori_loop(1, limit_ref[step, 1, outer * per + part], again, carry)

        lax.fori_loop(0, per, extra, 0)

    @pl.when(step == pl.num_programs(0) - 1)
    def _():
        for pair in range(pairs):
            for part in range(2):
                for half in range(freq // LANES):
                    start = part * freq + half * LANES
                    found = total[half, pl.ds(2 * pair + part, depth, stride=rows), :]
                    out_ref[pair, :, start : start + LANES] = found.astype(jnp.bfloat16)


def image_kernel(
    rows_ref, map_ref, ytab_ref, ztab_ref, out_ref, ready, near, far,
    near_out, near_in, far_out, far_in,
):
    wide, slabs, planes, _ = ready.shape
    coils = rows_ref.shape[0] // wide
    deals, shares = far.shape[0], far.shape[1]
    depth, freq = rows_ref.shape[1], rows_ref.shape[2] // 2
    slab, coil = lax.axis_index("slab"), lax.axis_index("coil")
    barrier = pltpu.get_barrier_semaphore()
    for hop in range(1, slabs):
        peer = {"slab": lax.rem(slab + hop, slabs)}
        pl.semaphore_signal(barrier, 1, device_id=peer, device_id_type=MESH)
    for hop in range(1, deals):
        peer = {"coil": lax.rem(coil + hop, deals)}
        pl.semaphore_signal(barrier, 1, device_id=peer, device_id_type=MESH)

    def near_copy(x, hop):
        peer = lax.rem(slab + hop, slabs)
        return pltpu.make_async_remote_copy(
            ready.at[x, peer], near.at[x, slab], near_out.at[x, hop], near_in.at[x, hop],
            device_id={"slab": peer}, device_id_type=MESH,
        )

    def far_copy(x, source, hop):
        share = lax.rem(source, shares)
        return pltpu.make_async_remote_copy(
            near.at[x, source], far.at[hop, share, x],
            far_out.at[hop, share, x], far_in.at[hop, share, x],
            device_id={"coil": lax.rem(coil + hop, deals)}, device_id_type=MESH,
        )

    for x in range(wide):
        real = imag = 0.0
        for c in range(coils):
            planar = jnp.dot(
                rows_ref[c * wide + x], ytab_ref[...], preferred_element_type=jnp.float32
            ).astype(jnp.bfloat16)
            planar = jnp.concatenate([planar[:, :freq], planar[:, freq:]], axis=0)
            image = jnp.dot(ztab_ref[...], planar, preferred_element_type=jnp.float32)
            image = image.astype(jnp.bfloat16).astype(jnp.float32)
            img_re, img_im = image[:depth], image[depth:]
            maps = map_ref[:, c, x].reshape(depth, 2 * freq).astype(jnp.float32)
            map_re, map_im = maps[:, :freq], maps[:, freq:]
            real = real + (map_re * img_re + map_im * img_im)
            imag = imag + (map_re * img_im - map_im * img_re)
        both = jnp.concatenate([real, imag], axis=1).astype(jnp.bfloat16)
        ready[x] = both.reshape(slabs, planes, 2 * freq)
        near[x, pl.ds(slab, 1)] = ready[x, pl.ds(slab, 1)]
        if x == 0:
            pl.semaphore_wait(barrier, slabs - 1 + deals - 1)
        for hop in range(1, slabs):
            near_copy(x, hop).start()

    for x in range(wide):
        for hop in range(slabs):
            source = lax.rem(slab + slabs - hop, slabs)
            if hop > 0:
                near_copy(x, hop).wait_recv()
            leap = lax.rem(source // shares + deals - coil, deals)

            @pl.when(leap > 0)
            def _():
                far_copy(x, source, leap).start()

    for x in range(wide):
        for share in range(shares):
            value = near[x, coil * shares + share].astype(jnp.float32)
            for hop in range(1, deals):
                far_copy(x, share, hop).wait_recv()
                value = value + far[hop, share, x].astype(jnp.float32)
            out_ref[:, share * wide + x, :] = value
    for x in range(wide):
        for hop in range(1, slabs):
            near_copy(x, hop).wait_send()
        for share in range(shares):
            for hop in range(1, deals):
                far_copy(x, share, hop).wait_send()


def per_device(samples, sample_pos, block_count, grid_block, block_slab, sensitivity):
    slab_total = lax.axis_size("slab")
    coil_total = lax.axis_size("coil")
    coils = samples.shape[0]
    blocks = samples.shape[1]
    planes = sensitivity.shape[1]
    rows_out = sensitivity.shape[2] * coil_total
    depth = planes * slab_total
    freq = sensitivity.shape[3] // 2
    x_here = rows_out // slab_total
    tile = math.gcd(blocks, 2048)
    tiles = blocks // tile
    chunks = tile // LANES
    unroll = math.gcd(tile // 16, 64)
    count = 2 * coils * rows_out
    each = 2 * coils * x_here

    row = pl.BlockSpec((1, tile), lambda b: (0, b))
    table = spread_table(across_table(coils, rows_out, x_here), 2 * coils)
    x_own = sensitivity.shape[2]
    maps = sensitivity.reshape(
        coil_total, coils, planes, x_own // x_here, x_here, 2 * freq
    ).transpose(0, 1, 3, 4, 2, 5)
    anywhere = pl.BlockSpec(memory_space=pl.ANY)
    sent, spots, limits, maps = pl.pallas_call(
        functools.partial(grid_kernel, coils, unroll, planes, freq),
        grid=(tiles,),
        in_specs=[
            pl.BlockSpec((CELLS, tile), lambda b: (0, b)),
            row,
            row,
            row,
            pl.BlockSpec((coils, tile, LANES), lambda b: (0, b, 0)),
            pl.BlockSpec(table.shape, lambda b: (0, 0)),
            anywhere,
        ],
        out_specs=[anywhere] * 4,
        out_shape=[
            jax.ShapeDtypeStruct((slab_total, tiles, each, tile), jnp.bfloat16),
            jax.ShapeDtypeStruct((slab_total, tiles, 2, tile), jnp.bfloat16),
            jax.ShapeDtypeStruct((slab_total, 8, LANES), jnp.int32),
            jax.ShapeDtypeStruct((slab_total, coils) + maps.shape[3:], jnp.bfloat16),
        ],
        scratch_shapes=[
            pltpu.VMEM((tile, LANES), jnp.float32),
            pltpu.VMEM((tile, 2 * coils * LANES), jnp.bfloat16),
            pltpu.VMEM((unroll, CLASSES, 8, LANES), jnp.float32),
            pltpu.VMEM((unroll, CLASSES, 8, LANES), jnp.float32),
            pltpu.VMEM((RUNS, count + 16, tile // RUNS), jnp.bfloat16),
            pltpu.VMEM((tiles, slab_total, each, tile), jnp.bfloat16),
            pltpu.VMEM((tiles, 2, tile), jnp.bfloat16),
            pltpu.VMEM((LANES, LANES), jnp.float32),
            pltpu.VMEM((LANES, LANES), jnp.float32),
            pltpu.VMEM((8, LANES), jnp.int32),
            pltpu.SemaphoreType.DMA((tiles, slab_total)),
            pltpu.SemaphoreType.DMA((tiles, slab_total)),
            pltpu.SemaphoreType.DMA((tiles,)),
            pltpu.SemaphoreType.DMA((tiles, slab_total)),
            pltpu.SemaphoreType.DMA((tiles, slab_total)),
            pltpu.SemaphoreType.DMA((tiles,)),
            pltpu.SemaphoreType.DMA((slab_total,)),
            pltpu.SemaphoreType.DMA((slab_total,)),
            pltpu.SemaphoreType.DMA,
            pltpu.SemaphoreType.DMA((coil_total, x_own // x_here)),
            pltpu.SemaphoreType.DMA((slab_total,)),
            pltpu.SemaphoreType.DMA,
        ],
        compiler_params=pltpu.CompilerParams(collective_id=0, has_side_effects=True),
        name="grid_x",
    )(
        sample_pos.T,
        block_count[None, :],
        grid_block[None, :],
        block_slab.reshape(1, blocks),
        samples,
        table,
        maps,
    )

    per = math.gcd(chunks, PER)
    ytab, ztab = right_table(freq), left_table(depth)
    pairs = each // 2
    imaged = pl.pallas_call(
        functools.partial(add_kernel, per),
        grid_spec=pltpu.PrefetchScalarGridSpec(
            num_scalar_prefetch=1,
            grid=(slab_total,),
            in_specs=[
                pl.BlockSpec((1, tiles, each, tile), lambda i, a: (i, 0, 0, 0)),
                pl.BlockSpec((1, tiles, 2, tile), lambda i, a: (i, 0, 0, 0)),
            ],
            out_specs=pl.BlockSpec((pairs, depth, 2 * freq), lambda i, a: (0, 0, 0)),
            scratch_shapes=[
                pltpu.VMEM((freq // LANES, (depth + SPAN) * each, LANES), jnp.float32)
            ],
        ),
        out_shape=jax.ShapeDtypeStruct((pairs, depth, 2 * freq), jnp.bfloat16),
        name="add_yz",
    )(limits, sent, spots)

    shares = x_own // x_here
    memory = pl.BlockSpec(memory_space=pltpu.VMEM)
    return pl.pallas_call(
        image_kernel,
        in_specs=[memory] * 4,
        out_specs=memory,
        out_shape=jax.ShapeDtypeStruct((planes, x_own, 2 * freq), jnp.float32),
        scratch_shapes=[
            pltpu.VMEM((x_here, slab_total, planes, 2 * freq), jnp.bfloat16),
            pltpu.VMEM((x_here, slab_total, planes, 2 * freq), jnp.bfloat16),
            pltpu.VMEM((coil_total, shares, x_here, planes, 2 * freq), jnp.bfloat16),
            pltpu.SemaphoreType.DMA((x_here, slab_total)),
            pltpu.SemaphoreType.DMA((x_here, slab_total)),
            pltpu.SemaphoreType.DMA((coil_total, shares, x_here)),
            pltpu.SemaphoreType.DMA((coil_total, shares, x_here)),
        ],
        compiler_params=pltpu.CompilerParams(collective_id=1, has_side_effects=True),
        name="image_sum",
    )(imaged, maps, ytab, ztab)


def solution(mesh):
    return jax.shard_map(
        per_device,
        mesh=mesh,
        in_specs=(
            P("coil", "slab", None),
            P("slab", None),
            P("slab"),
            P("slab"),
            P("slab", None),
            P(None, "slab", "coil", None),
        ),
        out_specs=P("slab", "coil", None),
        check_vma=False,
    )
```

```python
import functools
import math

import jax
import jax.numpy as jnp
import numpy as np
from jax import lax
from jax.experimental import pallas as pl
from jax.experimental.pallas import tpu as pltpu
from jax.sharding import PartitionSpec as P

KX = 256
CELLS = 64
CLASSES = 8
LANES = 128
RUNS = 4
STRETCH = LANES // RUNS
SPAN = 56
PER = 16
DEAD = 9984.0
NT = (((1,), (1,)), ((), ()))
MESH = pl.DeviceIdType.MESH


def twiddle(first, second, length):
    phase = (first * second % length).astype(np.float32) * np.float32(2.0 * math.pi / length)
    scale = np.float32(1.0 / math.sqrt(length))
    return np.cos(phase) * scale, np.sin(phase) * scale


def across_table(coils, rows_out, x_here):
    x0 = (KX - rows_out) // 2
    cosine, sine = twiddle(x0 + np.arange(rows_out)[:, None], np.arange(CELLS)[None, :], KX)
    upper = np.stack([cosine, -sine], axis=1)
    lower = np.stack([sine, cosine], axis=1)
    eye = np.eye(coils, dtype=np.float32)
    tables = []
    for one in (np.stack([upper, lower], axis=1), np.stack([-lower, upper], axis=1)):
        one = one.reshape(rows_out // x_here, 1, x_here, 2, 1, 2, CELLS)
        one = one * eye[None, :, None, None, :, None, None]
        tables.append(one.reshape(2 * coils * rows_out, 2 * coils * CELLS))
    return np.concatenate(tables, axis=0)


def right_table(length):
    cosine, sine = twiddle(np.arange(length)[:, None], np.arange(length)[None, :], length)
    upper = np.concatenate([cosine, sine], axis=1)
    lower = np.concatenate([-sine, cosine], axis=1)
    return jnp.asarray(np.concatenate([upper, lower], axis=0).astype(jnp.bfloat16))


def left_table(length):
    cosine, sine = twiddle(np.arange(length)[:, None], np.arange(length)[None, :], length)
    upper = np.concatenate([cosine, -sine], axis=1)
    lower = np.concatenate([sine, cosine], axis=1)
    return jnp.asarray(np.concatenate([upper, lower], axis=0).astype(jnp.bfloat16))


def spread_table(table, values):
    at = np.arange(2 * CELLS) % CELLS
    cell = CLASSES * (at % CLASSES) + at // CLASSES
    table = table.reshape(table.shape[0], values, CELLS)[:, :, cell]
    return jnp.asarray(table.reshape(table.shape[0], values * 2 * CELLS).astype(jnp.bfloat16))


def hot_rows(spots, depth):
    level = lax.broadcasted_iota(jnp.int32, (16, spots.shape[1]), 0).astype(jnp.float32)
    spots = jnp.broadcast_to(spots, (16, spots.shape[1])).astype(jnp.bfloat16)
    one, none = jnp.bfloat16(1), jnp.bfloat16(0)
    return jnp.concatenate(
        [
            jnp.where((level + at).astype(jnp.bfloat16) == spots, one, none)
            for at in range(0, depth, 16)
        ],
        axis=0,
    )


def permute(values, spots):
    length = spots.shape[1]
    deep = math.gcd(length, 256)
    hot = [hot_rows(spots - float(at), deep) for at in range(0, length, deep)]
    hot = jnp.concatenate(hot, axis=0)
    return lax.dot_general(values, hot, NT, preferred_element_type=jnp.float32)


def regroup(runs):
    rows, length = runs[0].shape
    place = lax.broadcasted_iota(jnp.int32, (rows, LANES), 1) // STRETCH
    for at in range(length // STRETCH):
        cut = slice(at // RUNS * LANES, at // RUNS * LANES + LANES)
        out = runs[0][:, cut]
        for run in range(1, RUNS):
            out = jnp.where(place == (at + run) % RUNS, runs[run][:, cut], out)
        yield at, out


def order(kz, run):
    length = kz.shape[1]
    pieces = length // LANES
    lane = lax.broadcasted_iota(jnp.int32, (1, length), 1).astype(jnp.float32)
    key = kz * float(length) + lane
    rank = jnp.zeros((1, length), jnp.float32)
    for piece in range(pieces):
        part = key[:, piece * LANES : (piece + 1) * LANES]
        part = jnp.broadcast_to(part, (LANES, LANES)).T
        part = jnp.concatenate([part] * pieces, axis=1)
        rank = rank + jnp.sum(jnp.where(part < key, 1.0, 0.0), axis=0, keepdims=True)
    rank = rank.astype(jnp.int32)
    seat = rank // STRETCH
    spot = seat // RUNS * LANES + (seat + run) % RUNS * STRETCH + rank % STRETCH
    return spot.astype(jnp.float32)


def grid_kernel(
    coils, unroll, planes, freq, pos_ref, count_ref, block_ref, slab_ref, val_ref, tab_ref, map_ref,
    lines_ref, every_ref, limits_ref, maps_ref,
    flat, cells, near, bump, placed, ready, spots, least, most, limits,
    line_out, line_in, line_own, spots_out, spots_in, spots_own,
    limit_out, limit_in, limit_own, map_out, map_in, map_own,
):
    turn_at = pl.program_id(0)
    tiles, slabs, each, tile = ready.shape
    rows = slabs * each
    deals, shares = map_ref.shape[0], map_ref.shape[2]
    slab, coil = lax.axis_index("slab"), lax.axis_index("coil")
    barrier = pltpu.get_barrier_semaphore()
    here = slab // shares == coil

    def line_copy(at, hop):
        peer = lax.rem(slab + hop, slabs)
        return pltpu.make_async_remote_copy(
            ready.at[at, peer], lines_ref.at[slab, at], line_out.at[at, hop], line_in.at[at, hop],
            device_id={"slab": peer}, device_id_type=MESH,
        )

    def line_keep(at):
        return pltpu.make_async_copy(
            ready.at[at, slab], lines_ref.at[slab, at], line_own.at[at]
        )

    def spots_copy(at, hop):
        peer = lax.rem(slab + hop, slabs)
        return pltpu.make_async_remote_copy(
            spots.at[at], every_ref.at[slab, at], spots_out.at[at, hop], spots_in.at[at, hop],
            device_id={"slab": peer}, device_id_type=MESH,
        )

    def spots_keep(at):
        return pltpu.make_async_copy(spots.at[at], every_ref.at[slab, at], spots_own.at[at])

    def limit_copy(hop):
        peer = lax.rem(slab + hop, slabs)
        return pltpu.make_async_remote_copy(
            limits, limits_ref.at[slab], limit_out.at[hop], limit_in.at[hop],
            device_id={"slab": peer}, device_id_type=MESH,
        )

    def limit_keep():
        return pltpu.make_async_copy(limits, limits_ref.at[slab], limit_own)

    def map_copy(deal, share):
        return pltpu.make_async_remote_copy(
            map_ref.at[deal, :, share], maps_ref.at[slab],
            map_out.at[deal, share], map_in.at[slab],
            device_id={"slab": coil * shares + share, "coil": deal}, device_id_type=MESH,
        )

    def map_take(source):
        return pltpu.make_async_remote_copy(
            map_ref.at[0, :, 0], maps_ref.at[source], map_out.at[0, 0], map_in.at[source],
            device_id={"slab": slab, "coil": coil}, device_id_type=MESH,
        )

    def map_keep():
        return pltpu.make_async_copy(
            map_ref.at[coil, :, lax.rem(slab, shares)], maps_ref.at[slab], map_own
        )

    def is_me(deal, share):
        return jnp.logical_and(coil * shares + share == slab, coil == deal)

    @pl.when(turn_at == 0)
    def _():
        for hop in range(1, slabs):
            pl.semaphore_signal(
                barrier, 1, device_id={"slab": lax.rem(slab + hop, slabs)}, device_id_type=MESH
            )
        for source in range(slabs):
            @pl.when(jnp.logical_not(jnp.logical_and(here, source == slab)))
            def _():
                pl.semaphore_signal(
                    barrier, 1, device_id={"slab": source, "coil": slab // shares},
                    device_id_type=MESH,
                )
    length = tile // RUNS
    chunks = tile // LANES

    for piece in range(chunks):
        cut = slice(piece * LANES, (piece + 1) * LANES)
        live = lax.broadcasted_iota(jnp.int32, (CELLS, LANES), 0) < count_ref[:, cut]
        place = jnp.where(live, pos_ref[:, cut].astype(jnp.float32), DEAD)
        both = jnp.concatenate([place, pltpu.roll(place, LANES - 8, 1)], axis=0)
        flat[cut, :] = both.astype(jnp.bfloat16).T

    segments = KX // CELLS
    kz = slab_ref[...] * planes + block_ref[...] // (segments * freq)
    ky = block_ref[...] // segments % freq
    seg = block_ref[...] % segments
    kz, ky = kz.astype(jnp.float32), ky.astype(jnp.float32)

    block = lax.broadcasted_iota(jnp.int32, (16, LANES), 0)
    upper = lax.broadcasted_iota(jnp.int32, (16, LANES), 1) >= CELLS
    odd = block >= 8
    own = [block % 2 == half for half in range(2)]
    head = block % 8 < 4
    mine = block % 4 // 2 == upper.astype(jnp.int32)
    level = lax.broadcasted_iota(jnp.int32, (CLASSES, LANES), 0).astype(jnp.float32)

    def step(g, slot):
        at = pl.ds(pl.multiple_of(g * 16, 16), 16)
        left = []
        for c in range(coils):
            straight = val_ref[c, at, :].astype(jnp.float32)
            turned = pltpu.roll(straight, CELLS, 1)
            for low, high in ((straight, turned), (turned, straight)):
                placed_here = jnp.where(
                    odd, jnp.where(upper, high, 0.0), jnp.where(upper, 0.0, low)
                )
                halves = [jnp.where(own[half], placed_here, 0.0) for half in range(2)]
                left.append(jnp.concatenate(halves, axis=1).astype(jnp.bfloat16))
        place = flat[at, :].astype(jnp.float32)[:8] * 0.125
        for r in range(CLASSES):
            offset = place - ((r + 0.5) * 0.125 - 0.5)
            seat = jnp.floor(offset)
            offset = (offset - seat) * 3.2 - 1.6
            rise = jnp.maximum(1.0 - offset * offset, 0.0)
            near[slot, r] = seat
            bump[slot, r] = rise * rise
        right = []
        for quad in range(4):
            halves = []
            for half in range(2):
                row = pl.ds(2 * quad + half, 1)
                parts = []
                for r in range(CLASSES):
                    seat = jnp.broadcast_to(near[slot, r, row, :], level.shape)
                    high = jnp.broadcast_to(bump[slot, r, row, :], level.shape)
                    parts.append(jnp.where(level == seat, high, 0.0))
                halves.append(jnp.concatenate(parts, axis=0).astype(jnp.bfloat16))
            right.append(jnp.concatenate(halves, axis=1))
        done = lax.dot_general(
            jnp.concatenate(left, axis=0),
            jnp.concatenate(right, axis=0),
            NT,
            preferred_element_type=jnp.float32,
        )
        for v in range(2 * coils):
            rows16 = slice(16 * v, 16 * v + 16)
            both = jnp.where(head, done[rows16, :LANES], done[rows16, LANES:])
            both = jnp.where(mine, both, 0.0)
            cells[at, LANES * v : LANES * (v + 1)] = both.astype(jnp.bfloat16)

    @pl.loop(0, tile // (16 * unroll))
    def _(outer):
        for slot in range(unroll):
            step(outer * unroll + slot, slot)

        @pl.when(jnp.logical_and(turn_at == 0, outer == 0))
        def _():
            pl.semaphore_wait(barrier, slabs - 1 + deals * shares - here.astype(jnp.int32))
            for deal in range(deals):
                for share in range(shares):
                    @pl.when(jnp.logical_not(is_me(deal, share)))
                    def _():
                        map_copy(deal, share).start()

            @pl.when(here)
            def _():
                map_keep().start()

    wide = 2 * coils
    x_here = each // wide
    line = lax.broadcasted_iota(jnp.int32, (rows, LANES), 0)
    x_at = line // each * x_here + line // 2 % x_here + (KX - rows // wide) // 2
    x_at = jnp.concatenate([x_at] * (length // LANES), axis=1)
    pad = jnp.zeros((14, length), jnp.float32)
    for run in range(RUNS):
        cut = slice(run * length, (run + 1) * length)
        moved = lax.dot_general(
            tab_ref[...], cells[cut, :], NT, preferred_element_type=jnp.float32
        )
        turn = (x_at * seg[:, cut]) & 3
        turned = jnp.where((turn & 1) == 0, moved[:rows], moved[rows:])
        turned = jnp.where(turn >= 2, -turned, turned)
        turned = jnp.concatenate([turned, kz[:, cut], ky[:, cut], pad], axis=0)
        spot = order(kz[:, cut], run)
        placed[run] = permute(turned.astype(jnp.bfloat16), spot).astype(jnp.bfloat16)

    @pl.when(turn_at == 0)
    def _():
        least[...] = jnp.full_like(least, 1.0e4)
        most[...] = jnp.zeros_like(most)

    for at, out in regroup([placed.at[run] for run in range(RUNS)]):
        for owner in range(slabs):
            ready[turn_at, owner, :, at * LANES : (at + 1) * LANES] = out[
                owner * each : (owner + 1) * each
            ]
        found = out[rows : rows + 2]
        spots[turn_at, :, at * LANES : (at + 1) * LANES] = found
        found = found.astype(jnp.float32)
        least[at : at + 1] = jnp.minimum(least[at : at + 1], found[0:1])
        most[at : at + 1] = jnp.maximum(most[at : at + 1], found[0:1])

    @pl.when(turn_at == tiles - 1)
    def _():
        step_down = max(8 // each, 1)
        low = jnp.min(least[...].T, axis=0, keepdims=True).astype(jnp.int32)
        low = low // step_down * step_down
        high = jnp.max(most[...].T, axis=0, keepdims=True).astype(jnp.int32)
        high = (high - low) // SPAN + 1
        limits[0:1] = low
        limits[1:2] = high
        limits[2:] = jnp.zeros((6, LANES), jnp.int32)

    for hop in range(1, slabs):
        line_copy(turn_at, hop).start()
        spots_copy(turn_at, hop).start()
    line_keep(turn_at).start()
    spots_keep(turn_at).start()

    @pl.when(turn_at == tiles - 1)
    def _():
        for hop in range(1, slabs):
            limit_copy(hop).start()
        limit_keep().start()
        for deal in range(deals):
            for share in range(shares):
                @pl.when(jnp.logical_not(is_me(deal, share)))
                def _():
                    map_copy(deal, share).wait_send()
        for source in range(slabs):
            @pl.when(jnp.logical_not(jnp.logical_and(here, source == slab)))
            def _():
                map_take(source).wait_recv()

        @pl.when(here)
        def _():
            map_keep().wait()

        for at in range(tiles):
            line_keep(at).wait()
            spots_keep(at).wait()
            for hop in range(1, slabs):
                line_copy(at, hop).wait()
                spots_copy(at, hop).wait()
        limit_keep().wait()
        for hop in range(1, slabs):
            limit_copy(hop).wait()


def add_kernel(
    per, limit_ref, vals_ref, spot_ref, out_ref, total
):
    step = pl.program_id(0)
    chunks = vals_ref.shape[3] // LANES
    tiles, rows = vals_ref.shape[1], vals_ref.shape[2]
    pairs, depth, freq = out_ref.shape[0], out_ref.shape[1], out_ref.shape[2] // 2
    deep = 16 // rows
    width = tiles * LANES
    inner = (lax.broadcasted_iota(jnp.int32, (16, width), 0) // rows).astype(jnp.float32)

    @pl.when(step == 0)
    def _():
        total[...] = jnp.zeros_like(total)

    def pick(outer, part, read):
        cut = pl.ds(pl.multiple_of((outer * per + part) * LANES, LANES), LANES)
        return jnp.concatenate([read(t, cut) for t in range(tiles)], axis=1)

    def add(outer, part, start):
        vals = pick(outer, part, lambda t, cut: vals_ref[0, t, :, cut])
        vals = jnp.concatenate([vals] * deep, axis=0)
        both = pick(outer, part, lambda t, cut: spot_ref[0, t, :, cut].astype(jnp.float32))
        base = jnp.full((16, width), start, jnp.int32).astype(jnp.float32)
        plane = jnp.broadcast_to(both[0:1], (16, width)) - base - inner
        plane = plane.astype(jnp.bfloat16)
        left = [
            jnp.where(plane == jnp.bfloat16(at), vals, jnp.bfloat16(0))
            for at in range(0, SPAN, deep)
        ]
        moved = lax.dot_general(
            jnp.concatenate(left, axis=0),
            hot_rows(both[1:2], freq),
            NT,
            preferred_element_type=jnp.float32,
        )
        at = pl.ds(pl.multiple_of(start * rows, 8), SPAN * rows)
        for half in range(freq // LANES):
            total[half, at, :] += moved[:, half * LANES : (half + 1) * LANES]

    @pl.loop(0, chunks // per)
    def _(outer):
        for part in range(per):
            add(outer, part, limit_ref[step, 0, outer * per + part])

        def extra(part, carry):
            first = limit_ref[step, 0, outer * per + part]

            def again(at, carry):
                add(outer, part, first + at * SPAN)
                return carry

            return lax.fori_loop(1, limit_ref[step, 1, outer * per + part], again, carry)

        lax.fori_loop(0, per, extra, 0)

    @pl.when(step == pl.num_programs(0) - 1)
    def _():
        for pair in range(pairs):
            for part in range(2):
                for half in range(freq // LANES):
                    start = part * freq + half * LANES
                    found = total[half, pl.ds(2 * pair + part, depth, stride=rows), :]
                    out_ref[pair, :, start : start + LANES] = found.astype(jnp.bfloat16)


def image_kernel(
    rows_ref, map_ref, ytab_ref, ztab_ref, out_ref, ready, near, far, sums,
    near_out, near_in, far_out, far_in,
):
    wide, slabs, planes, _ = ready.shape
    coils = rows_ref.shape[0] // wide
    deals, shares = far.shape[1], far.shape[2]
    depth, freq = rows_ref.shape[1], rows_ref.shape[2] // 2
    slab, coil = lax.axis_index("slab"), lax.axis_index("coil")
    barrier = pltpu.get_barrier_semaphore()
    for hop in range(1, slabs):
        peer = {"slab": lax.rem(slab + hop, slabs)}
        pl.semaphore_signal(barrier, 1, device_id=peer, device_id_type=MESH)
    for way in range(2):
        @pl.when(coil != (0 if way else deals - 1))
        def _():
            peer = {"coil": coil + 1 - 2 * way}
            pl.semaphore_signal(barrier, 1, device_id=peer, device_id_type=MESH)

    def near_copy(x, hop):
        peer = lax.rem(slab + hop, slabs)
        return pltpu.make_async_remote_copy(
            ready.at[x, peer], near.at[x, slab], near_out.at[x, hop], near_in.at[x, hop],
            device_id={"slab": peer}, device_id_type=MESH,
        )

    def line_copy(way, deal, share, x):
        spot = (way, deal, share, x)
        return pltpu.make_async_remote_copy(
            sums.at[spot], far.at[spot], far_out.at[spot], far_in.at[spot],
            device_id={"coil": coil + 1 - 2 * way}, device_id_type=MESH,
        )

    def own_part(deal, share, x):
        source = deal * shares + share
        hop = lax.rem(slab + slabs - source, slabs)

        @pl.when(hop > 0)
        def _():
            near_copy(x, hop).wait_recv()

        return near[x, source].astype(jnp.float32)

    def pass_on(way):
        last = deals - 1 if way else 0
        goals = range(deals - 1) if way else range(deals - 1, 0, -1)
        for deal in goals:
            ahead = coil > deal if way else coil < deal

            @pl.when(ahead)
            def _():
                for x in range(wide):
                    for share in range(shares):
                        sums[way, deal, share, x] = own_part(deal, share, x).astype(jnp.bfloat16)

                        @pl.when(coil != last)
                        def _():
                            line_copy(way, deal, share, x).wait_recv()
                            both = near[x, deal * shares + share].astype(jnp.float32)
                            both = both + far[way, deal, share, x].astype(jnp.float32)
                            sums[way, deal, share, x] = both.astype(jnp.bfloat16)

                        line_copy(way, deal, share, x).start()

    for x in range(wide):
        real = imag = 0.0
        for c in range(coils):
            planar = jnp.dot(
                rows_ref[c * wide + x], ytab_ref[...], preferred_element_type=jnp.float32
            ).astype(jnp.bfloat16)
            planar = jnp.concatenate([planar[:, :freq], planar[:, freq:]], axis=0)
            image = jnp.dot(ztab_ref[...], planar, preferred_element_type=jnp.float32)
            image = image.astype(jnp.bfloat16).astype(jnp.float32)
            img_re, img_im = image[:depth], image[depth:]
            maps = map_ref[:, c, x].reshape(depth, 2 * freq).astype(jnp.float32)
            map_re, map_im = maps[:, :freq], maps[:, freq:]
            real = real + (map_re * img_re + map_im * img_im)
            imag = imag + (map_re * img_im - map_im * img_re)
        both = jnp.concatenate([real, imag], axis=1).astype(jnp.bfloat16)
        ready[x] = both.reshape(slabs, planes, 2 * freq)
        near[x, pl.ds(slab, 1)] = ready[x, pl.ds(slab, 1)]
        if x == 0:
            ends = (coil == 0).astype(jnp.int32) + (coil == deals - 1).astype(jnp.int32)
            pl.semaphore_wait(barrier, slabs + 1 - ends)
        for hop in range(1, slabs):
            near_copy(x, hop).start()

    @pl.when(coil < deals // 2)
    def _():
        pass_on(0)
        pass_on(1)

    @pl.when(coil >= deals // 2)
    def _():
        pass_on(1)
        pass_on(0)

    for deal in range(deals):
        @pl.when(coil == deal)
        def _():
            for x in range(wide):
                for share in range(shares):
                    value = own_part(deal, share, x)
                    for way in range(2):
                        if deal != (deals - 1 if way else 0):
                            line_copy(way, deal, share, x).wait_recv()
                            value = value + far[way, deal, share, x].astype(jnp.float32)
                    out_ref[:, share * wide + x, :] = value

    for x in range(wide):
        for hop in range(1, slabs):
            near_copy(x, hop).wait_send()
        for share in range(shares):
            for way in range(2):
                for deal in range(deals):
                    ahead = coil > deal if way else coil < deal

                    @pl.when(ahead)
                    def _():
                        line_copy(way, deal, share, x).wait_send()


def per_device(samples, sample_pos, block_count, grid_block, block_slab, sensitivity):
    slab_total = lax.axis_size("slab")
    coil_total = lax.axis_size("coil")
    coils = samples.shape[0]
    blocks = samples.shape[1]
    planes = sensitivity.shape[1]
    rows_out = sensitivity.shape[2] * coil_total
    depth = planes * slab_total
    freq = sensitivity.shape[3] // 2
    x_here = rows_out // slab_total
    tile = math.gcd(blocks, 2048)
    tiles = blocks // tile
    chunks = tile // LANES
    unroll = math.gcd(tile // 16, 64)
    count = 2 * coils * rows_out
    each = 2 * coils * x_here

    row = pl.BlockSpec((1, tile), lambda b: (0, b))
    table = spread_table(across_table(coils, rows_out, x_here), 2 * coils)
    x_own = sensitivity.shape[2]
    maps = sensitivity.reshape(
        coil_total, coils, planes, x_own // x_here, x_here, 2 * freq
    ).transpose(0, 1, 3, 4, 2, 5)
    anywhere = pl.BlockSpec(memory_space=pl.ANY)
    sent, spots, limits, maps = pl.pallas_call(
        functools.partial(grid_kernel, coils, unroll, planes, freq),
        grid=(tiles,),
        in_specs=[
            pl.BlockSpec((CELLS, tile), lambda b: (0, b)),
            row,
            row,
            row,
            pl.BlockSpec((coils, tile, LANES), lambda b: (0, b, 0)),
            pl.BlockSpec(table.shape, lambda b: (0, 0)),
            anywhere,
        ],
        out_specs=[anywhere] * 4,
        out_shape=[
            jax.ShapeDtypeStruct((slab_total, tiles, each, tile), jnp.bfloat16),
            jax.ShapeDtypeStruct((slab_total, tiles, 2, tile), jnp.bfloat16),
            jax.ShapeDtypeStruct((slab_total, 8, LANES), jnp.int32),
            jax.ShapeDtypeStruct((slab_total, coils) + maps.shape[3:], jnp.bfloat16),
        ],
        scratch_shapes=[
            pltpu.VMEM((tile, LANES), jnp.bfloat16),
            pltpu.VMEM((tile, 2 * coils * LANES), jnp.bfloat16),
            pltpu.VMEM((unroll, CLASSES, 8, LANES), jnp.float32),
            pltpu.VMEM((unroll, CLASSES, 8, LANES), jnp.float32),
            pltpu.VMEM((RUNS, count + 16, tile // RUNS), jnp.bfloat16),
            pltpu.VMEM((tiles, slab_total, each, tile), jnp.bfloat16),
            pltpu.VMEM((tiles, 2, tile), jnp.bfloat16),
            pltpu.VMEM((LANES, LANES), jnp.float32),
            pltpu.VMEM((LANES, LANES), jnp.float32),
            pltpu.VMEM((8, LANES), jnp.int32),
            pltpu.SemaphoreType.DMA((tiles, slab_total)),
            pltpu.SemaphoreType.DMA((tiles, slab_total)),
            pltpu.SemaphoreType.DMA((tiles,)),
            pltpu.SemaphoreType.DMA((tiles, slab_total)),
            pltpu.SemaphoreType.DMA((tiles, slab_total)),
            pltpu.SemaphoreType.DMA((tiles,)),
            pltpu.SemaphoreType.DMA((slab_total,)),
            pltpu.SemaphoreType.DMA((slab_total,)),
            pltpu.SemaphoreType.DMA,
            pltpu.SemaphoreType.DMA((coil_total, x_own // x_here)),
            pltpu.SemaphoreType.DMA((slab_total,)),
            pltpu.SemaphoreType.DMA,
        ],
        compiler_params=pltpu.CompilerParams(collective_id=0, has_side_effects=True),
        name="grid_x",
    )(
        sample_pos.T,
        block_count[None, :],
        grid_block[None, :],
        block_slab.reshape(1, blocks),
        samples,
        table,
        maps,
    )

    per = math.gcd(chunks, PER)
    ytab, ztab = right_table(freq), left_table(depth)
    pairs = each // 2
    imaged = pl.pallas_call(
        functools.partial(add_kernel, per),
        grid_spec=pltpu.PrefetchScalarGridSpec(
            num_scalar_prefetch=1,
            grid=(slab_total,),
            in_specs=[
                pl.BlockSpec((1, tiles, each, tile), lambda i, a: (i, 0, 0, 0)),
                pl.BlockSpec((1, tiles, 2, tile), lambda i, a: (i, 0, 0, 0)),
            ],
            out_specs=pl.BlockSpec((pairs, depth, 2 * freq), lambda i, a: (0, 0, 0)),
            scratch_shapes=[
                pltpu.VMEM((freq // LANES, (depth + SPAN) * each, LANES), jnp.float32)
            ],
        ),
        out_shape=jax.ShapeDtypeStruct((pairs, depth, 2 * freq), jnp.bfloat16),
        name="add_yz",
    )(limits, sent, spots)

    shares = x_own // x_here
    memory = pl.BlockSpec(memory_space=pltpu.VMEM)
    return pl.pallas_call(
        image_kernel,
        in_specs=[memory] * 4,
        out_specs=memory,
        out_shape=jax.ShapeDtypeStruct((planes, x_own, 2 * freq), jnp.float32),
        scratch_shapes=[
            pltpu.VMEM((x_here, slab_total, planes, 2 * freq), jnp.bfloat16),
            pltpu.VMEM((x_here, slab_total, planes, 2 * freq), jnp.bfloat16),
            pltpu.VMEM((2, coil_total, shares, x_here, planes, 2 * freq), jnp.bfloat16),
            pltpu.VMEM((2, coil_total, shares, x_here, planes, 2 * freq), jnp.bfloat16),
            pltpu.SemaphoreType.DMA((x_here, slab_total)),
            pltpu.SemaphoreType.DMA((x_here, slab_total)),
            pltpu.SemaphoreType.DMA((2, coil_total, shares, x_here)),
            pltpu.SemaphoreType.DMA((2, coil_total, shares, x_here)),
        ],
        compiler_params=pltpu.CompilerParams(collective_id=1, has_side_effects=True),
        name="image_sum",
    )(imaged, maps, ytab, ztab)


def solution(mesh):
    return jax.shard_map(
        per_device,
        mesh=mesh,
        in_specs=(
            P("coil", "slab", None),
            P("slab", None),
            P("slab"),
            P("slab"),
            P("slab", None),
            P(None, "slab", "coil", None),
        ),
        out_specs=P("slab", "coil", None),
        check_vma=False,
    )
```

```python
import functools
import math

import jax
import jax.numpy as jnp
import numpy as np
from jax import lax
from jax.experimental import pallas as pl
from jax.experimental.pallas import tpu as pltpu
from jax.sharding import PartitionSpec as P

KX = 256
CELLS = 64
CLASSES = 8
LANES = 128
RUNS = 4
STRETCH = LANES // RUNS
SPAN = 56
PER = 16
DEAD = 9984.0
NT = (((1,), (1,)), ((), ()))
MESH = pl.DeviceIdType.MESH


def twiddle(first, second, length):
    phase = (first * second % length).astype(np.float32) * np.float32(2.0 * math.pi / length)
    scale = np.float32(1.0 / math.sqrt(length))
    return np.cos(phase) * scale, np.sin(phase) * scale


def across_table(coils, rows_out, x_here):
    x0 = (KX - rows_out) // 2
    cosine, sine = twiddle(x0 + np.arange(rows_out)[:, None], np.arange(CELLS)[None, :], KX)
    upper = np.stack([cosine, -sine], axis=1)
    lower = np.stack([sine, cosine], axis=1)
    eye = np.eye(coils, dtype=np.float32)
    tables = []
    for one in (np.stack([upper, lower], axis=1), np.stack([-lower, upper], axis=1)):
        one = one.reshape(rows_out // x_here, 1, x_here, 2, 1, 2, CELLS)
        one = one * eye[None, :, None, None, :, None, None]
        tables.append(one.reshape(2 * coils * rows_out, 2 * coils * CELLS))
    return np.concatenate(tables, axis=0)


def right_table(length):
    cosine, sine = twiddle(np.arange(length)[:, None], np.arange(length)[None, :], length)
    upper = np.concatenate([cosine, sine], axis=1)
    lower = np.concatenate([-sine, cosine], axis=1)
    return jnp.asarray(np.concatenate([upper, lower], axis=0).astype(jnp.bfloat16))


def left_table(length):
    cosine, sine = twiddle(np.arange(length)[:, None], np.arange(length)[None, :], length)
    upper = np.concatenate([cosine, -sine], axis=1)
    lower = np.concatenate([sine, cosine], axis=1)
    return jnp.asarray(np.concatenate([upper, lower], axis=0).astype(jnp.bfloat16))


def spread_table(table, values):
    at = np.arange(2 * CELLS) % CELLS
    cell = CLASSES * (at % CLASSES) + at // CLASSES
    table = table.reshape(table.shape[0], values, CELLS)[:, :, cell]
    return jnp.asarray(table.reshape(table.shape[0], values * 2 * CELLS).astype(jnp.bfloat16))


def hot_rows(spots, depth):
    level = lax.broadcasted_iota(jnp.int32, (16, spots.shape[1]), 0).astype(jnp.float32)
    spots = jnp.broadcast_to(spots, (16, spots.shape[1])).astype(jnp.bfloat16)
    one, none = jnp.bfloat16(1), jnp.bfloat16(0)
    return jnp.concatenate(
        [
            jnp.where((level + at).astype(jnp.bfloat16) == spots, one, none)
            for at in range(0, depth, 16)
        ],
        axis=0,
    )


def permute(values, spots):
    length = spots.shape[1]
    deep = math.gcd(length, 256)
    hot = [hot_rows(spots - float(at), deep) for at in range(0, length, deep)]
    hot = jnp.concatenate(hot, axis=0)
    return lax.dot_general(values, hot, NT, preferred_element_type=jnp.float32)


def regroup(runs):
    rows, length = runs[0].shape
    place = lax.broadcasted_iota(jnp.int32, (rows, LANES), 1) // STRETCH
    for at in range(length // STRETCH):
        cut = slice(at // RUNS * LANES, at // RUNS * LANES + LANES)
        out = runs[0][:, cut]
        for run in range(1, RUNS):
            out = jnp.where(place == (at + run) % RUNS, runs[run][:, cut], out)
        yield at, out


def order(kz, run):
    length = kz.shape[1]
    pieces = length // LANES
    lane = lax.broadcasted_iota(jnp.int32, (1, length), 1).astype(jnp.float32)
    key = kz * float(length) + lane
    rank = jnp.zeros((1, length), jnp.float32)
    for piece in range(pieces):
        part = key[:, piece * LANES : (piece + 1) * LANES]
        part = jnp.broadcast_to(part, (LANES, LANES)).T
        part = jnp.concatenate([part] * pieces, axis=1)
        rank = rank + jnp.sum(jnp.where(part < key, 1.0, 0.0), axis=0, keepdims=True)
    rank = rank.astype(jnp.int32)
    seat = rank // STRETCH
    spot = seat // RUNS * LANES + (seat + run) % RUNS * STRETCH + rank % STRETCH
    return spot.astype(jnp.float32)


def grid_kernel(
    coils, unroll, planes, freq, pos_ref, count_ref, block_ref, slab_ref, val_ref, tab_ref, map_ref,
    lines_ref, every_ref, limits_ref, maps_ref,
    flat, cells, near, bump, placed, ready, spots, least, most, limits,
    line_out, line_in, line_own, spots_out, spots_in, spots_own,
    limit_out, limit_in, limit_own, map_out, map_in, map_own,
):
    turn_at = pl.program_id(0)
    tiles, slabs, each, tile = ready.shape
    rows = slabs * each
    deals, shares = map_ref.shape[0], map_ref.shape[2]
    slab, coil = lax.axis_index("slab"), lax.axis_index("coil")
    barrier = pltpu.get_barrier_semaphore()
    here = slab // shares == coil

    def line_copy(at, hop):
        peer = lax.rem(slab + hop, slabs)
        return pltpu.make_async_remote_copy(
            ready.at[at, peer], lines_ref.at[slab, at], line_out.at[at, hop], line_in.at[at, hop],
            device_id={"slab": peer}, device_id_type=MESH,
        )

    def line_keep(at):
        return pltpu.make_async_copy(
            ready.at[at, slab], lines_ref.at[slab, at], line_own.at[at]
        )

    def spots_copy(at, hop):
        peer = lax.rem(slab + hop, slabs)
        return pltpu.make_async_remote_copy(
            spots.at[at], every_ref.at[slab, at], spots_out.at[at, hop], spots_in.at[at, hop],
            device_id={"slab": peer}, device_id_type=MESH,
        )

    def spots_keep(at):
        return pltpu.make_async_copy(spots.at[at], every_ref.at[slab, at], spots_own.at[at])

    def limit_copy(hop):
        peer = lax.rem(slab + hop, slabs)
        return pltpu.make_async_remote_copy(
            limits, limits_ref.at[slab], limit_out.at[hop], limit_in.at[hop],
            device_id={"slab": peer}, device_id_type=MESH,
        )

    def limit_keep():
        return pltpu.make_async_copy(limits, limits_ref.at[slab], limit_own)

    def map_copy(deal, share):
        return pltpu.make_async_remote_copy(
            map_ref.at[deal, :, share], maps_ref.at[slab],
            map_out.at[deal, share], map_in.at[slab],
            device_id={"slab": coil * shares + share, "coil": deal}, device_id_type=MESH,
        )

    def map_take(source):
        return pltpu.make_async_remote_copy(
            map_ref.at[0, :, 0], maps_ref.at[source], map_out.at[0, 0], map_in.at[source],
            device_id={"slab": slab, "coil": coil}, device_id_type=MESH,
        )

    def map_keep():
        return pltpu.make_async_copy(
            map_ref.at[coil, :, lax.rem(slab, shares)], maps_ref.at[slab], map_own
        )

    def is_me(deal, share):
        return jnp.logical_and(coil * shares + share == slab, coil == deal)

    @pl.when(turn_at == 0)
    def _():
        for hop in range(1, slabs):
            pl.semaphore_signal(
                barrier, 1, device_id={"slab": lax.rem(slab + hop, slabs)}, device_id_type=MESH
            )
        for source in range(slabs):
            @pl.when(jnp.logical_not(jnp.logical_and(here, source == slab)))
            def _():
                pl.semaphore_signal(
                    barrier, 1, device_id={"slab": source, "coil": slab // shares},
                    device_id_type=MESH,
                )
    length = tile // RUNS
    chunks = tile // LANES

    for piece in range(chunks):
        cut = slice(piece * LANES, (piece + 1) * LANES)
        live = lax.broadcasted_iota(jnp.int32, (CELLS, LANES), 0) < count_ref[:, cut]
        place = jnp.where(live, pos_ref[:, cut].astype(jnp.float32), DEAD)
        both = jnp.concatenate([place, pltpu.roll(place, LANES - 8, 1)], axis=0)
        flat[cut, :] = both.astype(jnp.bfloat16).T

    segments = KX // CELLS
    kz = slab_ref[...] * planes + block_ref[...] // (segments * freq)
    ky = block_ref[...] // segments % freq
    seg = block_ref[...] % segments
    kz, ky = kz.astype(jnp.float32), ky.astype(jnp.float32)

    block = lax.broadcasted_iota(jnp.int32, (16, LANES), 0)
    upper = lax.broadcasted_iota(jnp.int32, (16, LANES), 1) >= CELLS
    odd = block >= 8
    own = [block % 2 == half for half in range(2)]
    head = block % 8 < 4
    mine = block % 4 // 2 == upper.astype(jnp.int32)
    level = lax.broadcasted_iota(jnp.int32, (CLASSES, LANES), 0).astype(jnp.float32)

    def step(g, slot):
        at = pl.ds(pl.multiple_of(g * 16, 16), 16)
        left = []
        for c in range(coils):
            straight = val_ref[c, at, :].astype(jnp.float32)
            turned = pltpu.roll(straight, CELLS, 1)
            for low, high in ((straight, turned), (turned, straight)):
                placed_here = jnp.where(
                    odd, jnp.where(upper, high, 0.0), jnp.where(upper, 0.0, low)
                )
                halves = [jnp.where(own[half], placed_here, 0.0) for half in range(2)]
                left.append(jnp.concatenate(halves, axis=1).astype(jnp.bfloat16))
        place = flat[at, :].astype(jnp.float32)[:8] * 0.125
        for r in range(CLASSES):
            offset = place - ((r + 0.5) * 0.125 - 0.5)
            seat = jnp.floor(offset)
            offset = (offset - seat) * 3.2 - 1.6
            rise = jnp.maximum(1.0 - offset * offset, 0.0)
            near[slot, r] = seat
            bump[slot, r] = rise * rise
        right = []
        for quad in range(4):
            halves = []
            for half in range(2):
                row = pl.ds(2 * quad + half, 1)
                parts = []
                for r in range(CLASSES):
                    seat = jnp.broadcast_to(near[slot, r, row, :], level.shape)
                    high = jnp.broadcast_to(bump[slot, r, row, :], level.shape)
                    parts.append(jnp.where(level == seat, high, 0.0))
                halves.append(jnp.concatenate(parts, axis=0).astype(jnp.bfloat16))
            right.append(jnp.concatenate(halves, axis=1))
        done = lax.dot_general(
            jnp.concatenate(left, axis=0),
            jnp.concatenate(right, axis=0),
            NT,
            preferred_element_type=jnp.float32,
        )
        for v in range(2 * coils):
            rows16 = slice(16 * v, 16 * v + 16)
            both = jnp.where(head, done[rows16, :LANES], done[rows16, LANES:])
            both = jnp.where(mine, both, 0.0)
            cells[at, LANES * v : LANES * (v + 1)] = both.astype(jnp.bfloat16)

    @pl.loop(0, tile // (16 * unroll))
    def _(outer):
        for slot in range(unroll):
            step(outer * unroll + slot, slot)

        @pl.when(jnp.logical_and(turn_at == 0, outer == 0))
        def _():
            pl.semaphore_wait(barrier, slabs - 1 + deals * shares - here.astype(jnp.int32))
            for deal in range(deals):
                for share in range(shares):
                    @pl.when(jnp.logical_not(is_me(deal, share)))
                    def _():
                        map_copy(deal, share).start()

            @pl.when(here)
            def _():
                map_keep().start()

    wide = 2 * coils
    x_here = each // wide
    line = lax.broadcasted_iota(jnp.int32, (rows, LANES), 0)
    x_at = line // each * x_here + line // 2 % x_here + (KX - rows // wide) // 2
    x_at = jnp.concatenate([x_at] * (length // LANES), axis=1)
    pad = jnp.zeros((14, length), jnp.float32)
    for run in range(RUNS):
        cut = slice(run * length, (run + 1) * length)
        moved = lax.dot_general(
            tab_ref[...], cells[cut, :], NT, preferred_element_type=jnp.float32
        )
        turn = (x_at * seg[:, cut]) & 3
        turned = jnp.where((turn & 1) == 0, moved[:rows], moved[rows:])
        turned = jnp.where(turn >= 2, -turned, turned)
        turned = jnp.concatenate([turned, kz[:, cut], ky[:, cut], pad], axis=0)
        spot = order(kz[:, cut], run)
        placed[run] = permute(turned.astype(jnp.bfloat16), spot).astype(jnp.bfloat16)

    @pl.when(turn_at == 0)
    def _():
        least[...] = jnp.full_like(least, 1.0e4)
        most[...] = jnp.zeros_like(most)

    for at, out in regroup([placed.at[run] for run in range(RUNS)]):
        for owner in range(slabs):
            ready[turn_at, owner, :, at * LANES : (at + 1) * LANES] = out[
                owner * each : (owner + 1) * each
            ]
        found = out[rows : rows + 2]
        spots[turn_at, :, at * LANES : (at + 1) * LANES] = found
        found = found.astype(jnp.float32)
        least[at : at + 1] = jnp.minimum(least[at : at + 1], found[0:1])
        most[at : at + 1] = jnp.maximum(most[at : at + 1], found[0:1])

    @pl.when(turn_at == tiles - 1)
    def _():
        step_down = max(8 // each, 1)
        low = jnp.min(least[...].T, axis=0, keepdims=True).astype(jnp.int32)
        low = low // step_down * step_down
        high = jnp.max(most[...].T, axis=0, keepdims=True).astype(jnp.int32)
        high = (high - low) // SPAN + 1
        limits[0:1] = low
        limits[1:2] = high
        limits[2:] = jnp.zeros((6, LANES), jnp.int32)

    for hop in range(1, slabs):
        line_copy(turn_at, hop).start()
        spots_copy(turn_at, hop).start()
    line_keep(turn_at).start()
    spots_keep(turn_at).start()

    @pl.when(turn_at == tiles - 1)
    def _():
        for hop in range(1, slabs):
            limit_copy(hop).start()
        limit_keep().start()
        for deal in range(deals):
            for share in range(shares):
                @pl.when(jnp.logical_not(is_me(deal, share)))
                def _():
                    map_copy(deal, share).wait_send()
        for source in range(slabs):
            @pl.when(jnp.logical_not(jnp.logical_and(here, source == slab)))
            def _():
                map_take(source).wait_recv()

        @pl.when(here)
        def _():
            map_keep().wait()

        for at in range(tiles):
            line_keep(at).wait()
            spots_keep(at).wait()
            for hop in range(1, slabs):
                line_copy(at, hop).wait()
                spots_copy(at, hop).wait()
        limit_keep().wait()
        for hop in range(1, slabs):
            limit_copy(hop).wait()


def add_kernel(
    per, limit_ref, vals_ref, spot_ref, out_ref, total
):
    step = pl.program_id(0)
    chunks = vals_ref.shape[3] // LANES
    tiles, rows = vals_ref.shape[1], vals_ref.shape[2]
    pairs, depth, freq = out_ref.shape[0], out_ref.shape[1], out_ref.shape[2] // 2
    deep = 16 // rows
    width = tiles * LANES
    inner = (lax.broadcasted_iota(jnp.int32, (16, width), 0) // rows).astype(jnp.float32)

    @pl.when(step == 0)
    def _():
        total[...] = jnp.zeros_like(total)

    def pick(outer, part, read):
        cut = pl.ds(pl.multiple_of((outer * per + part) * LANES, LANES), LANES)
        return jnp.concatenate([read(t, cut) for t in range(tiles)], axis=1)

    def add(outer, part, start):
        vals = pick(outer, part, lambda t, cut: vals_ref[0, t, :, cut])
        vals = jnp.concatenate([vals] * deep, axis=0)
        both = pick(outer, part, lambda t, cut: spot_ref[0, t, :, cut].astype(jnp.float32))
        base = jnp.full((16, width), start, jnp.int32).astype(jnp.float32)
        plane = jnp.broadcast_to(both[0:1], (16, width)) - base - inner
        plane = plane.astype(jnp.bfloat16)
        left = [
            jnp.where(plane == jnp.bfloat16(at), vals, jnp.bfloat16(0))
            for at in range(0, SPAN, deep)
        ]
        moved = lax.dot_general(
            jnp.concatenate(left, axis=0),
            hot_rows(both[1:2], freq),
            NT,
            preferred_element_type=jnp.float32,
        )
        at = pl.ds(pl.multiple_of(start * rows, 8), SPAN * rows)
        for half in range(freq // LANES):
            total[half, at, :] += moved[:, half * LANES : (half + 1) * LANES]

    @pl.loop(0, chunks // per)
    def _(outer):
        for part in range(per):
            add(outer, part, limit_ref[step, 0, outer * per + part])

        def extra(part, carry):
            first = limit_ref[step, 0, outer * per + part]

            def again(at, carry):
                add(outer, part, first + at * SPAN)
                return carry

            return lax.fori_loop(1, limit_ref[step, 1, outer * per + part], again, carry)

        lax.fori_loop(0, per, extra, 0)

    @pl.when(step == pl.num_programs(0) - 1)
    def _():
        for pair in range(pairs):
            for part in range(2):
                for half in range(freq // LANES):
                    start = part * freq + half * LANES
                    found = total[half, pl.ds(2 * pair + part, depth, stride=rows), :]
                    out_ref[pair, :, start : start + LANES] = found.astype(jnp.bfloat16)


def image_kernel(
    rows_ref, map_ref, ytab_ref, ztab_ref, out_ref, ready, near, far, sums,
    near_out, near_in, far_out, far_in,
):
    wide, slabs, planes, _ = ready.shape
    coils = rows_ref.shape[0] // wide
    deals, shares = far.shape[1], far.shape[2]
    depth, freq = rows_ref.shape[1], rows_ref.shape[2] // 2
    slab, coil = lax.axis_index("slab"), lax.axis_index("coil")
    barrier = pltpu.get_barrier_semaphore()
    for hop in range(1, slabs):
        peer = {"slab": lax.rem(slab + hop, slabs)}
        pl.semaphore_signal(barrier, 1, device_id=peer, device_id_type=MESH)
    for way in range(2):
        @pl.when(coil != (0 if way else deals - 1))
        def _():
            peer = {"coil": coil + 1 - 2 * way}
            pl.semaphore_signal(barrier, 1, device_id=peer, device_id_type=MESH)

    def near_copy(x, hop):
        peer = lax.rem(slab + hop, slabs)
        return pltpu.make_async_remote_copy(
            ready.at[x, peer], near.at[x, slab], near_out.at[x, hop], near_in.at[x, hop],
            device_id={"slab": peer}, device_id_type=MESH,
        )

    def line_copy(way, deal, share, x):
        spot = (way, deal, share, x)
        return pltpu.make_async_remote_copy(
            sums.at[spot], far.at[spot], far_out.at[spot], far_in.at[spot],
            device_id={"coil": coil + 1 - 2 * way}, device_id_type=MESH,
        )

    def own_part(deal, share, x):
        source = deal * shares + share
        hop = lax.rem(slab + slabs - source, slabs)

        @pl.when(hop > 0)
        def _():
            near_copy(x, hop).wait_recv()

        return near[x, source].astype(jnp.float32)

    def pass_on(way, x):
        last = deals - 1 if way else 0
        goals = range(deals - 1) if way else range(deals - 1, 0, -1)
        for deal in goals:
            ahead = coil > deal if way else coil < deal

            @pl.when(ahead)
            def _():
                for share in range(shares):
                    sums[way, deal, share, x] = own_part(deal, share, x).astype(jnp.bfloat16)

                    @pl.when(coil != last)
                    def _():
                        line_copy(way, deal, share, x).wait_recv()
                        both = near[x, deal * shares + share].astype(jnp.float32)
                        both = both + far[way, deal, share, x].astype(jnp.float32)
                        sums[way, deal, share, x] = both.astype(jnp.bfloat16)

                    line_copy(way, deal, share, x).start()

    for x in range(wide):
        real = imag = 0.0
        for c in range(coils):
            planar = jnp.dot(
                rows_ref[c * wide + x], ytab_ref[...], preferred_element_type=jnp.float32
            ).astype(jnp.bfloat16)
            planar = jnp.concatenate([planar[:, :freq], planar[:, freq:]], axis=0)
            image = jnp.dot(ztab_ref[...], planar, preferred_element_type=jnp.float32)
            image = image.astype(jnp.bfloat16).astype(jnp.float32)
            img_re, img_im = image[:depth], image[depth:]
            maps = map_ref[:, c, x].reshape(depth, 2 * freq).astype(jnp.float32)
            map_re, map_im = maps[:, :freq], maps[:, freq:]
            real = real + (map_re * img_re + map_im * img_im)
            imag = imag + (map_re * img_im - map_im * img_re)
        both = jnp.concatenate([real, imag], axis=1).astype(jnp.bfloat16)
        ready[x] = both.reshape(slabs, planes, 2 * freq)
        near[x, pl.ds(slab, 1)] = ready[x, pl.ds(slab, 1)]
        if x == 0:
            ends = (coil == 0).astype(jnp.int32) + (coil == deals - 1).astype(jnp.int32)
            pl.semaphore_wait(barrier, slabs + 1 - ends)
        for hop in range(1, slabs):
            near_copy(x, hop).start()

    @pl.when(coil < deals // 2)
    def _():
        for x in range(wide):
            pass_on(0, x)
            pass_on(1, x)

    @pl.when(coil >= deals // 2)
    def _():
        for x in range(wide):
            pass_on(1, x)
            pass_on(0, x)

    for deal in range(deals):
        @pl.when(coil == deal)
        def _():
            for x in range(wide):
                for share in range(shares):
                    value = own_part(deal, share, x)
                    for way in range(2):
                        if deal != (deals - 1 if way else 0):
                            line_copy(way, deal, share, x).wait_recv()
                            value = value + far[way, deal, share, x].astype(jnp.float32)
                    out_ref[:, share * wide + x, :] = value

    for x in range(wide):
        for hop in range(1, slabs):
            near_copy(x, hop).wait_send()
        for share in range(shares):
            for way in range(2):
                for deal in range(deals):
                    ahead = coil > deal if way else coil < deal

                    @pl.when(ahead)
                    def _():
                        line_copy(way, deal, share, x).wait_send()


def per_device(samples, sample_pos, block_count, grid_block, block_slab, sensitivity):
    slab_total = lax.axis_size("slab")
    coil_total = lax.axis_size("coil")
    coils = samples.shape[0]
    blocks = samples.shape[1]
    planes = sensitivity.shape[1]
    rows_out = sensitivity.shape[2] * coil_total
    depth = planes * slab_total
    freq = sensitivity.shape[3] // 2
    x_here = rows_out // slab_total
    tile = math.gcd(blocks, 2048)
    tiles = blocks // tile
    chunks = tile // LANES
    unroll = math.gcd(tile // 16, 64)
    count = 2 * coils * rows_out
    each = 2 * coils * x_here

    row = pl.BlockSpec((1, tile), lambda b: (0, b))
    table = spread_table(across_table(coils, rows_out, x_here), 2 * coils)
    x_own = sensitivity.shape[2]
    maps = sensitivity.reshape(
        coil_total, coils, planes, x_own // x_here, x_here, 2 * freq
    ).transpose(0, 1, 3, 4, 2, 5)
    anywhere = pl.BlockSpec(memory_space=pl.ANY)
    sent, spots, limits, maps = pl.pallas_call(
        functools.partial(grid_kernel, coils, unroll, planes, freq),
        grid=(tiles,),
        in_specs=[
            pl.BlockSpec((CELLS, tile), lambda b: (0, b)),
            row,
            row,
            row,
            pl.BlockSpec((coils, tile, LANES), lambda b: (0, b, 0)),
            pl.BlockSpec(table.shape, lambda b: (0, 0)),
            anywhere,
        ],
        out_specs=[anywhere] * 4,
        out_shape=[
            jax.ShapeDtypeStruct((slab_total, tiles, each, tile), jnp.bfloat16),
            jax.ShapeDtypeStruct((slab_total, tiles, 2, tile), jnp.bfloat16),
            jax.ShapeDtypeStruct((slab_total, 8, LANES), jnp.int32),
            jax.ShapeDtypeStruct((slab_total, coils) + maps.shape[3:], jnp.bfloat16),
        ],
        scratch_shapes=[
            pltpu.VMEM((tile, LANES), jnp.bfloat16),
            pltpu.VMEM((tile, 2 * coils * LANES), jnp.bfloat16),
            pltpu.VMEM((unroll, CLASSES, 8, LANES), jnp.float32),
            pltpu.VMEM((unroll, CLASSES, 8, LANES), jnp.float32),
            pltpu.VMEM((RUNS, count + 16, tile // RUNS), jnp.bfloat16),
            pltpu.VMEM((tiles, slab_total, each, tile), jnp.bfloat16),
            pltpu.VMEM((tiles, 2, tile), jnp.bfloat16),
            pltpu.VMEM((LANES, LANES), jnp.float32),
            pltpu.VMEM((LANES, LANES), jnp.float32),
            pltpu.VMEM((8, LANES), jnp.int32),
            pltpu.SemaphoreType.DMA((tiles, slab_total)),
            pltpu.SemaphoreType.DMA((tiles, slab_total)),
            pltpu.SemaphoreType.DMA((tiles,)),
            pltpu.SemaphoreType.DMA((tiles, slab_total)),
            pltpu.SemaphoreType.DMA((tiles, slab_total)),
            pltpu.SemaphoreType.DMA((tiles,)),
            pltpu.SemaphoreType.DMA((slab_total,)),
            pltpu.SemaphoreType.DMA((slab_total,)),
            pltpu.SemaphoreType.DMA,
            pltpu.SemaphoreType.DMA((coil_total, x_own // x_here)),
            pltpu.SemaphoreType.DMA((slab_total,)),
            pltpu.SemaphoreType.DMA,
        ],
        compiler_params=pltpu.CompilerParams(collective_id=0, has_side_effects=True),
        name="grid_x",
    )(
        sample_pos.T,
        block_count[None, :],
        grid_block[None, :],
        block_slab.reshape(1, blocks),
        samples,
        table,
        maps,
    )

    per = math.gcd(chunks, PER)
    ytab, ztab = right_table(freq), left_table(depth)
    pairs = each // 2
    imaged = pl.pallas_call(
        functools.partial(add_kernel, per),
        grid_spec=pltpu.PrefetchScalarGridSpec(
            num_scalar_prefetch=1,
            grid=(slab_total,),
            in_specs=[
                pl.BlockSpec((1, tiles, each, tile), lambda i, a: (i, 0, 0, 0)),
                pl.BlockSpec((1, tiles, 2, tile), lambda i, a: (i, 0, 0, 0)),
            ],
            out_specs=pl.BlockSpec((pairs, depth, 2 * freq), lambda i, a: (0, 0, 0)),
            scratch_shapes=[
                pltpu.VMEM((freq // LANES, (depth + SPAN) * each, LANES), jnp.float32)
            ],
        ),
        out_shape=jax.ShapeDtypeStruct((pairs, depth, 2 * freq), jnp.bfloat16),
        name="add_yz",
    )(limits, sent, spots)

    shares = x_own // x_here
    memory = pl.BlockSpec(memory_space=pltpu.VMEM)
    return pl.pallas_call(
        image_kernel,
        in_specs=[memory] * 4,
        out_specs=memory,
        out_shape=jax.ShapeDtypeStruct((planes, x_own, 2 * freq), jnp.float32),
        scratch_shapes=[
            pltpu.VMEM((x_here, slab_total, planes, 2 * freq), jnp.bfloat16),
            pltpu.VMEM((x_here, slab_total, planes, 2 * freq), jnp.bfloat16),
            pltpu.VMEM((2, coil_total, shares, x_here, planes, 2 * freq), jnp.bfloat16),
            pltpu.VMEM((2, coil_total, shares, x_here, planes, 2 * freq), jnp.bfloat16),
            pltpu.SemaphoreType.DMA((x_here, slab_total)),
            pltpu.SemaphoreType.DMA((x_here, slab_total)),
            pltpu.SemaphoreType.DMA((2, coil_total, shares, x_here)),
            pltpu.SemaphoreType.DMA((2, coil_total, shares, x_here)),
        ],
        compiler_params=pltpu.CompilerParams(collective_id=1, has_side_effects=True),
        name="image_sum",
    )(imaged, maps, ytab, ztab)


def solution(mesh):
    return jax.shard_map(
        per_device,
        mesh=mesh,
        in_specs=(
            P("coil", "slab", None),
            P("slab", None),
            P("slab"),
            P("slab"),
            P("slab", None),
            P(None, "slab", "coil", None),
        ),
        out_specs=P("slab", "coil", None),
        check_vma=False,
    )
```
